32 devices in a mesh: dp: 32 (over z, y, x, core).
Axes of the slice: x: 2, y: 2, z: 4, core: 2. Of those that a mesh axis runs over, the one named last changes fastest.
Arguments:
- features: bfloat16 [32768, 768], P('dp'), may hold values from -6 to 6
- pos_conv: bfloat16 [32768, 768], P('dp'), may hold values from -3 to 3
- segment_ids: int32 [32, 1024], P('dp'), may hold values from 0 to 3, never falling along the last dimension, each value on 1 to 512 neighbouring positions
- frame_valid: int32 [32, 1024], P('dp'), may hold values 0 or 1
- cotangent: bfloat16 [32768, 768], P('dp'), may hold values from -6 to 6
- qkv_weight: float32 [768, 2304], P('dp'), may hold values from -0.21875 to 0.21875
- proj_weight: float32 [768, 768], P('dp'), may hold values from -1.75 to 1.75
- expand_weight: float32 [768, 3072], P('dp'), may hold values from -0.21875 to 0.21875
- reduce_weight: float32 [3072, 768], P('dp'), may hold values from -0.109375 to 0.109375
- norm_gains: float32 [2, 768], P(None, 'dp'), may hold values from 0.5 to 1.5
- bias_vector: float32 [7680], P('dp'), may hold values from -1.5 to 1.5
- qkv_moment: float32 [768, 2304], P('dp'), may hold values from -1086.116 to 1086.116
- proj_moment: float32 [768, 768], P('dp'), may hold values from -108.6116 to 108.6116
- expand_moment: float32 [768, 3072], P('dp'), may hold values from -325.8348 to 325.8348
- reduce_moment: float32 [3072, 768], P('dp'), may hold values from -651.6696 to 651.6696
- gains_moment: float32 [2, 768], P(None, 'dp'), may hold values from -1086.116 to 1086.116
- bias_moment: float32 [7680], P('dp'), may hold values from -1086.116 to 1086.116
- qkv_average: float32 [768, 2304], P('dp'), may hold values from -0.21875 to 0.21875
- proj_average: float32 [768, 768], P('dp'), may hold values from -1.75 to 1.75
- expand_average: float32 [768, 3072], P('dp'), may hold values from -0.21875 to 0.21875
- reduce_average: float32 [3072, 768], P('dp'), may hold values from -0.109375 to 0.109375
- gains_average: float32 [2, 768], P(None, 'dp'), may hold values from 0.5 to 1.5
- bias_average: float32 [7680], P('dp'), may hold values from -1.5 to 1.5
Outputs:
- layer_out: bfloat16 [32768, 768], P('dp')
- grad_input: bfloat16 [32768, 768], P('dp')
- qkv_grad: float32 [768, 2304], P('dp')
- proj_grad: float32 [768, 768], P('dp')
- expand_grad: float32 [768, 3072], P('dp')
- reduce_grad: float32 [3072, 768], P('dp')
- gains_grad: float32 [2, 768], P(None, 'dp')
- bias_grad: float32 [7680], P('dp')
- qkv_master: float32 [768, 2304], P('dp')
- proj_master: float32 [768, 768], P('dp')
- expand_master: float32 [768, 3072], P('dp')
- reduce_master: float32 [3072, 768], P('dp')
- gains_master: float32 [2, 768], P(None, 'dp')
- bias_master: float32 [7680], P('dp')
- qkv_velocity: float32 [768, 2304], P('dp')
- proj_velocity: float32 [768, 768], P('dp')
- expand_velocity: float32 [768, 3072], P('dp')
- reduce_velocity: float32 [3072, 768], P('dp')
- gains_velocity: float32 [2, 768], P(None, 'dp')
- bias_velocity: float32 [7680], P('dp')
- qkv_smooth: float32 [768, 2304], P('dp')
- proj_smooth: float32 [768, 768], P('dp')
- expand_smooth: float32 [768, 3072], P('dp')
- reduce_smooth: float32 [3072, 768], P('dp')
- gains_smooth: float32 [2, 768], P(None, 'dp')
- bias_smooth: float32 [7680], P('dp')
The draws below stay inside these ranges and needn't reach their ends.
Inputs may be any that keep to these rules, and one draw needn't show every extreme that they name: `segment_ids`: each row lists one device's utterances: numbers 0 to 3 in order, each a run of 1 to 512 frames, one of exactly 512. `frame_valid`: 1 marks a frame with audio.
All inputs are finite; a program needn't handle non-finite values. No bound on the sum of `frame_valid` on one device may be relied on, other than what follows from the above.
Results may differ from the reference program's by a relative error of at most 0.015.
The reference program's roundings to bfloat16 on the way count: a program that leaves them out, or rounds other values in their place, can miss the bound.
Values may be sent and summed in bfloat16 or wider, within the bound.
A program may use at most 320 MiB of HBM per device.

```python
import math
import jax
import jax.numpy as jnp
import numpy as np
from jax import lax

D = 768
H = 12
HD = 64
FF = 3072
TOK_DEV = 1024
UTT_DEV = 4
UTT_MAX = 512
TOKENS = 32768
N_DP = 32


def set_ends(array, own_key, low, top_value):
    longest = array.shape.index(max(array.shape))
    spots = []
    for shift in (0, 1):
        where = [jax.random.randint(jax.random.fold_in(own_key, axis), (), 0, length) for axis, length in enumerate(array.shape)]
        where[longest] = (where[longest] + shift) % array.shape[longest]
        spots.append(tuple(where))
    return array.at[spots[0]].set(low).at[spots[1]].set(top_value)


def block_scale(rng, extent, cuts, least, high):
    level, own = 1.0, jax.random.fold_in(rng, 6)
    for axis_at, parts in cuts:
        draws = jnp.exp(jax.random.uniform(jax.random.fold_in(own, axis_at), (parts,), jnp.float32, least / len(cuts), high / len(cuts)))
        level = level * jnp.repeat(draws, extent[axis_at] // parts).reshape([-1 if axis == axis_at else 1 for axis in range(len(extent))])
    return level


def split_up(count, total, limit, skew):
    loads = [(1 << 20) // math.isqrt(standing ** skew) + 1 for standing in range(2, count + 1)]
    surplus, counts = total - limit - (count - 1), [1] * (count - 1)
    while surplus > 0:
        free = [i for i in range(count - 1) if counts[i] < limit]
        whole, remaining = sum([loads[i] for i in free]), surplus
        for i in free:
            more = min(limit - counts[i], max(1, remaining * loads[i] // whole), surplus)
            counts[i] = counts[i] + more
            surplus = surplus - more
    return np.array([limit] + counts)


def ragged(stream_key, number_of, total, most, skew):
    if number_of == 2:
        one = jax.random.randint(stream_key, (), max(1, total - most), min(most, total - 1) + 1)
        return jnp.stack([one, total - one])
    sizes = jnp.asarray(split_up(number_of, total, most, skew), jnp.int32)
    couples = (number_of - 1) // 2
    giver, receiver = sizes[1:1 + 2 * couples:2], sizes[2:2 + 2 * couples:2]
    room = jnp.minimum(giver - 1, most - receiver)
    moved = jax.random.randint(jax.random.fold_in(stream_key, 1), (couples,), 0, 1 << 20) % (room + 1)
    sizes = sizes.at[1:1 + 2 * couples:2].set(giver - moved).at[2:2 + 2 * couples:2].set(receiver + moved)
    return sizes[jax.random.permutation(jax.random.fold_in(stream_key, 2), number_of)]


def noise(stream_key, extent, deviation, most, shards=(), held_as=jnp.bfloat16):
    gain = block_scale(stream_key, extent, shards, -0.22, 0.18) if shards else 1.0
    values = jax.random.normal(stream_key, extent, jnp.float32) * deviation * gain
    return jnp.minimum(jnp.maximum(values, -most), most).astype(held_as)


def setup_inputs(seed: int = 0) -> dict:
    seeds = jax.random.split(jax.random.key(seed), 24)
    features = noise(seeds[0], (TOKENS, D), 1.0, 6.0, ((0, 32),))
    pos_conv = noise(seeds[1], (TOKENS, D), 0.5, 3.0, ((0, 32),))
    segment_ids = jax.vmap(lambda own: jnp.searchsorted(jnp.cumsum(ragged(own, UTT_DEV, TOK_DEV, UTT_MAX, 2)), jnp.arange(TOK_DEV), side="right"))(jax.random.split(seeds[2], N_DP)).reshape((N_DP, TOK_DEV)).astype(jnp.int32)
    frame_valid = set_ends((jax.random.randint(seeds[3], (N_DP, TOK_DEV), 0, 8) < 7).astype(jnp.int32), jax.random.fold_in(seeds[3], 1), 0, 1)
    cotangent = noise(seeds[4], (TOKENS, D), 1.0, 6.0, ((0, 32),))
    qkv_weight = noise(seeds[5], (D, 3 * D), D ** -0.5, 0.21875, ((0, 32),), jnp.float32)
    proj_weight = noise(seeds[6], (D, D), (D // 64) ** -0.5, 1.75, ((0, 32),), jnp.float32)
    expand_weight = noise(seeds[7], (D, FF), D ** -0.5, 0.21875, ((0, 32),), jnp.float32)
    reduce_weight = noise(seeds[8], (FF, D), FF ** -0.5, 0.109375, ((0, 32),), jnp.float32)
    norm_gains = jnp.clip(1.0 + 0.1 * jax.random.normal(seeds[9], (2, D), jnp.float32), 0.5, 1.5)
    bias_vector = noise(seeds[10], (6 * D + FF,), 0.3, 1.5, ((0, 32),), jnp.float32)
    qkv_moment = noise(seeds[11], (D, 3 * D), (1.0 * (TOK_DEV * N_DP) ** 0.5), 1086.116, ((0, 32),), jnp.float32)
    proj_moment = noise(seeds[12], (D, D), (0.1 * (TOK_DEV * N_DP) ** 0.5), 108.6116, ((0, 32),), jnp.float32)
    expand_moment = noise(seeds[13], (D, FF), (0.3 * (TOK_DEV * N_DP) ** 0.5), 325.8348, ((0, 32),), jnp.float32)
    reduce_moment = noise(seeds[14], (FF, D), (0.6 * (TOK_DEV * N_DP) ** 0.5), 651.6696, ((0, 32),), jnp.float32)
    gains_moment = noise(seeds[15], (2, D), (1.0 * (TOK_DEV * N_DP) ** 0.5), 1086.116, ((1, 32),), jnp.float32)
    bias_moment = noise(seeds[16], (6 * D + FF,), (1.0 * (TOK_DEV * N_DP) ** 0.5), 1086.116, ((0, 32),), jnp.float32)
    qkv_average = noise(seeds[17], (D, 3 * D), D ** -0.5, 0.21875, ((0, 32),), jnp.float32)
    proj_average = noise(seeds[18], (D, D), (D // 64) ** -0.5, 1.75, ((0, 32),), jnp.float32)
    expand_average = noise(seeds[19], (D, FF), D ** -0.5, 0.21875, ((0, 32),), jnp.float32)
    reduce_average = noise(seeds[20], (FF, D), FF ** -0.5, 0.109375, ((0, 32),), jnp.float32)
    gains_average = jnp.clip(1.0 + 0.1 * jax.random.normal(seeds[21], (2, D), jnp.float32), 0.5, 1.5)
    bias_average = noise(seeds[22], (6 * D + FF,), 0.3, 1.5, ((0, 32),), jnp.float32)
    return {"features": features, "pos_conv": pos_conv, "segment_ids": segment_ids, "frame_valid": frame_valid, "cotangent": cotangent, "qkv_weight": qkv_weight, "proj_weight": proj_weight, "expand_weight": expand_weight, "reduce_weight": reduce_weight, "norm_gains": norm_gains, "bias_vector": bias_vector, "qkv_moment": qkv_moment, "proj_moment": proj_moment, "expand_moment": expand_moment, "reduce_moment": reduce_moment, "gains_moment": gains_moment, "bias_moment": bias_moment, "qkv_average": qkv_average, "proj_average": proj_average, "expand_average": expand_average, "reduce_average": reduce_average, "gains_average": gains_average, "bias_average": bias_average}


highest = lax.Precision.HIGHEST
rate_matrix = 0.04
rate_proj = 0.5
rate_small = 0.2

@jax.custom_vjp
def low(v):
    return lax.optimization_barrier(v.astype(jnp.bfloat16)).astype(jnp.float32)

@jax.custom_vjp
def low_back(v):
    return v

def low_keep(v):
    return (low(v), None)

def low_pass(kept, grad):
    return (grad,)

def back_keep(v):
    return (v, None)

def back_low(kept, grad):
    return (low(grad),)
low.defvjp(low_keep, low_pass)
low_back.defvjp(back_keep, back_low)

def layer_norm(residual, gain_row, offset):
    center = residual - lax.optimization_barrier(jnp.mean(residual, axis=-1, keepdims=True))
    spread = lax.optimization_barrier(jnp.mean(center * center, axis=-1, keepdims=True))
    return center * lax.rsqrt(spread + 1e-05) * gain_row + offset

def gelu_exact(argument):
    return 0.5 * argument * (1.0 + jax.scipy.special.erf(argument * 0.7071067811865476))

def attend(block_data):
    queries, key_heads, values, segment_rows, valid_rows = block_data
    column = jnp.arange(TOK_DEV)
    allowed = (segment_rows[:, None] == segment_rows[None, :]) & ((valid_rows[None, :] > 0) | (column[:, None] == column[None, :]))
    scores = jnp.einsum('qhe,khe->hqk', queries, key_heads, precision=highest) * 0.125
    scores = low_back(scores)
    scores = jnp.where(allowed[None], scores, -1000000000.0)
    maximum = lax.optimization_barrier(jnp.max(scores, axis=-1, keepdims=True))
    exponent = jnp.exp(scores - maximum)
    weights_now = low(exponent / lax.optimization_barrier(jnp.sum(exponent, axis=-1, keepdims=True)))
    return jnp.einsum('hqk,khe->qhe', weights_now, values, precision=highest)

def nesterov(master, gradient, moment, average, step_rate):
    velocity = 0.5 * moment + gradient
    renewed = master - step_rate * (gradient + 0.5 * velocity)
    smooth = 0.5 * average + 0.5 * renewed
    return (renewed, velocity, smooth)

def reference(features, pos_conv, segment_ids, frame_valid, cotangent, qkv_weight, proj_weight, expand_weight, reduce_weight, norm_gains, bias_vector, qkv_moment, proj_moment, expand_moment, reduce_moment, gains_moment, bias_moment, qkv_average, proj_average, expand_average, reduce_average, gains_average, bias_average):
    valid_col = frame_valid.reshape(TOKENS, 1).astype(jnp.float32)
    position = pos_conv.astype(jnp.float32)

    def forward(inputs, qkv_full, proj_full, expand_full, reduce_full, gains_full, bias_full):
        qkv_full = low(qkv_full)
        proj_full = low(proj_full)
        expand_full = low(expand_full)
        reduce_full = low(reduce_full)
        gains_full = low(gains_full)
        bias_full = low(bias_full)
        entry_sum = (inputs + position) * valid_col
        entry_low = low(entry_sum)
        qkv_bias = jnp.concatenate([bias_full[0:D], jnp.zeros((D,), jnp.float32), bias_full[D:2 * D]])
        qkv_rows = low_back(low(jnp.dot(entry_low, qkv_full, precision=highest) + qkv_bias))
        shaped = qkv_rows.reshape(N_DP, TOK_DEV, 3, H, HD)
        context = lax.map(jax.checkpoint(attend), (shaped[:, :, 0], shaped[:, :, 1], shaped[:, :, 2], segment_ids, frame_valid))
        context = low_back(low(context.reshape(TOKENS, D)))
        attended = low_back(jnp.dot(context, proj_full, precision=highest) + bias_full[2 * D:3 * D])
        normed = layer_norm(entry_sum + attended, gains_full[0], bias_full[4 * D + FF:5 * D + FF])
        normed_low = low(normed)
        pre_act = low_back(jnp.dot(normed_low, expand_full, precision=highest) + bias_full[3 * D:3 * D + FF])
        activated = low(gelu_exact(pre_act))
        ffn_out = low_back(jnp.dot(activated, reduce_full, precision=highest) + bias_full[3 * D + FF:4 * D + FF])
        return layer_norm(normed + ffn_out, gains_full[1], bias_full[5 * D + FF:6 * D + FF])
    layer_float, pull_back = jax.vjp(forward, features.astype(jnp.float32), qkv_weight, proj_weight, expand_weight, reduce_weight, norm_gains, bias_vector)
    grads = pull_back(cotangent.astype(jnp.float32))
    matrix_rate = rate_matrix / math.sqrt(TOKENS)
    proj_step = rate_proj / math.sqrt(TOKENS)
    small_step = rate_small / math.sqrt(TOKENS)
    qkv_new = nesterov(qkv_weight, grads[1], qkv_moment, qkv_average, matrix_rate)
    proj_new = nesterov(proj_weight, grads[2], proj_moment, proj_average, proj_step)
    expand_new = nesterov(expand_weight, grads[3], expand_moment, expand_average, matrix_rate)
    reduce_new = nesterov(reduce_weight, grads[4], reduce_moment, reduce_average, matrix_rate)
    gains_new = nesterov(norm_gains, grads[5], gains_moment, gains_average, small_step)
    bias_new = nesterov(bias_vector, grads[6], bias_moment, bias_average, small_step)
    return (layer_float.astype(jnp.bfloat16), grads[0].astype(jnp.bfloat16), grads[1], grads[2], grads[3], grads[4], grads[5], grads[6], qkv_new[0], proj_new[0], expand_new[0], reduce_new[0], gains_new[0], bias_new[0], qkv_new[1], proj_new[1], expand_new[1], reduce_new[1], gains_new[1], bias_new[1], qkv_new[2], proj_new[2], expand_new[2], reduce_new[2], gains_new[2], bias_new[2])
```

```python
import functools
import math

import jax
import jax.numpy as jnp
from jax import lax
from jax.experimental import pallas as pl
from jax.experimental.pallas import tpu as pltpu
from jax.sharding import PartitionSpec as P

D = 768
H = 12
HD = 64
FF = 3072
TOK = 1024
HALF = 512

EPSILON = 1e-05
MASKED = -1000000000.0
rate_matrix = 0.04
rate_proj = 0.5
rate_small = 0.2

f32 = jnp.float32
bf16 = jnp.bfloat16
NN = (((1,), (0,)), ((), ()))
NT = (((1,), (1,)), ((), ()))
TN = (((0,), (0,)), ((), ()))
MESH = pl.DeviceIdType.MESH
VMEM_LIMIT = 60 << 20
IN_VMEM = pl.BlockSpec(memory_space=pltpu.VMEM)
IN_HBM = pl.BlockSpec(memory_space=pl.ANY)
S = jax.ShapeDtypeStruct


def dot(a, b, dims):
    return lax.dot_general(a, b, dims, preferred_element_type=f32)


def lane_half(h, shape):
    return (lax.broadcasted_iota(jnp.int32, shape, 1) // HD) == h


def params(**more):
    return pltpu.CompilerParams(vmem_limit_bytes=VMEM_LIMIT, **more)


class Place:
    def __init__(self):
        me = lax.axis_index("dp")
        self.me = me
        self.c, self.x, self.y, self.z = me % 2, (me // 2) % 2, (me // 4) % 2, me // 8
        self.chip = me // 2
        self.partner = me + 1 - 2 * self.c
        self.xn = me + 2 - 4 * self.x
        self.yn = me + 4 - 8 * self.y
        self.up = me + 8
        self.down = me - 8
        z = self.z
        first = jnp.where(z == 0, 1, jnp.where(z == 1, 0, jnp.where(z == 2, 3, 2)))
        second = jnp.where(z == 0, 2, jnp.where(z == 1, 2, 1))
        third = jnp.where(z < 2, 3, 0)
        self.order = (z, first, second, third)

    def other(self, zz, dx=False, dy=False):
        x = 1 - self.x if dx else self.x
        y = 1 - self.y if dy else self.y
        return zz * 4 + y * 2 + x

    def greet(self):
        barrier = pltpu.get_barrier_semaphore()
        for other in (self.partner, self.xn, self.yn):
            pl.semaphore_signal(barrier, inc=1, device_id=(other,), device_id_type=MESH)

        @pl.when(self.z < 3)
        def _():
            pl.semaphore_signal(barrier, inc=1, device_id=(self.up,), device_id_type=MESH)

        @pl.when(self.z > 0)
        def _():
            pl.semaphore_signal(barrier, inc=1, device_id=(self.down,), device_id_type=MESH)

        ends = jnp.where((self.z == 0) | (self.z == 3), 4, 5)
        pl.semaphore_wait(barrier, ends)


def remote(src, dst, send, recv, other):
    return pltpu.make_async_remote_copy(
        src_ref=src, dst_ref=dst, send_sem=send, recv_sem=recv, device_id=(other,), device_id_type=MESH
    )


def arrived(view, sem):
    pltpu.make_async_copy(view, view, sem).wait()


DMA = pltpu.SemaphoreType.DMA


class Gather:
    def __init__(self, place, shard, full, scratch):
        self.p = place
        self.shard = shard
        self.full = full
        self.rows = 2 * shard.shape[0]
        self.half = shard.shape[1] // 2
        self.stage, self.own, self.ls, self.zs, self.zr, self.xs, self.xr, self.ys, self.yr, self.hs, self.hr, self.ps, self.pr = scratch

    @staticmethod
    def scratch(rows, cols, dtype):
        return [pltpu.VMEM((2 * rows, cols), f32), pltpu.VMEM((2 * rows, cols), dtype), DMA((4,)), DMA((5,))] + [DMA((4,))] * 9

    def cut(self, c):
        return pl.ds(pl.multiple_of(c * self.half, 128), self.half)

    def at(self, chip, count=1):
        start = pl.multiple_of(chip * self.rows, 16)
        return self.full.at[pl.ds(start, count * self.rows), self.cut(self.p.c)]

    def loads(self):
        p = self.p
        mine = self.stage.at[pl.ds(pl.multiple_of(p.c * (self.rows // 2), 8), self.rows // 2)]
        return pltpu.make_async_copy(self.shard, mine, self.ls.at[0]), remote(self.shard, mine, self.ls.at[1], self.ls.at[2], p.partner)

    def keep(self):
        return pltpu.make_async_copy(self.own.at[:, self.cut(self.p.c)], self.at(self.p.chip), self.ls.at[3])

    def along_z(self, k):
        p = self.p
        zz = p.order[k]
        view = self.at(p.other(zz))
        src = view if k else self.own.at[:, self.cut(p.c)]
        up = remote(src, view, self.zs.at[k], self.zr.at[zz], p.up)
        if k == 0:
            down = remote(src, view, self.zs.at[4], self.zr.at[zz], p.down)
            return (p.z < 3, up), (p.z > 0, down)
        down = remote(src, view, self.zs.at[k], self.zr.at[zz], p.down)
        return ((p.z < 3) & (zz < p.z), up), ((p.z > 0) & (zz > p.z), down)

    def across(self, k):
        p = self.p
        zz = p.order[k]
        view = self.at(p.other(zz))
        src = view if k else self.own.at[:, self.cut(p.c)]
        return (
            remote(src, view, self.xs.at[zz], self.xr.at[zz], p.xn),
            remote(src, view, self.ys.at[zz], self.yr.at[zz], p.yn),
        )

    def onward(self, k):
        p = self.p
        zz = p.order[k]
        even = k % 2 == 0
        view = self.at(p.other(zz, dx=even, dy=not even))
        return remote(view, view, self.hs.at[zz], self.hr.at[zz], p.yn if even else p.xn)

    def to_partner(self, k):
        zz = self.p.order[k]
        view = self.at(4 * zz, 4)
        return remote(view, view, self.ps.at[zz], self.pr.at[zz], self.p.partner)

    def load(self):
        for copy in self.loads():
            copy.start()

    def begin(self):
        local, pair = self.loads()
        local.wait()
        pair.wait_recv()
        self.own[...] = self.stage[...].astype(self.own.dtype)
        for cond, copy in self.along_z(0):
            pl.when(cond)(copy.start)
        for copy in self.across(0):
            copy.start()
        self.keep().start()

    def column(self, k):
        zz = self.p.order[k]
        arrived(self.at(self.p.other(zz)), self.zr.at[zz])
        for cond, copy in self.along_z(k):
            pl.when(cond)(copy.start)
        for copy in self.across(k):
            copy.start()

    def plane(self, k):
        p = self.p
        zz = p.order[k]
        even = k % 2 == 0
        arrived(self.at(p.other(zz, dx=even, dy=not even)), (self.xr if even else self.yr).at[zz])
        self.onward(k).start()

    def corner(self, k):
        p = self.p
        zz = p.order[k]
        even = k % 2 == 0
        arrived(self.at(p.other(zz, dx=not even, dy=even)), (self.yr if even else self.xr).at[zz])
        arrived(self.at(p.other(zz, True, True)), self.hr.at[zz])
        if k == 0:
            self.keep().wait()
        self.to_partner(k).start()

    def step(self, s):
        if s == 0:
            self.begin()
        if 1 <= s <= 3:
            self.column(s)
        if 1 <= s <= 4:
            self.plane(s - 1)
        if 2 <= s <= 5:
            self.corner(s - 2)
        if s == 6:
            self.finish()

    def finish(self):
        p = self.p
        for zz in range(4):
            start = pl.multiple_of(4 * zz * self.rows, 16)
            arrived(self.full.at[pl.ds(start, 4 * self.rows), self.cut(1 - p.c)], self.pr.at[zz])
        self.loads()[1].wait_send()
        for k in range(4):
            for cond, copy in self.along_z(k):
                pl.when(cond)(copy.wait_send)
            for copy in self.across(k):
                copy.wait_send()
            self.onward(k).wait_send()
            self.to_partner(k).wait_send()


GATHER_SCRATCH = 13


def gather_kernel(count, *refs):
    shards, fulls, rest = refs[:count], refs[count : 2 * count], refs[2 * count :]
    place = Place()
    place.greet()
    jobs = [Gather(place, shards[i], fulls[i], rest[i * GATHER_SCRATCH : (i + 1) * GATHER_SCRATCH]) for i in range(count)]
    for job in jobs:
        job.load()
    for t in range(count + 6):
        for i, job in enumerate(jobs):
            if 0 <= t - i <= 6:
                job.step(t - i)


def gather_all(shards, dtypes):
    count = len(shards)
    return pl.pallas_call(
        functools.partial(gather_kernel, count),
        in_specs=[IN_HBM] * count,
        out_specs=[IN_HBM] * count,
        out_shape=[S((32 * s.shape[0], s.shape[1]), d) for s, d in zip(shards, dtypes)],
        scratch_shapes=sum([Gather.scratch(*s.shape, d) for s, d in zip(shards, dtypes)], []),
        compiler_params=params(collective_id=0, has_side_effects=True),
        name="gather",
    )(*shards)


class Scatter:
    def __init__(self, place, grad, out, scratch):
        self.p = place
        self.grad = grad
        self.out = out
        self.rows = 2 * out.shape[0]
        self.half = out.shape[1] // 2
        self.bp, self.bh, self.bx, self.by, self.bz, self.fin = scratch[:6]
        self.ps, self.pr, self.hs, self.hr, self.xs, self.xr, self.ys, self.yr, self.zs, self.zr, self.fs = scratch[6:]

    @staticmethod
    def scratch(rows, cols, dtype):
        rows, half = 2 * rows, cols // 2
        bufs = [pltpu.VMEM((n * rows, half), dtype) for n in (16, 4, 4, 4, 5)]
        return bufs + [pltpu.VMEM((rows, half), f32)] + [DMA((4,))] * 9 + [DMA((5,)), DMA((3,))]

    def cut(self, c):
        return pl.ds(pl.multiple_of(c * self.half, 128), self.half)

    def span(self, n, count=1):
        return pl.ds(pl.multiple_of(n * self.rows, 16), count * self.rows)

    def at(self, chip):
        return self.grad.at[self.span(chip), self.cut(self.p.c)]

    def slot(self, buf, n):
        return buf.at[self.span(n)]

    def add(self, view, *terms):
        total = view[...].astype(f32)
        for term in terms:
            total = total + term[...].astype(f32)
        view[...] = total.astype(view.dtype)

    def to_partner(self, zz):
        p = self.p
        src = self.grad.at[self.span(4 * zz, 4), self.cut(1 - p.c)]
        return remote(src, self.bp.at[self.span(4 * zz, 4)], self.ps.at[zz], self.pr.at[zz], p.partner)

    def corner(self, k):
        p = self.p
        zz = p.order[k]
        return remote(self.at(p.other(zz, True, True)), self.slot(self.bh, zz), self.hs.at[zz], self.hr.at[zz], p.xn if k % 2 else p.yn)

    def side(self, k, along_x):
        p = self.p
        zz = p.order[k]
        src = self.at(p.other(zz, dx=along_x, dy=not along_x))
        if along_x:
            return remote(src, self.slot(self.bx, zz), self.xs.at[zz], self.xr.at[zz], p.xn)
        return remote(src, self.slot(self.by, zz), self.ys.at[zz], self.yr.at[zz], p.yn)

    def chain(self, k):
        p = self.p
        zz = p.order[k]
        src = self.at(p.other(zz))
        up = remote(src, self.slot(self.bz, zz), self.zs.at[k], self.zr.at[zz], p.up)
        place = jnp.where(zz == p.z - 1, 4, zz)
        down = remote(src, self.slot(self.bz, place), self.zs.at[k], self.zr.at[place], p.down)
        return (zz > p.z, up), (zz < p.z, down)

    def last(self):
        p = self.p
        rows = self.rows // 2
        part = lambda c: self.fin.at[pl.ds(pl.multiple_of(c * rows, 8), rows)]
        dst = self.out.at[:, self.cut(p.c)]
        return pltpu.make_async_copy(part(p.c), dst, self.fs.at[0]), remote(part(1 - p.c), dst, self.fs.at[1], self.fs.at[2], p.partner)

    def step(self, s):
        if s == 0:
            for k in (3, 2, 1, 0):
                self.to_partner(self.p.order[k]).start()
        if 1 <= s <= 4:
            self.pair(4 - s)
        if 2 <= s <= 5:
            self.side_on(5 - s)
        if 3 <= s <= 5:
            self.column(6 - s)
        if s == 6:
            self.total()
        if s == 7:
            self.finish()

    def pair(self, k):
        p = self.p
        zz = p.order[k]
        self.to_partner(zz).wait_recv()

        @pl.loop(0, 4)
        def _(j):
            chip = 4 * zz + j
            self.add(self.at(chip), self.slot(self.bp, chip))

        self.corner(k).start()
        self.side(k, along_x=k % 2 == 1).start()

    def side_on(self, k):
        p = self.p
        zz = p.order[k]
        even = k % 2 == 0
        self.corner(k).wait_recv()
        self.add(self.at(p.other(zz, dx=even, dy=not even)), self.slot(self.bh, zz))
        self.side(k, along_x=even).start()

    def gathered(self, k):
        zz = self.p.order[k]
        self.side(k, True).wait_recv()
        self.side(k, False).wait_recv()
        self.add(self.at(self.p.other(zz)), self.slot(self.bx, zz), self.slot(self.by, zz))

    def column(self, k):
        p = self.p
        zz = p.order[k]
        self.gathered(k)

        @pl.when(((zz > p.z) & (p.z > 0)) | ((zz < p.z) & (p.z < 3)))
        def _():
            arrived(self.slot(self.bz, zz), self.zr.at[zz])
            self.add(self.at(p.other(zz)), self.slot(self.bz, zz))

        for cond, copy in self.chain(k):
            pl.when(cond)(copy.start)

    def total(self):
        p = self.p
        self.gathered(0)
        self.fin[...] = self.at(p.chip)[...].astype(f32)

        @pl.when(p.z > 0)
        def _():
            arrived(self.slot(self.bz, p.z), self.zr.at[p.z])
            self.fin[...] += self.slot(self.bz, p.z)[...].astype(f32)

        @pl.when(p.z < 3)
        def _():
            arrived(self.slot(self.bz, 4), self.zr.at[4])
            self.fin[...] += self.slot(self.bz, 4)[...].astype(f32)

        for copy in self.last():
            copy.start()

    def finish(self):
        p = self.p
        for k in range(4):
            self.to_partner(p.order[k]).wait_send()
            self.corner(k).wait_send()
            self.side(k, True).wait_send()
            self.side(k, False).wait_send()
            if k:
                for cond, copy in self.chain(k):
                    pl.when(cond)(copy.wait_send)
        local, pair = self.last()
        local.wait()
        pair.wait_send()
        arrived(self.out.at[:, self.cut(1 - p.c)], self.fs.at[2])


SCATTER_SCRATCH = 17


def scatter_kernel(count, *refs):
    inputs, outs, rest = refs[:count], refs[count : 2 * count], refs[2 * count :]
    place = Place()
    place.greet()
    each = SCATTER_SCRATCH + 2
    jobs, loads = [], []
    for i in range(count):
        held, load, *own = rest[i * each : (i + 1) * each]
        jobs.append(Scatter(place, held, outs[i], own))
        loads.append(pltpu.make_async_copy(inputs[i], held, load))
        loads[-1].start()
    for t in range(count + 7):
        for i, job in enumerate(jobs):
            s = t - i
            if s == 0:
                loads[i].wait()
            if 0 <= s <= 7:
                job.step(s)


def scatter_all(grads):
    count = len(grads)
    scratch = []
    for g in grads:
        scratch += [pltpu.VMEM(g.shape, g.dtype), DMA(())]
        scratch += Scatter.scratch(g.shape[0] // 32, g.shape[1], g.dtype)
    return pl.pallas_call(
        functools.partial(scatter_kernel, count),
        in_specs=[IN_HBM] * count,
        out_specs=[IN_VMEM] * count,
        out_shape=[S((g.shape[0] // 32, g.shape[1]), f32) for g in grads],
        scratch_shapes=scratch,
        compiler_params=params(collective_id=1, has_side_effects=True),
        name="scatter",
    )(*grads)


def rotation(segments):
    counts = [jnp.sum((segments == u).astype(jnp.int32)) for u in range(3)]
    before, start = jnp.int32(0), jnp.int32(0)
    taken = jnp.bool_(False)
    for u in range(4):
        here = (counts[u] == HALF) & ~taken if u < 3 else ~taken
        start = jnp.where(here, before, start)
        taken = taken | here
        if u < 3:
            before = before + counts[u]
    return start


def column_of(row):
    return jnp.broadcast_to(row, (128, row.shape[1])).T


def entry_kernel(feat_ref, pos_ref, cot_ref, seg_ref, valid_ref, start_ref, entry_ref, low_ref, cot_out_ref, bias_ref, valid_out_ref):
    back = lax.rem(TOK - start_ref[0], TOK)
    valid = valid_ref[...].astype(f32)
    seg = seg_ref[...].astype(f32)
    entry = (feat_ref[...].astype(f32) + pos_ref[...].astype(f32)) * column_of(valid)[:, :1]
    entry = pltpu.roll(entry, back, 0)
    entry_ref[...] = entry
    low_ref[...] = entry.astype(bf16)
    cot_out_ref[...] = pltpu.roll(cot_ref[...], back, 0)
    valid = pltpu.roll(jnp.broadcast_to(valid, (8, TOK)), back, 1)[:1]
    seg = pltpu.roll(jnp.broadcast_to(seg, (8, TOK)), back, 1)[:1]
    valid_out_ref[...] = column_of(valid)
    for h in range(2):
        part = slice(h * HALF, (h + 1) * HALF)
        seg_col = column_of(seg[:, part])[:, :1]
        same = seg_col == seg[:, part]
        rows = lax.broadcasted_iota(jnp.int32, (HALF, HALF), 0)
        cols = lax.broadcasted_iota(jnp.int32, (HALF, HALF), 1)
        allowed = same & ((valid[:, part] > 0.0) | (rows == cols))
        bias_ref[h] = jnp.where(allowed, 0.0, MASKED)


def qkv_kernel(low_ref, weight_ref, bias_ref, out_ref):
    for k in range(3):
        part = slice(k * D, (k + 1) * D)
        out_ref[:, part] = (dot(low_ref[...], weight_ref[:, part], NN) + bias_ref[:, part]).astype(bf16)


def attend_kernel(q_ref, k_ref, v_ref, bias_ref, out_ref, prob_ref):
    q, k, v = q_ref[...] * jnp.bfloat16(0.125), k_ref[...], v_ref[...]
    outs = []
    for h in range(2):
        qh = jnp.where(lane_half(h, q.shape), q, jnp.bfloat16(0))
        scores = dot(qh, k, NT) + bias_ref[0]
        scores = jnp.exp(scores - jnp.max(scores, 1, keepdims=True))
        probs = (scores * (1.0 / jnp.sum(scores, 1, keepdims=True))).astype(bf16)
        prob_ref[h] = probs
        outs.append(dot(probs, v, NN))
    out_ref[...] = jnp.where(lane_half(0, outs[0].shape), outs[0], outs[1]).astype(bf16)


def attend_back_kernel(q_ref, k_ref, v_ref, grad_ref, ctx_ref, prob_ref, dq_ref, dk_ref, dv_ref):
    q, k, v, grad = q_ref[...], k_ref[...], v_ref[...], grad_ref[...]
    product = grad.astype(f32) * ctx_ref[...].astype(f32)
    dq, dk, dv = [], [], []
    for h in range(2):
        lanes = lane_half(h, grad.shape)
        grad_h = jnp.where(lanes, grad, jnp.bfloat16(0))
        row_dot = jnp.sum(jnp.where(lanes, product, 0.0), 1, keepdims=True)
        probs = prob_ref[h]
        ds = (probs.astype(f32) * (dot(grad_h, v, NT) - row_dot)).astype(bf16)
        dq.append(dot(ds, k, NN))
        dk.append(dot(ds, q, TN))
        dv.append(dot(probs, grad, TN))
    lanes = lane_half(0, grad.shape)
    dq_ref[...] = (jnp.where(lanes, dq[0], dq[1]) * 0.125).astype(bf16)
    dk_ref[...] = (jnp.where(lanes, dk[0], dk[1]) * 0.125).astype(bf16)
    dv_ref[...] = jnp.where(lanes, dv[0], dv[1]).astype(bf16)


def pair_block(offset):
    return pl.BlockSpec((HALF, 2 * HD), lambda i, j: (i, offset + j))


PROBS = pl.BlockSpec((2, HALF, HALF), lambda i, j: (i * (H // 2) + j, 0, 0))


def attend(qkv, bias):
    return pl.pallas_call(
        attend_kernel,
        grid=(2, H // 2),
        in_specs=[pair_block(0), pair_block(H // 2), pair_block(H), pl.BlockSpec((1, HALF, HALF), lambda i, j: (i, 0, 0))],
        out_specs=[pair_block(0), PROBS],
        out_shape=[S((TOK, D), bf16), S((2 * H, HALF, HALF), bf16)],
        compiler_params=params(),
        name="attend",
    )(qkv, qkv, qkv, bias)


def attend_back(qkv, grad, ctx, probs):
    return pl.pallas_call(
        attend_back_kernel,
        grid=(2, H // 2),
        in_specs=[pair_block(0), pair_block(H // 2), pair_block(H), pair_block(0), pair_block(0), PROBS],
        out_specs=[pair_block(0)] * 3,
        out_shape=[S((TOK, D), bf16)] * 3,
        compiler_params=params(),
        name="attend_back",
    )(qkv, qkv, qkv, grad, ctx, probs)


ROWS = 256
COLS = 768


def normed_of(residual):
    center = residual - jnp.mean(residual, 1, keepdims=True)
    scale = lax.rsqrt(jnp.mean(center * center, 1, keepdims=True) + EPSILON)
    return center * scale, scale


def norm_back(grad, gain, unit, scale):
    grad = grad * gain
    return scale * (grad - jnp.mean(grad, 1, keepdims=True) - unit * jnp.mean(grad * unit, 1, keepdims=True))


def ffn_kernel(
    ctx_ref, entry_ref, cot_ref, proj_ref, expand_ref, reduce_ref, vec_ref, b1_ref,
    out_ref, first_ref, gctx_ref, dproj_ref, dexpand_ref, dreduce_ref, dvec_ref, db1_ref,
    low_ref, act_ref, gffn_ref, gpre_ref, gbranch_ref, pre_ref, cdf_ref,
):
    dvec_ref[...] = jnp.zeros_like(dvec_ref)
    db1_ref[...] = jnp.zeros_like(db1_ref)
    b_o, b_2, g_1, g_2, c_1, c_2 = [vec_ref[i : i + 1, :] for i in range(6)]

    @pl.loop(0, TOK // ROWS)
    def _(t):
        rows = pl.ds(pl.multiple_of(t * ROWS, ROWS), ROWS)
        unit_1, scale_1 = normed_of(entry_ref[rows, :] + dot(ctx_ref[rows, :], proj_ref[...], NN) + b_o)
        normed = unit_1 * g_1 + c_1
        low = normed.astype(bf16)
        low_ref[rows, :] = low
        total = normed + b_2
        for k in range(FF // COLS):
            cols = slice(k * COLS, (k + 1) * COLS)
            pre = dot(low, expand_ref[:, cols], NN) + b1_ref[:, cols]
            cdf = 0.5 + 0.5 * lax.erf(pre * 0.7071067811865476)
            pre_ref[:, cols] = pre
            cdf_ref[:, cols] = cdf
            act = (pre * cdf).astype(bf16)
            act_ref[rows, cols] = act
            total = total + dot(act, reduce_ref[cols, :], NN)
        unit_2, scale_2 = normed_of(total)
        out_ref[rows, :] = (unit_2 * g_2 + c_2).astype(bf16)
        grad = cot_ref[rows, :].astype(f32)
        dvec_ref[3:4, :] += jnp.sum(grad * unit_2, 0, keepdims=True)
        dvec_ref[5:6, :] += jnp.sum(grad, 0, keepdims=True)
        total = norm_back(grad, g_2, unit_2, scale_2)
        gffn = total.astype(bf16)
        gffn_ref[rows, :] = gffn
        dvec_ref[1:2, :] += jnp.sum(gffn.astype(f32), 0, keepdims=True)
        for k in range(FF // COLS):
            cols = slice(k * COLS, (k + 1) * COLS)
            pre = pre_ref[:, cols]
            slope = cdf_ref[:, cols] + pre * (0.3989422804014327 * jnp.exp(-0.5 * pre * pre))
            gpre = (dot(gffn, reduce_ref[cols, :], NT) * slope).astype(bf16)
            gpre_ref[rows, cols] = gpre
            db1_ref[:, cols] += jnp.sum(gpre.astype(f32), 0, keepdims=True)
            total = total + dot(gpre, expand_ref[:, cols], NT)
        dvec_ref[2:3, :] += jnp.sum(total * unit_1, 0, keepdims=True)
        dvec_ref[4:5, :] += jnp.sum(total, 0, keepdims=True)
        first = norm_back(total, g_1, unit_1, scale_1)
        first_ref[rows, :] = first
        branch = first.astype(bf16)
        gbranch_ref[rows, :] = branch
        dvec_ref[0:1, :] += jnp.sum(branch.astype(f32), 0, keepdims=True)
        gctx_ref[rows, :] = dot(branch, proj_ref[...], NT).astype(bf16)

    @pl.loop(0, FF // 256)
    def _(t):
        part = pl.ds(pl.multiple_of(t * 256, 256), 256)
        dreduce_ref[part, :] = dot(act_ref[:, part], gffn_ref[...], TN).astype(bf16)
        dexpand_ref[:, part] = dot(low_ref[...], gpre_ref[:, part], TN).astype(bf16)

    @pl.loop(0, D // 256)
    def _(t):
        part = pl.ds(pl.multiple_of(t * 256, 256), 256)
        dproj_ref[part, :] = dot(ctx_ref[:, part], gbranch_ref[...], TN).astype(bf16)


def ffn(*arrays):
    return pl.pallas_call(
        ffn_kernel,
        in_specs=[IN_VMEM] * 8,
        out_specs=[IN_VMEM] * 8,
        out_shape=[
            S((TOK, D), bf16), S((TOK, D), f32), S((TOK, D), bf16), S((D, D), bf16),
            S((D, FF), bf16), S((FF, D), bf16), S((8, D), f32), S((1, FF), f32),
        ],
        scratch_shapes=[
            pltpu.VMEM((TOK, D), bf16), pltpu.VMEM((TOK, FF), bf16), pltpu.VMEM((TOK, D), bf16), pltpu.VMEM((TOK, FF), bf16),
            pltpu.VMEM((TOK, D), bf16), pltpu.VMEM((ROWS, FF), f32), pltpu.VMEM((ROWS, FF), f32),
        ],
        compiler_params=pltpu.CompilerParams(vmem_limit_bytes=62 << 20),
        name="ffn",
    )(*arrays)


def tail_kernel(low_ref, dq_ref, dk_ref, dv_ref, weight_ref, first_ref, valid_ref, out_ref, start_ref, grad_ref, input_ref, layer_ref, sums_ref):
    total = first_ref[...]
    for k, part_ref in enumerate((dq_ref, dk_ref, dv_ref)):
        part = slice(k * D, (k + 1) * D)
        grad_ref[:, part] = dot(low_ref[...], part_ref[...], TN).astype(bf16)
        total = total + dot(part_ref[...], weight_ref[:, part], NT)
        sums_ref[k : k + 1, :] = jnp.sum(part_ref[...].astype(f32), 0, keepdims=True)
    total = (total * valid_ref[:, :1]).astype(bf16)
    input_ref[...] = pltpu.roll(total, start_ref[0], 0)
    layer_ref[...] = pltpu.roll(out_ref[...], start_ref[0], 0)


def update_kernel(rates, *refs):
    for i, rate in enumerate(rates):
        w_ref, g_ref, m_ref, a_ref = refs[4 * i : 4 * i + 4]
        outs = refs[4 * len(rates) + 4 * i : 4 * len(rates) + 4 * i + 4]
        grad = g_ref[...]
        velocity = 0.5 * m_ref[...] + grad
        master = w_ref[...] - rate * (grad + 0.5 * velocity)
        for ref, value in zip(outs, (grad, master, velocity, 0.5 * a_ref[...] + 0.5 * master)):
            ref[...] = value


def update(rates, arrays):
    return pl.pallas_call(
        functools.partial(update_kernel, rates),
        in_specs=[IN_VMEM] * len(arrays),
        out_specs=[IN_VMEM] * len(arrays),
        out_shape=[S(a.shape, f32) for a in arrays],
        compiler_params=params(),
        name="update",
    )(*arrays)


def whole(kernel, name, shapes, *arrays, scalars=()):
    return pl.pallas_call(
        kernel,
        in_specs=[IN_VMEM] * len(arrays) + [pl.BlockSpec(memory_space=pltpu.SMEM)] * len(scalars),
        out_specs=[IN_VMEM] * len(shapes),
        out_shape=[S(*s) for s in shapes],
        compiler_params=params(),
        name=name,
    )(*arrays, *scalars)


def rounded(x):
    return lax.reduce_precision(x, 8, 7)


def packed(bias_rows, gain_rows):
    n = bias_rows.shape[0]
    rows = jnp.stack([jnp.pad(r, ((0, 0), (0, 256 - r.shape[1]))) for r in (bias_rows, gain_rows)], axis=1)
    return jnp.pad(rows, ((0, 0), (0, 6), (0, 0))).reshape(8 * n, 256)


def local(linked, *args):
    (
        features, pos_conv, segment_ids, frame_valid, cotangent,
        qkv_weight, proj_weight, expand_weight, reduce_weight, norm_gains, bias_vector,
        qkv_moment, proj_moment, expand_moment, reduce_moment, gains_moment, bias_moment,
        qkv_average, proj_average, expand_average, reduce_average, gains_average, bias_average,
    ) = args
    ranks = lax.axis_size("dp")
    bias_len = bias_vector.shape[0]
    gain_len = norm_gains.shape[1]
    shards = [qkv_weight, proj_weight, expand_weight, reduce_weight]
    small = packed(rounded(bias_vector)[None], rounded(norm_gains).reshape(1, -1))
    if linked:
        small_full, qkv_full, proj_full, expand_full, reduce_full = gather_all([small] + shards, [f32] + [bf16] * 4)
    else:
        small_full, qkv_full, proj_full, expand_full, reduce_full = [
            lax.all_gather(s, "dp", axis=0, tiled=True) for s in [small] + [w.astype(bf16) for w in shards]
        ]
    small_full = small_full.reshape(ranks, 8, 256)
    bias_full = small_full[:, 0, :bias_len].reshape(-1)
    gains_full = small_full[:, 1, : 2 * gain_len].reshape(ranks, 2, gain_len).transpose(1, 0, 2).reshape(2, D)
    start = rotation(segment_ids)[None]
    entry, entry_low, cot, mask, valid = whole(
        entry_kernel,
        "entry",
        [((TOK, D), f32), ((TOK, D), bf16), ((TOK, D), bf16), ((2, HALF, HALF), f32), ((TOK, 128), f32)],
        features, pos_conv, cotangent, segment_ids, frame_valid, scalars=(start,),
    )
    qkv_bias = jnp.concatenate([bias_full[:D], jnp.zeros((D,), f32), bias_full[D : 2 * D]])[None]
    (qkv,) = whole(qkv_kernel, "qkv", [((TOK, 3 * D), bf16)], entry_low, qkv_full, qkv_bias)
    ctx, probs = attend(qkv, mask)
    vectors = jnp.concatenate(
        [
            bias_full[2 * D : 3 * D][None], bias_full[3 * D + FF : 4 * D + FF][None], gains_full,
            bias_full[4 * D + FF :].reshape(2, D), jnp.zeros((2, D), f32),
        ]
    )
    layer, first, grad_ctx, proj_part, expand_part, reduce_part, dvec, db1 = ffn(
        ctx, entry, cot, proj_full, expand_full, reduce_full, vectors, bias_full[3 * D : 3 * D + FF][None]
    )
    dq, dk, dv = attend_back(qkv, grad_ctx, ctx, probs)
    qkv_part, grad_input, layer_out, sums = whole(
        tail_kernel,
        "tail",
        [((D, 3 * D), bf16), ((TOK, D), bf16), ((TOK, D), bf16), ((8, D), f32)],
        entry_low, dq, dk, dv, qkv_full, first, valid, layer, scalars=(start,),
    )
    bias_part = jnp.concatenate([sums[0], sums[2], dvec[0], db1[0], dvec[1], dvec[4], dvec[5]]).reshape(ranks, bias_len)
    gain_part = dvec[2:4].reshape(2, ranks, gain_len).transpose(1, 0, 2).reshape(ranks, 2 * gain_len)
    parts = [reduce_part, expand_part, proj_part, qkv_part, packed(bias_part, gain_part)]
    if linked:
        parts = scatter_all(parts)
    else:
        parts = [lax.psum_scatter(p.astype(f32), "dp", scatter_dimension=0, tiled=True) for p in parts]
    reduce_grad, expand_grad, proj_grad, qkv_grad, small_grad = parts
    root = math.sqrt(ranks * features.shape[0])
    matrix, proj, little = rate_matrix / root, rate_proj / root, rate_small / root
    updated = update(
        (matrix, proj, matrix, matrix),
        [
            qkv_weight, qkv_grad, qkv_moment, qkv_average,
            proj_weight, proj_grad, proj_moment, proj_average,
            expand_weight, expand_grad, expand_moment, expand_average,
            reduce_weight, reduce_grad, reduce_moment, reduce_average,
        ],
    )

    def nesterov(master, gradient, moment, average):
        velocity = 0.5 * moment + gradient
        renewed = master - little * (gradient + 0.5 * velocity)
        return gradient, renewed, velocity, 0.5 * average + 0.5 * renewed

    gains_new = nesterov(norm_gains, small_grad[1, : 2 * gain_len].reshape(2, gain_len), gains_moment, gains_average)
    bias_new = nesterov(bias_vector, small_grad[0, :bias_len], bias_moment, bias_average)
    results = [layer_out, grad_input]
    for i in range(4):
        results += [updated[i], updated[4 + i], updated[8 + i], updated[12 + i], gains_new[i], bias_new[i]]
    return tuple(results)


def solution(mesh):
    linked = mesh.shape["dp"] == 32
    rows, lanes, line = P("dp", None), P(None, "dp"), P("dp")
    six = (rows, rows, rows, rows, lanes, line)
    return jax.shard_map(
        functools.partial(local, linked),
        mesh=mesh,
        in_specs=(rows,) * 5 + six * 3,
        out_specs=(rows, rows) + six * 4,
        check_vma=False,
    )
```

```python
import functools
import math

import jax
import jax.numpy as jnp
from jax import lax
from jax.experimental import pallas as pl
from jax.experimental.pallas import tpu as pltpu
from jax.sharding import PartitionSpec as P

D = 768
H = 12
HD = 64
FF = 3072
TOK = 1024
HALF = 512
ROWS = 256
COLS = 768

EPSILON = 1e-05
MASKED = -1000000000.0
rate_matrix = 0.04
rate_proj = 0.5
rate_small = 0.2

f32 = jnp.float32
bf16 = jnp.bfloat16
NN = (((1,), (0,)), ((), ()))
NT = (((1,), (1,)), ((), ()))
TN = (((0,), (0,)), ((), ()))
MESH = pl.DeviceIdType.MESH
VMEM_LIMIT = 60 << 20
IN_VMEM = pl.BlockSpec(memory_space=pltpu.VMEM)
IN_HBM = pl.BlockSpec(memory_space=pl.ANY)
S = jax.ShapeDtypeStruct


def dot(a, b, dims):
    return lax.dot_general(a, b, dims, preferred_element_type=f32)


def lane_half(h, shape):
    return (lax.broadcasted_iota(jnp.int32, shape, 1) // HD) == h


def params(**more):
    return pltpu.CompilerParams(vmem_limit_bytes=VMEM_LIMIT, **more)


class Place:
    def __init__(self):
        me = lax.axis_index("dp")
        self.me = me
        self.c, self.x, self.y, self.z = me % 2, (me // 2) % 2, (me // 4) % 2, me // 8
        self.chip = me // 2
        self.partner = me + 1 - 2 * self.c
        self.xn = me + 2 - 4 * self.x
        self.yn = me + 4 - 8 * self.y
        self.up = me + 8
        self.down = me - 8
        z = self.z
        first = jnp.where(z == 0, 1, jnp.where(z == 1, 0, jnp.where(z == 2, 3, 2)))
        second = jnp.where(z == 0, 2, jnp.where(z == 1, 2, 1))
        third = jnp.where(z < 2, 3, 0)
        self.order = (z, first, second, third)

    def other(self, zz, dx=False, dy=False):
        x = 1 - self.x if dx else self.x
        y = 1 - self.y if dy else self.y
        return zz * 4 + y * 2 + x

    def greet(self, *more):
        barrier = pltpu.get_barrier_semaphore()
        for other in (self.partner, self.xn, self.yn, *more):
            pl.semaphore_signal(barrier, inc=1, device_id=(other,), device_id_type=MESH)

        @pl.when(self.z < 3)
        def _():
            pl.semaphore_signal(barrier, inc=1, device_id=(self.up,), device_id_type=MESH)

        @pl.when(self.z > 0)
        def _():
            pl.semaphore_signal(barrier, inc=1, device_id=(self.down,), device_id_type=MESH)

        ends = jnp.where((self.z == 0) | (self.z == 3), 4, 5)
        pl.semaphore_wait(barrier, ends + len(more))


def remote(src, dst, send, recv, other):
    return pltpu.make_async_remote_copy(
        src_ref=src, dst_ref=dst, send_sem=send, recv_sem=recv, device_id=(other,), device_id_type=MESH
    )


def arrived(view, sem):
    pltpu.make_async_copy(view, view, sem).wait()


DMA = pltpu.SemaphoreType.DMA


class Gather:
    def __init__(self, place, shard, full, scratch):
        self.p = place
        self.shard = shard
        self.full = full
        self.rows = 2 * shard.shape[0]
        self.half = shard.shape[1] // 2
        self.stage, self.own, self.ls, self.zs, self.zr, self.xs, self.xr, self.ys, self.yr, self.hs, self.hr, self.ps, self.pr = scratch

    @staticmethod
    def scratch(rows, cols, dtype):
        return [pltpu.VMEM((2 * rows, cols), f32), pltpu.VMEM((2 * rows, cols), dtype), DMA((4,)), DMA((5,))] + [DMA((4,))] * 9

    def cut(self, c):
        return pl.ds(pl.multiple_of(c * self.half, 128), self.half)

    def at(self, chip, count=1):
        start = pl.multiple_of(chip * self.rows, 16)
        return self.full.at[pl.ds(start, count * self.rows), self.cut(self.p.c)]

    def loads(self):
        p = self.p
        mine = self.stage.at[pl.ds(pl.multiple_of(p.c * (self.rows // 2), 8), self.rows // 2)]
        return pltpu.make_async_copy(self.shard, mine, self.ls.at[0]), remote(self.shard, mine, self.ls.at[1], self.ls.at[2], p.partner)

    def keep(self):
        return pltpu.make_async_copy(self.own.at[:, self.cut(self.p.c)], self.at(self.p.chip), self.ls.at[3])

    def along_z(self, k):
        p = self.p
        zz = p.order[k]
        view = self.at(p.other(zz))
        src = view if k else self.own.at[:, self.cut(p.c)]
        up = remote(src, view, self.zs.at[k], self.zr.at[zz], p.up)
        if k == 0:
            down = remote(src, view, self.zs.at[4], self.zr.at[zz], p.down)
            return (p.z < 3, up), (p.z > 0, down)
        down = remote(src, view, self.zs.at[k], self.zr.at[zz], p.down)
        return ((p.z < 3) & (zz < p.z), up), ((p.z > 0) & (zz > p.z), down)

    def across(self, k):
        p = self.p
        zz = p.order[k]
        view = self.at(p.other(zz))
        src = view if k else self.own.at[:, self.cut(p.c)]
        return (
            remote(src, view, self.xs.at[zz], self.xr.at[zz], p.xn),
            remote(src, view, self.ys.at[zz], self.yr.at[zz], p.yn),
        )

    def onward(self, k):
        p = self.p
        zz = p.order[k]
        even = k % 2 == 0
        view = self.at(p.other(zz, dx=even, dy=not even))
        return remote(view, view, self.hs.at[zz], self.hr.at[zz], p.yn if even else p.xn)

    def to_partner(self, k):
        zz = self.p.order[k]
        view = self.at(4 * zz, 4)
        return remote(view, view, self.ps.at[zz], self.pr.at[zz], self.p.partner)

    def load(self):
        for copy in self.loads():
            copy.start()

    def begin(self):
        local, pair = self.loads()
        local.wait()
        pair.wait_recv()
        self.own[...] = self.stage[...].astype(self.own.dtype)
        for cond, copy in self.along_z(0):
            pl.when(cond)(copy.start)
        for copy in self.across(0):
            copy.start()
        self.keep().start()

    def column(self, k):
        zz = self.p.order[k]
        arrived(self.at(self.p.other(zz)), self.zr.at[zz])
        for cond, copy in self.along_z(k):
            pl.when(cond)(copy.start)
        for copy in self.across(k):
            copy.start()

    def plane(self, k):
        p = self.p
        zz = p.order[k]
        even = k % 2 == 0
        arrived(self.at(p.other(zz, dx=even, dy=not even)), (self.xr if even else self.yr).at[zz])
        self.onward(k).start()

    def corner(self, k):
        p = self.p
        zz = p.order[k]
        even = k % 2 == 0
        arrived(self.at(p.other(zz, dx=not even, dy=even)), (self.yr if even else self.xr).at[zz])
        arrived(self.at(p.other(zz, True, True)), self.hr.at[zz])
        if k == 0:
            self.keep().wait()
        self.to_partner(k).start()

    def step(self, s):
        if s == 0:
            self.begin()
        if 1 <= s <= 3:
            self.column(s)
        if 1 <= s <= 4:
            self.plane(s - 1)
        if 2 <= s <= 5:
            self.corner(s - 2)
        if s == 6:
            self.finish()

    def finish(self):
        p = self.p
        for zz in range(4):
            start = pl.multiple_of(4 * zz * self.rows, 16)
            arrived(self.full.at[pl.ds(start, 4 * self.rows), self.cut(1 - p.c)], self.pr.at[zz])
        self.loads()[1].wait_send()
        for k in range(4):
            for cond, copy in self.along_z(k):
                pl.when(cond)(copy.wait_send)
            for copy in self.across(k):
                copy.wait_send()
            self.onward(k).wait_send()
            self.to_partner(k).wait_send()


GATHER_SCRATCH = 13


class Scatter:
    def __init__(self, place, grad, out, scratch):
        self.p = place
        self.grad = grad
        self.out = out
        self.rows = 2 * out.shape[0]
        self.half = out.shape[1] // 2
        self.bp, self.bh, self.bx, self.by, self.bz, self.fin = scratch[:6]
        self.ps, self.pr, self.hs, self.hr, self.xs, self.xr, self.ys, self.yr, self.zs, self.zr, self.fs = scratch[6:]

    @staticmethod
    def scratch(rows, cols, dtype):
        rows, half = 2 * rows, cols // 2
        bufs = [pltpu.VMEM((n * rows, half), dtype) for n in (16, 4, 4, 4, 5)]
        return bufs + [pltpu.VMEM((rows, half), f32)] + [DMA((4,))] * 9 + [DMA((5,)), DMA((3,))]

    def cut(self, c):
        return pl.ds(pl.multiple_of(c * self.half, 128), self.half)

    def span(self, n, count=1):
        return pl.ds(pl.multiple_of(n * self.rows, 16), count * self.rows)

    def at(self, chip):
        return self.grad.at[self.span(chip), self.cut(self.p.c)]

    def slot(self, buf, n):
        return buf.at[self.span(n)]

    def add(self, view, *terms):
        total = view[...].astype(f32)
        for term in terms:
            total = total + term[...].astype(f32)
        view[...] = total.astype(view.dtype)

    def to_partner(self, zz):
        p = self.p
        src = self.grad.at[self.span(4 * zz, 4), self.cut(1 - p.c)]
        return remote(src, self.bp.at[self.span(4 * zz, 4)], self.ps.at[zz], self.pr.at[zz], p.partner)

    def corner(self, k):
        p = self.p
        zz = p.order[k]
        return remote(self.at(p.other(zz, True, True)), self.slot(self.bh, zz), self.hs.at[zz], self.hr.at[zz], p.xn if k % 2 else p.yn)

    def side(self, k, along_x):
        p = self.p
        zz = p.order[k]
        src = self.at(p.other(zz, dx=along_x, dy=not along_x))
        if along_x:
            return remote(src, self.slot(self.bx, zz), self.xs.at[zz], self.xr.at[zz], p.xn)
        return remote(src, self.slot(self.by, zz), self.ys.at[zz], self.yr.at[zz], p.yn)

    def chain(self, k):
        p = self.p
        zz = p.order[k]
        src = self.at(p.other(zz))
        up = remote(src, self.slot(self.bz, zz), self.zs.at[k], self.zr.at[zz], p.up)
        place = jnp.where(zz == p.z - 1, 4, zz)
        down = remote(src, self.slot(self.bz, place), self.zs.at[k], self.zr.at[place], p.down)
        return (zz > p.z, up), (zz < p.z, down)

    def last(self):
        p = self.p
        rows = self.rows // 2
        part = lambda c: self.fin.at[pl.ds(pl.multiple_of(c * rows, 8), rows)]
        dst = self.out.at[:, self.cut(p.c)]
        return pltpu.make_async_copy(part(p.c), dst, self.fs.at[0]), remote(part(1 - p.c), dst, self.fs.at[1], self.fs.at[2], p.partner)

    def step(self, s):
        if s == 0:
            for k in (3, 2, 1, 0):
                self.to_partner(self.p.order[k]).start()
        if 1 <= s <= 4:
            self.pair(4 - s)
        if 2 <= s <= 5:
            self.side_on(5 - s)
        if 3 <= s <= 5:
            self.column(6 - s)
        if s == 6:
            self.total()
        if s == 7:
            self.finish()

    def pair(self, k):
        p = self.p
        zz = p.order[k]
        self.to_partner(zz).wait_recv()

        @pl.loop(0, 4)
        def _(j):
            chip = 4 * zz + j
            self.add(self.at(chip), self.slot(self.bp, chip))

        self.corner(k).start()
        self.side(k, along_x=k % 2 == 1).start()

    def side_on(self, k):
        p = self.p
        zz = p.order[k]
        even = k % 2 == 0
        self.corner(k).wait_recv()
        self.add(self.at(p.other(zz, dx=even, dy=not even)), self.slot(self.bh, zz))
        self.side(k, along_x=even).start()

    def gathered(self, k):
        zz = self.p.order[k]
        self.side(k, True).wait_recv()
        self.side(k, False).wait_recv()
        self.add(self.at(self.p.other(zz)), self.slot(self.bx, zz), self.slot(self.by, zz))

    def column(self, k):
        p = self.p
        zz = p.order[k]
        self.gathered(k)

        @pl.when(((zz > p.z) & (p.z > 0)) | ((zz < p.z) & (p.z < 3)))
        def _():
            arrived(self.slot(self.bz, zz), self.zr.at[zz])
            self.add(self.at(p.other(zz)), self.slot(self.bz, zz))

        for cond, copy in self.chain(k):
            pl.when(cond)(copy.start)

    def total(self):
        p = self.p
        self.gathered(0)
        self.fin[...] = self.at(p.chip)[...].astype(f32)

        @pl.when(p.z > 0)
        def _():
            arrived(self.slot(self.bz, p.z), self.zr.at[p.z])
            self.fin[...] += self.slot(self.bz, p.z)[...].astype(f32)

        @pl.when(p.z < 3)
        def _():
            arrived(self.slot(self.bz, 4), self.zr.at[4])
            self.fin[...] += self.slot(self.bz, 4)[...].astype(f32)

        for copy in self.last():
            copy.start()

    def finish(self):
        p = self.p
        for k in range(4):
            self.to_partner(p.order[k]).wait_send()
            self.corner(k).wait_send()
            self.side(k, True).wait_send()
            self.side(k, False).wait_send()
            if k:
                for cond, copy in self.chain(k):
                    pl.when(cond)(copy.wait_send)
        local, pair = self.last()
        local.wait()
        pair.wait_send()
        arrived(self.out.at[:, self.cut(1 - p.c)], self.fs.at[2])


SCATTER_SCRATCH = 17


def events(plan, it):
    for at, steps in plan.items():

        def now(steps=steps):
            for step in steps:
                step()

        pl.when(it == at)(now)


def looped(count, body, plan=None):
    @pl.loop(0, count)
    def _(it):
        if plan:
            events(plan, it)
        body(it)


def paced(steps, count, first=0):
    plan = {}
    for n, step in enumerate(steps):
        plan.setdefault(first + n * (count - first) // len(steps), []).append(step)
    return plan


def tile(t, size):
    return pl.ds(pl.multiple_of(t * size, size), size)


def rotation(seg):
    counts = [jnp.sum(jnp.where(seg == u, 1.0, 0.0), 1, keepdims=True) for u in range(3)]
    start = counts[0] + counts[1] + counts[2]
    start = jnp.where(counts[2] == HALF, counts[0] + counts[1], start)
    start = jnp.where(counts[1] == HALF, counts[0], start)
    return jnp.where(counts[0] == HALF, 0.0, start)


def turn(t, start, back):
    row = (lax.broadcasted_iota(jnp.int32, (ROWS, TOK), 0) + t * ROWS).astype(f32)
    col = lax.broadcasted_iota(jnp.int32, (ROWS, TOK), 1).astype(f32)
    source = row - start if back else row + start
    source = jnp.where(source < 0.0, source + TOK, jnp.where(source >= TOK, source - TOK, source))
    return jnp.where(source == col, 1.0, 0.0).astype(bf16)


def column_of(row):
    return jnp.broadcast_to(row, (128, row.shape[1])).T


def attend_pair(q, k, v, bias, prob_ref):
    q = q * jnp.bfloat16(0.125)
    outs = []
    for h in range(2):
        qh = jnp.where(lane_half(h, q.shape), q, jnp.bfloat16(0))
        scores = dot(qh, k, NT) + bias
        scores = jnp.exp(scores - jnp.max(scores, 1, keepdims=True))
        probs = (scores * (1.0 / jnp.sum(scores, 1, keepdims=True))).astype(bf16)
        prob_ref[h] = probs
        outs.append(dot(probs, v, NN))
    return jnp.where(lane_half(0, outs[0].shape), outs[0], outs[1]).astype(bf16)


def attend_pair_back(q, k, v, grad, ctx, prob_ref):
    product = grad.astype(f32) * ctx.astype(f32)
    dq, dk, dv = [], [], []
    for h in range(2):
        lanes = lane_half(h, grad.shape)
        grad_h = jnp.where(lanes, grad, jnp.bfloat16(0))
        row_dot = jnp.sum(jnp.where(lanes, product, 0.0), 1, keepdims=True)
        probs = prob_ref[h]
        ds = (probs.astype(f32) * (dot(grad_h, v, NT) - row_dot)).astype(bf16)
        dq.append(dot(ds, k, NN))
        dk.append(dot(ds, q, TN))
        dv.append(dot(probs, grad, TN))
    lanes = lane_half(0, grad.shape)
    return [
        (jnp.where(lanes, dq[0], dq[1]) * 0.125).astype(bf16),
        (jnp.where(lanes, dk[0], dk[1]) * 0.125).astype(bf16),
        jnp.where(lanes, dv[0], dv[1]).astype(bf16),
    ]


def bias_row(small_ref, first, bias_len):
    total = jnp.zeros((8, 1024), f32)
    lanes = lax.broadcasted_iota(jnp.int32, (8, 256), 1)
    for d in range(first // bias_len, (first + D - 1) // bias_len + 1):
        piece = jnp.where(lanes < bias_len, jnp.broadcast_to(small_ref[8 * d : 8 * d + 1, :], (8, 256)), 0.0)
        piece = jnp.concatenate([piece, jnp.zeros((8, 768), f32)], axis=1)
        shift = (bias_len * d - first) % 1024
        total = total + (pltpu.roll(piece, shift, 1) if shift else piece)
    return total[:1, :D]


PAIRS = H // 2


def entry_tile(t, start, stack, feat, pos, cot, entry, low, cot_out):
    rows = tile(t, ROWS)
    matrix = turn(t, start, False)
    valid = dot(matrix, stack, NT)[:, 0:1]
    value = (dot(matrix, feat[...], NN) + dot(matrix, pos[...], NN)) * valid
    entry[rows, :] = value
    low[rows, :] = value.astype(bf16)
    cot_out[rows, :] = dot(matrix, cot[...], NN).astype(bf16)


def mask_half(h, start, stack, mask):
    matrix = jnp.concatenate([turn(2 * h, start, False), turn(2 * h + 1, start, False)], axis=0)
    by_row = dot(stack, matrix, NT)
    by_col = dot(matrix, stack, NT)
    rows = lax.broadcasted_iota(jnp.int32, (HALF, HALF), 0)
    cols = lax.broadcasted_iota(jnp.int32, (HALF, HALF), 1)
    allowed = (by_col[:, 1:2] == by_row[1:2, :]) & ((by_row[0:1, :] > 0.0) | (rows == cols))
    mask[h] = jnp.where(allowed, 0.0, MASKED)


def stack_of(valid, seg):
    row = lax.broadcasted_iota(jnp.int32, (8, TOK), 0)
    both = jnp.where(row == 0, valid.astype(f32), jnp.where(row == 1, seg.astype(f32), 0.0))
    return both.astype(bf16)


def front_kernel(linked, bias_len, *refs):
    n = 5
    shards, refs = refs[:n], refs[n:]
    (feat_in, pos_in, cot_in, seg_ref, valid_ref), refs = refs[:5], refs[5:]
    fulls, refs = refs[:n], refs[n:]
    (entry_out, low_out, cot_out, qkv_out, ctx_out, prob_out), refs = refs[:6], refs[6:]
    (feat, pos, cot_raw, entry, low, cot, mask, small, weight, bias, qkv, ctx, probs, ins, outs, psem), refs = refs[:16], refs[16:]
    loads = [pltpu.make_async_copy(a, b, ins.at[i]) for i, (a, b) in enumerate(((feat_in, feat), (pos_in, pos), (cot_in, cot_raw)))]
    stores = [
        pltpu.make_async_copy(a, b, outs.at[i])
        for i, (a, b) in enumerate(((entry, entry_out), (low, low_out), (cot, cot_out), (qkv, qkv_out), (ctx, ctx_out), (small, fulls[0]), (weight, fulls[1])))
    ]
    for copy in loads:
        copy.start()
    plans = [{}, {}, {}, {}]
    if linked:
        place = Place()
        place.greet()
        homes = [small, weight, *fulls[2:]]
        jobs = [Gather(place, shards[i], homes[i], refs[i * GATHER_SCRATCH : (i + 1) * GATHER_SCRATCH]) for i in range(n)]
        for job in jobs:
            job.load()
        step = lambda i, s: functools.partial(jobs[i].step, s)
        step(1, 0)()
        step(0, 0)()
        waves = [[(1, 1), (0, 1)], [(1, 2), (0, 2)], [(1, 3), (0, 3), (2, 0), (3, 0)], [(1, 4), (0, 4)], [(1, 5), (0, 5)], [(1, 6), (0, 6)]]
        before = [step(*e) for wave in waves for e in wave]
        plans[0] = paced(before[:4], 4)
        middle, late = before[4:10], before[10:]
        after = [
            (2, 1), (3, 1), (4, 0), (2, 2), (3, 2), (2, 3), (4, 1), (3, 3), (2, 4), (4, 2), (3, 4), (2, 5), (4, 3), (3, 5), (2, 6), (4, 4), (3, 6), (4, 5), (4, 6),
        ]
        after = [step(*e) for e in after]
        plans[2] = paced(after[:7], 9)
        plans[3] = paced(after[7:17], 2 * PAIRS)
        end = after[17:]
    else:
        middle, late, end = [], [], []
        for i, (a, b) in enumerate(((shards[0], small), (shards[1], weight))):
            copy = pltpu.make_async_copy(a, b, psem.at[i])
            copy.start()
            copy.wait()
    for copy in loads:
        copy.wait()
    seg = seg_ref[...]
    start = rotation(seg)
    stack = stack_of(valid_ref[...], seg)
    looped(4, lambda t: entry_tile(t, start, stack, feat, pos, cot_raw, entry, low, cot), plans[0])
    for copy in stores[:3]:
        copy.start()
    for h in range(2):
        for run in middle[3 * h : 3 * h + 3]:
            run()
        mask_half(h, start, stack, mask)
    for run in late:
        run()
    bias[0:1, 0:D] = bias_row(small, 0, bias_len)
    bias[0:1, D : 2 * D] = jnp.zeros((1, D), f32)
    bias[0:1, 2 * D : 3 * D] = bias_row(small, D, bias_len)
    if linked:
        for copy in stores[5:]:
            copy.start()

    def project(t):
        cols = tile(t, 256)
        qkv[:, cols] = (dot(low[...], weight[:, cols], NN) + bias[0:1, cols]).astype(bf16)

    looped(9, project, plans[2])
    stores[3].start()

    def prob_store(it):
        return pltpu.make_async_copy(probs.at[it % 2], prob_out.at[pl.ds(2 * it, 2)], psem.at[it % 2])

    def attention(it):
        half, pair = it // PAIRS, it % PAIRS
        rows = tile(half, HALF)
        cut = lambda which: qkv[rows, tile(which * PAIRS + pair, 2 * HD)]

        @pl.when(it >= 2)
        def _():
            prob_store(it - 2).wait()

        ctx[rows, tile(pair, 2 * HD)] = attend_pair(cut(0), cut(1), cut(2), mask[half], probs.at[it % 2])
        prob_store(it).start()

    looped(2 * PAIRS, attention, plans[3])
    stores[4].start()
    for run in end:
        run()
    prob_store(2 * PAIRS - 2).wait()
    prob_store(2 * PAIRS - 1).wait()
    for copy in stores[: 7 if linked else 5]:
        copy.wait()


def front(linked, bias_len, shards, features, pos_conv, cotangent, segments, valid):
    dtypes = [f32] + [bf16] * 4
    fulls = [S((32 * s.shape[0], s.shape[1]) if linked else (8, 128), d) for s, d in zip(shards, dtypes)]
    small_shape = (256, 256) if linked else shards[0].shape
    scratch = [
        pltpu.VMEM((TOK, D), bf16), pltpu.VMEM((TOK, D), bf16), pltpu.VMEM((TOK, D), bf16),
        pltpu.VMEM((TOK, D), f32), pltpu.VMEM((TOK, D), bf16), pltpu.VMEM((TOK, D), bf16),
        pltpu.VMEM((2, HALF, HALF), f32), pltpu.VMEM(small_shape, f32), pltpu.VMEM((D, 3 * D), bf16), pltpu.VMEM((8, 3 * D), f32),
        pltpu.VMEM((TOK, 3 * D), bf16), pltpu.VMEM((TOK, D), bf16), pltpu.VMEM((2, 2, HALF, HALF), bf16),
        DMA((3,)), DMA((7,)), DMA((2,)),
    ]
    if linked:
        scratch += sum([Gather.scratch(*s.shape, d) for s, d in zip(shards, dtypes)], [])
    more = dict(collective_id=0, has_side_effects=True) if linked else {}
    return pl.pallas_call(
        functools.partial(front_kernel, linked, bias_len),
        in_specs=[IN_HBM] * 8 + [IN_VMEM] * 2,
        out_specs=[IN_HBM] * 11,
        out_shape=fulls
        + [S((TOK, D), f32), S((TOK, D), bf16), S((TOK, D), bf16), S((TOK, 3 * D), bf16), S((TOK, D), bf16), S((2 * H, HALF, HALF), bf16)],
        scratch_shapes=scratch,
        compiler_params=params(**more),
        name="front",
    )(*shards, features, pos_conv, cotangent, segments, valid)


def normed_of(residual):
    center = residual - jnp.mean(residual, 1, keepdims=True)
    scale = lax.rsqrt(jnp.mean(center * center, 1, keepdims=True) + EPSILON)
    return center * scale, scale


def norm_back(grad, gain, unit, scale):
    grad = grad * gain
    return scale * (grad - jnp.mean(grad, 1, keepdims=True) - unit * jnp.mean(grad * unit, 1, keepdims=True))


def ffn_kernel(
    ctx_ref, entry_ref, cot_ref, proj_ref, expand_ref, reduce_ref, vec_ref, b1_ref, seg_ref,
    out_ref, first_ref, gctx_ref, dproj_ref, dexpand_ref, dreduce_ref, dvec_ref, db1_ref,
    layer_ref, low_ref, act_ref, gffn_ref, gpre_ref, gbranch_ref, pre_ref, cdf_ref,
):
    dvec_ref[...] = jnp.zeros_like(dvec_ref)
    db1_ref[...] = jnp.zeros_like(db1_ref)
    b_o, b_2, g_1, g_2, c_1, c_2 = [vec_ref[i : i + 1, :] for i in range(6)]

    @pl.loop(0, TOK // ROWS)
    def _(t):
        rows = pl.ds(pl.multiple_of(t * ROWS, ROWS), ROWS)
        unit_1, scale_1 = normed_of(entry_ref[rows, :] + dot(ctx_ref[rows, :], proj_ref[...], NN) + b_o)
        normed = unit_1 * g_1 + c_1
        low = normed.astype(bf16)
        low_ref[rows, :] = low
        total = normed + b_2
        for k in range(FF // COLS):
            cols = slice(k * COLS, (k + 1) * COLS)
            pre = dot(low, expand_ref[:, cols], NN) + b1_ref[:, cols]
            cdf = 0.5 + 0.5 * lax.erf(pre * 0.7071067811865476)
            pre_ref[:, cols] = pre
            cdf_ref[:, cols] = cdf
            act = (pre * cdf).astype(bf16)
            act_ref[rows, cols] = act
            total = total + dot(act, reduce_ref[cols, :], NN)
        unit_2, scale_2 = normed_of(total)
        layer_ref[rows, :] = (unit_2 * g_2 + c_2).astype(bf16)
        grad = cot_ref[rows, :].astype(f32)
        dvec_ref[3:4, :] += jnp.sum(grad * unit_2, 0, keepdims=True)
        dvec_ref[5:6, :] += jnp.sum(grad, 0, keepdims=True)
        total = norm_back(grad, g_2, unit_2, scale_2)
        gffn = total.astype(bf16)
        gffn_ref[rows, :] = gffn
        dvec_ref[1:2, :] += jnp.sum(gffn.astype(f32), 0, keepdims=True)
        for k in range(FF // COLS):
            cols = slice(k * COLS, (k + 1) * COLS)
            pre = pre_ref[:, cols]
            slope = cdf_ref[:, cols] + pre * (0.3989422804014327 * jnp.exp(-0.5 * pre * pre))
            gpre = (dot(gffn, reduce_ref[cols, :], NT) * slope).astype(bf16)
            gpre_ref[rows, cols] = gpre
            db1_ref[:, cols] += jnp.sum(gpre.astype(f32), 0, keepdims=True)
            total = total + dot(gpre, expand_ref[:, cols], NT)
        dvec_ref[2:3, :] += jnp.sum(total * unit_1, 0, keepdims=True)
        dvec_ref[4:5, :] += jnp.sum(total, 0, keepdims=True)
        first = norm_back(total, g_1, unit_1, scale_1)
        first_ref[rows, :] = first
        branch = first.astype(bf16)
        gbranch_ref[rows, :] = branch
        dvec_ref[0:1, :] += jnp.sum(branch.astype(f32), 0, keepdims=True)
        gctx_ref[rows, :] = dot(branch, proj_ref[...], NT).astype(bf16)

    start = rotation(seg_ref[...])

    @pl.loop(0, TOK // ROWS)
    def _(t):
        out_ref[tile(t, ROWS), :] = dot(turn(t, start, True), layer_ref[...], NN).astype(bf16)

    @pl.loop(0, FF // 256)
    def _(t):
        part = pl.ds(pl.multiple_of(t * 256, 256), 256)
        dreduce_ref[part, :] = dot(act_ref[:, part], gffn_ref[...], TN).astype(bf16)
        dexpand_ref[:, part] = dot(low_ref[...], gpre_ref[:, part], TN).astype(bf16)

    @pl.loop(0, D // 256)
    def _(t):
        part = pl.ds(pl.multiple_of(t * 256, 256), 256)
        dproj_ref[part, :] = dot(ctx_ref[:, part], gbranch_ref[...], TN).astype(bf16)


def ffn(*arrays):
    return pl.pallas_call(
        ffn_kernel,
        in_specs=[IN_VMEM] * 9,
        out_specs=[IN_VMEM] * 8,
        out_shape=[
            S((TOK, D), bf16), S((TOK, D), f32), S((TOK, D), bf16), S((D, D), bf16),
            S((D, FF), bf16), S((FF, D), bf16), S((8, D), f32), S((1, FF), f32),
        ],
        scratch_shapes=[
            pltpu.VMEM((TOK, D), bf16), pltpu.VMEM((TOK, D), bf16), pltpu.VMEM((TOK, FF), bf16), pltpu.VMEM((TOK, D), bf16), pltpu.VMEM((TOK, FF), bf16),
            pltpu.VMEM((TOK, D), bf16), pltpu.VMEM((ROWS, FF), f32), pltpu.VMEM((ROWS, FF), f32),
        ],
        compiler_params=pltpu.CompilerParams(vmem_limit_bytes=62 << 20),
        name="ffn",
    )(*arrays)


class Exchange:
    def __init__(self, place, total, slots, send, recv):
        z = place.z
        self.others = (place.partner, place.xn, place.yn, place.me + 8 - 16 * (z % 2), place.me + 16 - 32 * (z // 2))
        self.total, self.slots, self.send, self.recv = total, slots, send, recv

    def copy(self, n):
        return remote(self.slots.at[n], self.slots.at[5 + n], self.send.at[n], self.recv.at[n], self.others[n])

    def begin(self, n):
        self.slots[n] = self.total[...]
        self.copy(n).start()

    def end(self, n):
        self.copy(n).wait()
        self.total[...] += self.slots[5 + n]


VECTOR_ROWS = 72


def put(vector, row, value):
    for i in range(value.shape[1] // 128):
        vector[row + i : row + i + 1, :] = value[:, 128 * i : 128 * (i + 1)]


def back_kernel(linked, *refs):
    n = 3
    parts, refs = refs[:n], refs[n:]
    (qkv_in, grad_in, ctx_in, prob_in, low_in, weight_in, first_in, dvec_ref, db1_ref, seg_ref, valid_ref), refs = refs[:11], refs[11:]
    if linked:
        outs, refs = refs[: n + 1], refs[n + 1 :]
    else:
        (qkv_part,), refs = refs[:1], refs[1:]
    (vector, input_out), refs = refs[:2], refs[2:]
    (qkv, grad, ctx, probs, low, weight, first, dqkv, inner, ins, psem), refs = refs[:11], refs[11:]
    loads = [
        pltpu.make_async_copy(a, b, ins.at[i])
        for i, (a, b) in enumerate(((qkv_in, qkv), (grad_in, grad), (ctx_in, ctx), (low_in, low), (weight_in, weight), (first_in, first)))
    ]

    def prob_load(it):
        return pltpu.make_async_copy(prob_in.at[pl.ds(2 * it, 2)], probs.at[it % 2], psem.at[it % 2])

    for copy in loads[:3]:
        copy.start()
    prob_load(0).start()
    plans = [{}, {}, {}]
    end = []
    if linked:
        (slots, send, recv), refs = refs[:3], refs[3:]
        each = SCATTER_SCRATCH + 1
        place = Place()
        held = [refs[i * each] for i in range(n + 1)]
        jobs = [Scatter(place, held[i], outs[i], refs[i * each + 1 : (i + 1) * each]) for i in range(n + 1)]
        swap = Exchange(place, vector, slots, send, recv)
        fetch = [pltpu.make_async_copy(parts[i], held[i], ins.at[6 + i]) for i in range(n)]
        for copy in fetch:
            copy.start()
        place.greet(swap.others[4])
        for i in range(n):
            fetch[i].wait()
            jobs[i].step(0)
        qkv_part = held[n]
        r, e, p, q = jobs
        do = lambda f, *a: functools.partial(f, *a)
        plans[0] = paced(
            [
                do(r.pair, 3), do(r.pair, 2), do(r.pair, 1), do(r.side_on, 3), do(r.pair, 0), do(r.side_on, 2), do(e.pair, 3), do(r.side_on, 1),
                do(e.pair, 2), do(r.side_on, 0), do(e.pair, 1), do(r.column, 3),
            ],
            2 * PAIRS,
        )
        plans[1] = paced([do(e.side_on, 3), do(e.pair, 0), do(r.column, 2), do(e.side_on, 2)], 9)
        plans[2] = paced([do(e.side_on, 1), do(p.pair, 3), do(r.column, 1), do(e.side_on, 0)], 4)
        end = [
            do(p.pair, 2), do(p.pair, 1), do(e.column, 3), do(p.side_on, 3), do(p.pair, 0), do(r.total), do(p.side_on, 2), do(q.pair, 3), do(p.side_on, 1),
            do(e.column, 2), do(q.pair, 2), do(p.side_on, 0), do(e.column, 1), do(q.side_on, 3), do(q.pair, 1), do(p.column, 3), do(q.side_on, 2), do(q.pair, 0),
            do(e.total), do(p.column, 2), do(swap.end, 0), do(swap.begin, 1), do(q.side_on, 1), do(q.column, 3), do(p.column, 1),
            do(swap.end, 1), do(swap.begin, 2), do(q.side_on, 0), do(q.column, 2), do(swap.end, 2), do(swap.begin, 3), do(p.total),
            do(q.column, 1), do(swap.end, 3), do(swap.begin, 4), do(q.total), do(swap.end, 4), do(r.finish), do(e.finish), do(p.finish), do(q.finish),
        ]
    for copy in loads[3:]:
        copy.start()
    for copy in loads[:3]:
        copy.wait()

    def attention(it):
        half, pair = it // PAIRS, it % PAIRS
        rows = tile(half, HALF)
        cut = lambda ref, which: ref[rows, tile(which * PAIRS + pair, 2 * HD)]

        @pl.when(it < 2 * PAIRS - 1)
        def _():
            prob_load(it + 1).start()

        prob_load(it).wait()
        three = attend_pair_back(cut(qkv, 0), cut(qkv, 1), cut(qkv, 2), cut(grad, 0), cut(ctx, 0), probs.at[it % 2])
        for which, value in enumerate(three):
            dqkv[rows, tile(which * PAIRS + pair, 2 * HD)] = value

    looped(2 * PAIRS, attention, plans[0])
    for copy in loads[3:]:
        copy.wait()

    def weight_grad(t):
        cols = tile(t, 256)
        qkv_part[:, cols] = dot(low[...], dqkv[:, cols], TN).astype(bf16)

    looped(9, weight_grad, plans[1])
    for which, row in ((0, 0), (2, 6)):
        put(vector, row, jnp.sum(dqkv[:, which * D : (which + 1) * D].astype(f32), 0, keepdims=True))
    put(vector, 18, db1_ref[...])
    for row, at in ((0, 12), (1, 42), (4, 48), (5, 54), (2, 60), (3, 66)):
        put(vector, at, dvec_ref[row : row + 1, :])
    if linked:
        jobs[n].step(0)
        swap.begin(0)

    def input_grad(t):
        rows = tile(t, ROWS)
        inner[rows, :] = (first[rows, :] + dot(dqkv[rows, :], weight[...], NT)).astype(bf16)

    looped(4, input_grad, plans[2])
    start = rotation(seg_ref[...])

    def turn_back(t):
        rows = tile(t, ROWS)
        input_out[rows, :] = dot(turn(t, start, True), inner[...], NN).astype(bf16)

    looped(4, turn_back)
    input_out[...] = input_out[...] * column_of(valid_ref[...].astype(f32))[:, :1].astype(bf16)
    for run in end:
        run()


def back(linked, parts, *arrays):
    shapes = [p.shape for p in parts] + [(D, 3 * D)]
    outs = [S((r // 32, c), f32) for r, c in shapes] if linked else [S((D, 3 * D), bf16)]
    outs += [S((VECTOR_ROWS, 128), f32), S((TOK, D), bf16)]
    scratch = [
        pltpu.VMEM((TOK, 3 * D), bf16), pltpu.VMEM((TOK, D), bf16), pltpu.VMEM((TOK, D), bf16), pltpu.VMEM((2, 2, HALF, HALF), bf16),
        pltpu.VMEM((TOK, D), bf16), pltpu.VMEM((D, 3 * D), bf16), pltpu.VMEM((TOK, D), f32), pltpu.VMEM((TOK, 3 * D), bf16),
        pltpu.VMEM((TOK, D), bf16), DMA((9,)), DMA((2,)),
    ]
    more = {}
    if linked:
        more = dict(collective_id=1, has_side_effects=True)
        scratch += [pltpu.VMEM((10, VECTOR_ROWS, 128), f32), DMA((5,)), DMA((5,))]
        for r, c in shapes:
            scratch += [pltpu.VMEM((r, c), bf16)] + Scatter.scratch(r // 32, c, bf16)
    return pl.pallas_call(
        functools.partial(back_kernel, linked),
        in_specs=[IN_HBM] * 10 + [IN_VMEM] * 4,
        out_specs=[IN_VMEM] * len(outs),
        out_shape=outs,
        scratch_shapes=scratch,
        compiler_params=params(**more),
        name="back",
    )(*parts, *arrays)


def update_kernel(rates, *refs):
    for i, rate in enumerate(rates):
        w_ref, g_ref, m_ref, a_ref = refs[4 * i : 4 * i + 4]
        outs = refs[4 * len(rates) + 4 * i : 4 * len(rates) + 4 * i + 4]
        grad = g_ref[...]
        velocity = 0.5 * m_ref[...] + grad
        master = w_ref[...] - rate * (grad + 0.5 * velocity)
        for ref, value in zip(outs, (grad, master, velocity, 0.5 * a_ref[...] + 0.5 * master)):
            ref[...] = value


def update(rates, arrays):
    return pl.pallas_call(
        functools.partial(update_kernel, rates),
        in_specs=[IN_VMEM] * len(arrays),
        out_specs=[IN_VMEM] * len(arrays),
        out_shape=[S(a.shape, f32) for a in arrays],
        compiler_params=params(),
        name="update",
    )(*arrays)


def rounded(x):
    return lax.reduce_precision(x, 8, 7)


def local(linked, *args):
    (
        features, pos_conv, segment_ids, frame_valid, cotangent,
        qkv_weight, proj_weight, expand_weight, reduce_weight, norm_gains, bias_vector,
        qkv_moment, proj_moment, expand_moment, reduce_moment, gains_moment, bias_moment,
        qkv_average, proj_average, expand_average, reduce_average, gains_average, bias_average,
    ) = args
    ranks = lax.axis_size("dp")
    me = lax.axis_index("dp")
    bias_len = bias_vector.shape[0]
    gain_len = norm_gains.shape[1]
    small = jnp.stack([jnp.pad(rounded(r), (0, 256 - r.shape[0])) for r in (bias_vector, norm_gains.reshape(-1))])
    small = jnp.pad(small, ((0, 6), (0, 0)))
    shards = [small, qkv_weight, proj_weight, expand_weight, reduce_weight]
    if not linked:
        shards = [lax.all_gather(s, "dp", axis=0, tiled=True) for s in [small] + [w.astype(bf16) for w in shards[1:]]]
    *fulls, entry, entry_low, cot, qkv, ctx, probs = front(
        linked, bias_len, shards, features, pos_conv, cotangent, segment_ids, frame_valid
    )
    small_full, qkv_full, proj_full, expand_full, reduce_full = fulls if linked else shards
    small_full = small_full.reshape(ranks, 8, 256)
    bias_full = small_full[:, 0, :bias_len].reshape(-1)
    gains_full = small_full[:, 1, : 2 * gain_len].reshape(ranks, 2, gain_len).transpose(1, 0, 2).reshape(2, D)
    vectors = jnp.concatenate(
        [
            bias_full[2 * D : 3 * D][None], bias_full[3 * D + FF : 4 * D + FF][None], gains_full,
            bias_full[4 * D + FF :].reshape(2, D), jnp.zeros((2, D), f32),
        ]
    )
    layer_out, first, grad_ctx, proj_part, expand_part, reduce_part, dvec, db1 = ffn(
        ctx, entry, cot, proj_full, expand_full, reduce_full, vectors, bias_full[3 * D : 3 * D + FF][None], segment_ids
    )
    parts = [reduce_part, expand_part, proj_part]
    *sums, vector, grad_input = back(
        linked, parts, qkv, grad_ctx, ctx, probs, entry_low, qkv_full, first, dvec, db1, segment_ids, frame_valid
    )
    if not linked:
        sums = [lax.psum_scatter(p.astype(f32), "dp", scatter_dimension=0, tiled=True) for p in parts + sums]
        vector = lax.psum(vector, "dp")
    reduce_grad, expand_grad, proj_grad, qkv_grad = sums
    vector = vector.reshape(-1)
    bias_grad = lax.dynamic_slice(vector, (me * bias_len,), (bias_len,))
    gains_grad = lax.dynamic_slice(vector[6 * D + FF :].reshape(2, D), (0, me * gain_len), (2, gain_len))
    root = math.sqrt(ranks * features.shape[0])
    matrix, proj, little = rate_matrix / root, rate_proj / root, rate_small / root
    updated = update(
        (matrix, proj, matrix, matrix),
        [
            qkv_weight, qkv_grad, qkv_moment, qkv_average,
            proj_weight, proj_grad, proj_moment, proj_average,
            expand_weight, expand_grad, expand_moment, expand_average,
            reduce_weight, reduce_grad, reduce_moment, reduce_average,
        ],
    )

    def nesterov(master, gradient, moment, average):
        velocity = 0.5 * moment + gradient
        renewed = master - little * (gradient + 0.5 * velocity)
        return gradient, renewed, velocity, 0.5 * average + 0.5 * renewed

    gains_new = nesterov(norm_gains, gains_grad, gains_moment, gains_average)
    bias_new = nesterov(bias_vector, bias_grad, bias_moment, bias_average)
    results = [layer_out, grad_input]
    for i in range(4):
        results += [updated[i], updated[4 + i], updated[8 + i], updated[12 + i], gains_new[i], bias_new[i]]
    return tuple(results)


def solution(mesh):
    linked = mesh.shape["dp"] == 32
    rows, lanes, line = P("dp", None), P(None, "dp"), P("dp")
    six = (rows, rows, rows, rows, lanes, line)
    return jax.shard_map(
        functools.partial(local, linked),
        mesh=mesh,
        in_specs=(rows,) * 5 + six * 3,
        out_specs=(rows, rows) + six * 4,
        check_vma=False,
    )
```

```python
import functools
import math

import jax
import jax.numpy as jnp
from jax import lax
from jax.experimental import pallas as pl
from jax.experimental.pallas import tpu as pltpu
from jax.sharding import PartitionSpec as P

D = 768
H = 12
HD = 64
FF = 3072
TOK = 1024
HALF = 512
SPREAD, LAG = 1.6, 3.0
GATHER_SPREAD, GATHER_LAG = 1.0, 2.0
ROWS = 256
COLS = 768

EPSILON = 1e-05
MASKED = -1000000000.0
rate_matrix = 0.04
rate_proj = 0.5
rate_small = 0.2

f32 = jnp.float32
bf16 = jnp.bfloat16
NN = (((1,), (0,)), ((), ()))
NT = (((1,), (1,)), ((), ()))
TN = (((0,), (0,)), ((), ()))
MESH = pl.DeviceIdType.MESH
VMEM_LIMIT = 60 << 20
IN_VMEM = pl.BlockSpec(memory_space=pltpu.VMEM)
IN_HBM = pl.BlockSpec(memory_space=pl.ANY)
S = jax.ShapeDtypeStruct


def dot(a, b, dims):
    return lax.dot_general(a, b, dims, preferred_element_type=f32)


def lane_half(h, shape):
    return (lax.broadcasted_iota(jnp.int32, shape, 1) // HD) == h


def params(**more):
    return pltpu.CompilerParams(vmem_limit_bytes=VMEM_LIMIT, **more)


class Place:
    def __init__(self):
        me = lax.axis_index("dp")
        self.me = me
        self.c, self.x, self.y, self.z = me % 2, (me // 2) % 2, (me // 4) % 2, me // 8
        self.chip = me // 2
        self.partner = me + 1 - 2 * self.c
        self.xn = me + 2 - 4 * self.x
        self.yn = me + 4 - 8 * self.y
        self.up = me + 8
        self.down = me - 8
        z = self.z
        first = jnp.where(z == 0, 1, jnp.where(z == 1, 0, jnp.where(z == 2, 3, 2)))
        second = jnp.where(z == 0, 2, jnp.where(z == 1, 2, 1))
        third = jnp.where(z < 2, 3, 0)
        self.order = (z, first, second, third)

    def other(self, zz, dx=False, dy=False):
        x = 1 - self.x if dx else self.x
        y = 1 - self.y if dy else self.y
        return zz * 4 + y * 2 + x

    def greet(self, *more):
        barrier = pltpu.get_barrier_semaphore()
        for other in (self.partner, self.xn, self.yn, *more):
            pl.semaphore_signal(barrier, inc=1, device_id=(other,), device_id_type=MESH)

        @pl.when(self.z < 3)
        def _():
            pl.semaphore_signal(barrier, inc=1, device_id=(self.up,), device_id_type=MESH)

        @pl.when(self.z > 0)
        def _():
            pl.semaphore_signal(barrier, inc=1, device_id=(self.down,), device_id_type=MESH)

        ends = jnp.where((self.z == 0) | (self.z == 3), 4, 5)
        pl.semaphore_wait(barrier, ends + len(more))


def remote(src, dst, send, recv, other):
    return pltpu.make_async_remote_copy(
        src_ref=src, dst_ref=dst, send_sem=send, recv_sem=recv, device_id=(other,), device_id_type=MESH
    )


def arrived(view, sem):
    pltpu.make_async_copy(view, view, sem).wait()


DMA = pltpu.SemaphoreType.DMA


class Gather:
    def __init__(self, place, shard, full, strips, scratch):
        self.p = place
        self.shard = shard
        self.full = full
        self.strips = strips
        self.rows = 2 * shard.shape[0]
        self.half = full.shape[1] // 2
        self.stage, self.own, self.ls, self.zs, self.zr, self.xs, self.xr, self.ys, self.yr, self.hs, self.hr, self.ps, self.pr = scratch

    @staticmethod
    def scratch(rows, cols, dtype):
        return [pltpu.VMEM((2 * rows, cols), f32), pltpu.VMEM((2 * rows, cols), dtype), DMA((10,)), DMA((5,))] + [DMA((4,))] * 9

    def cut(self, c):
        return pl.ds(pl.multiple_of(c * self.half, 128), self.half)

    def at(self, chip, count=1):
        start = pl.multiple_of(chip * self.rows, 16)
        return self.full.at[pl.ds(start, count * self.rows), self.cut(self.p.c)]

    def loads(self):
        p = self.p
        rows = pl.ds(pl.multiple_of(p.c * (self.rows // 2), 8), self.rows // 2)
        pairs = []
        for n, (src, dst, width) in enumerate(self.strips):
            part, mine = self.shard.at[:, src : src + width], self.stage.at[rows, dst : dst + width]
            pairs.append(
                (
                    pltpu.make_async_copy(part, mine, self.ls.at[3 * n]),
                    remote(part, mine, self.ls.at[3 * n + 1], self.ls.at[3 * n + 2], p.partner),
                )
            )
        return pairs

    def keep(self):
        return pltpu.make_async_copy(self.own.at[:, self.cut(self.p.c)], self.at(self.p.chip), self.ls.at[9])

    def along_z(self, k):
        p = self.p
        zz = p.order[k]
        view = self.at(p.other(zz))
        src = view if k else self.own.at[:, self.cut(p.c)]
        up = remote(src, view, self.zs.at[k], self.zr.at[zz], p.up)
        if k == 0:
            down = remote(src, view, self.zs.at[4], self.zr.at[zz], p.down)
            return (p.z < 3, up), (p.z > 0, down)
        down = remote(src, view, self.zs.at[k], self.zr.at[zz], p.down)
        return ((p.z < 3) & (zz < p.z), up), ((p.z > 0) & (zz > p.z), down)

    def across(self, k):
        p = self.p
        zz = p.order[k]
        view = self.at(p.other(zz))
        src = view if k else self.own.at[:, self.cut(p.c)]
        return (
            remote(src, view, self.xs.at[zz], self.xr.at[zz], p.xn),
            remote(src, view, self.ys.at[zz], self.yr.at[zz], p.yn),
        )

    def onward(self, k):
        p = self.p
        zz = p.order[k]
        even = k % 2 == 0
        view = self.at(p.other(zz, dx=even, dy=not even))
        return remote(view, view, self.hs.at[zz], self.hr.at[zz], p.yn if even else p.xn)

    def to_partner(self, k):
        zz = self.p.order[k]
        view = self.at(4 * zz, 4)
        return remote(view, view, self.ps.at[zz], self.pr.at[zz], self.p.partner)

    def load(self):
        for local, pair in self.loads():
            local.start()
            pair.start()

    def begin(self):
        for local, pair in self.loads():
            local.wait()
            pair.wait_recv()
        self.own[...] = self.stage[...].astype(self.own.dtype)
        for cond, copy in self.along_z(0):
            pl.when(cond)(copy.start)
        for copy in self.across(0):
            copy.start()
        self.keep().start()

    def column(self, k):
        zz = self.p.order[k]
        arrived(self.at(self.p.other(zz)), self.zr.at[zz])
        for cond, copy in self.along_z(k):
            pl.when(cond)(copy.start)
        for copy in self.across(k):
            copy.start()

    def plane(self, k):
        p = self.p
        zz = p.order[k]
        even = k % 2 == 0
        arrived(self.at(p.other(zz, dx=even, dy=not even)), (self.xr if even else self.yr).at[zz])
        self.onward(k).start()

    def corner(self, k):
        p = self.p
        zz = p.order[k]
        even = k % 2 == 0
        arrived(self.at(p.other(zz, dx=not even, dy=even)), (self.yr if even else self.xr).at[zz])
        arrived(self.at(p.other(zz, True, True)), self.hr.at[zz])
        if k == 0:
            self.keep().wait()
        self.to_partner(k).start()

    def arrive(self, k):
        p = self.p
        zz = p.order[k]
        start = pl.multiple_of(4 * zz * self.rows, 16)
        arrived(self.full.at[pl.ds(start, 4 * self.rows), self.cut(1 - p.c)], self.pr.at[zz])

    def arrive_all(self):
        for k in range(4):
            self.arrive(k)

    def drain(self):
        for local, pair in self.loads():
            pair.wait_send()
        for k in range(4):
            for cond, copy in self.along_z(k):
                pl.when(cond)(copy.wait_send)
            for copy in self.across(k):
                copy.wait_send()
            self.onward(k).wait_send()
            self.to_partner(k).wait_send()

    def timetable(self, begin, unit):
        do = functools.partial
        u, lag = unit * GATHER_SPREAD, GATHER_LAG
        c1 = begin + u + lag
        c2, c3 = c1 + u + lag, c1 + 2 * (u + lag)
        p0, p1, p2, p3 = c1, c1 + 2 * u + lag, c2 + 2 * u + lag, c3 + 2 * u + lag
        hop = 2 * u + lag
        return [
            (begin, self.begin),
            (c1, do(self.column, 1)),
            (p0, do(self.plane, 0)),
            (c2, do(self.column, 2)),
            (p0 + hop, do(self.corner, 0)),
            (p1, do(self.plane, 1)),
            (c3, do(self.column, 3)),
            (p2, do(self.plane, 2)),
            (p1 + hop, do(self.corner, 1)),
            (p3, do(self.plane, 3)),
            (p2 + hop, do(self.corner, 2)),
            (p3 + hop, do(self.corner, 3)),
        ]


GATHER_SCRATCH = 13


class Scatter:
    def __init__(self, place, grad, out, scratch):
        self.p = place
        self.grad = grad
        self.out = out
        self.rows = 2 * out.shape[0]
        self.half = out.shape[1] // 2
        self.bp, self.bh, self.bx, self.by, self.bz, self.fin = scratch[:6]
        self.ps, self.pr, self.hs, self.hr, self.xs, self.xr, self.ys, self.yr, self.zs, self.zr, self.fs = scratch[6:]

    @staticmethod
    def scratch(rows, cols, dtype):
        rows, half = 2 * rows, cols // 2
        bufs = [pltpu.VMEM((n * rows, half), dtype) for n in (16, 4, 4, 4, 5)]
        return bufs + [pltpu.VMEM((rows, half), f32)] + [DMA((4,))] * 9 + [DMA((5,)), DMA((3,))]

    def cut(self, c):
        return pl.ds(pl.multiple_of(c * self.half, 128), self.half)

    def span(self, n, count=1):
        return pl.ds(pl.multiple_of(n * self.rows, 16), count * self.rows)

    def at(self, chip):
        return self.grad.at[self.span(chip), self.cut(self.p.c)]

    def slot(self, buf, n):
        return buf.at[self.span(n)]

    def add(self, view, *terms):
        total = view[...].astype(f32)
        for term in terms:
            total = total + term[...].astype(f32)
        view[...] = total.astype(view.dtype)

    def to_partner(self, zz):
        p = self.p
        src = self.grad.at[self.span(4 * zz, 4), self.cut(1 - p.c)]
        return remote(src, self.bp.at[self.span(4 * zz, 4)], self.ps.at[zz], self.pr.at[zz], p.partner)

    def corner(self, k):
        p = self.p
        zz = p.order[k]
        return remote(self.at(p.other(zz, True, True)), self.slot(self.bh, zz), self.hs.at[zz], self.hr.at[zz], p.xn if k % 2 else p.yn)

    def side(self, k, along_x):
        p = self.p
        zz = p.order[k]
        src = self.at(p.other(zz, dx=along_x, dy=not along_x))
        if along_x:
            return remote(src, self.slot(self.bx, zz), self.xs.at[zz], self.xr.at[zz], p.xn)
        return remote(src, self.slot(self.by, zz), self.ys.at[zz], self.yr.at[zz], p.yn)

    def chain(self, k):
        p = self.p
        zz = p.order[k]
        src = self.at(p.other(zz))
        up = remote(src, self.slot(self.bz, zz), self.zs.at[k], self.zr.at[zz], p.up)
        place = jnp.where(zz == p.z - 1, 4, zz)
        down = remote(src, self.slot(self.bz, place), self.zs.at[k], self.zr.at[place], p.down)
        return (zz > p.z, up), (zz < p.z, down)

    def last(self):
        p = self.p
        rows = self.rows // 2
        part = lambda c: self.fin.at[pl.ds(pl.multiple_of(c * rows, 8), rows)]
        dst = self.out.at[:, self.cut(p.c)]
        return pltpu.make_async_copy(part(p.c), dst, self.fs.at[0]), remote(part(1 - p.c), dst, self.fs.at[1], self.fs.at[2], p.partner)

    def exchange(self, k):
        self.to_partner(self.p.order[k]).start()

    def timetable(self, begin, unit):
        do = functools.partial
        u, lag = unit * SPREAD, LAG
        e = [begin + 1 + 0.35 * u * (n + 1) for n in range(4)]
        side = [e[0] + u + lag, e[1] + u + lag, e[0] + 3 * u + lag, e[1] + 3.5 * u + lag]
        full = [e[1] + 3 * u + lag, e[0] + 3.5 * u + lag, e[0] + 5.5 * u + lag, e[0] + 6.5 * u + lag]
        relay = [full[0] + u + lag, full[1] + u + lag]
        relay.append(max(relay[0] + u + lag, full[2] + 0.1))
        steps = [(max(relay[2] + u + lag, full[3]), self.total)]
        for n, k in enumerate((3, 2, 1, 0)):
            steps.append((e[n], do(self.pair, k)))
            steps.append((side[n], do(self.side_on, k)))
            if k:
                steps.append((full[n], do(self.column, k)))
                steps.append((relay[n], do(self.relay, k)))
        return steps

    def pair(self, k):
        p = self.p
        zz = p.order[k]
        self.to_partner(zz).wait_recv()

        @pl.loop(0, 4)
        def _(j):
            chip = 4 * zz + j
            self.add(self.at(chip), self.slot(self.bp, chip))

        self.corner(k).start()
        self.side(k, along_x=k % 2 == 1).start()

    def side_on(self, k):
        p = self.p
        zz = p.order[k]
        even = k % 2 == 0
        self.corner(k).wait_recv()
        self.add(self.at(p.other(zz, dx=even, dy=not even)), self.slot(self.bh, zz))
        self.side(k, along_x=even).start()

    def gathered(self, k):
        zz = self.p.order[k]
        self.side(k, True).wait_recv()
        self.side(k, False).wait_recv()
        self.add(self.at(self.p.other(zz)), self.slot(self.bx, zz), self.slot(self.by, zz))

    def column(self, k):
        p = self.p
        zz = p.order[k]
        self.gathered(k)
        ends = (p.z == 0) | (p.z == 3)
        for cond, copy in self.chain(k):
            pl.when(cond & ends)(copy.start)

    def relay(self, k):
        p = self.p
        zz = p.order[k]

        @pl.when((p.z == 1) | (p.z == 2))
        def _():
            arrived(self.slot(self.bz, zz), self.zr.at[zz])
            self.add(self.at(p.other(zz)), self.slot(self.bz, zz))
            for cond, copy in self.chain(k):
                pl.when(cond)(copy.start)

    def total(self):
        p = self.p
        self.gathered(0)
        self.fin[...] = self.at(p.chip)[...].astype(f32)

        @pl.when(p.z > 0)
        def _():
            arrived(self.slot(self.bz, p.z), self.zr.at[p.z])
            self.fin[...] += self.slot(self.bz, p.z)[...].astype(f32)

        @pl.when(p.z < 3)
        def _():
            arrived(self.slot(self.bz, 4), self.zr.at[4])
            self.fin[...] += self.slot(self.bz, 4)[...].astype(f32)

        for copy in self.last():
            copy.start()

    def finish(self):
        p = self.p
        for k in range(4):
            self.to_partner(p.order[k]).wait_send()
            self.corner(k).wait_send()
            self.side(k, True).wait_send()
            self.side(k, False).wait_send()
            if k:
                for cond, copy in self.chain(k):
                    pl.when(cond)(copy.wait_send)
        local, pair = self.last()
        local.wait()
        pair.wait_send()
        arrived(self.out.at[:, self.cut(1 - p.c)], self.fs.at[2])


SCATTER_SCRATCH = 17


DELAY_P, DELAY_E, DELAY_T = 3.0, -1.5, 2.0
TIMES = ((0, 0.8), (1, 0.8), (3, 0.8), (6, 0.8), (8, 3.2), (22, 3.2), (0.1, 0.3))


class Steps:
    def __init__(self):
        self.queue = []
        self.clock = 0.0

    def add(self, steps):
        self.queue = sorted(self.queue + steps, key=lambda step: step[0])

    def due(self):
        now = [step for time, step in self.queue if time <= self.clock]
        self.queue = [entry for entry in self.queue if entry[0] > self.clock]
        return now

    def run(self, spend=0.0):
        for step in self.due():
            step()
        self.clock += spend

    def until(self, last):
        while self.queue:
            time, step = self.queue.pop(0)
            step()
            if step is last:
                return

    def loop(self, count, spend, body):
        plan = {}
        for it in range(count):
            plan[it] = self.due()
            self.clock += spend

        @pl.loop(0, count)
        def _(it):
            for at, steps in plan.items():
                if steps:

                    def now(steps=steps):
                        for step in steps:
                            step()

                    pl.when(it == at)(now)
            body(it)


def tile(t, size):
    return pl.ds(pl.multiple_of(t * size, size), size)


def cols_of(n, width):
    return pl.ds(pl.multiple_of(n * width, 128), width)


def rotation(seg):
    counts = [jnp.sum(jnp.where(seg == u, 1.0, 0.0), 1, keepdims=True) for u in range(3)]
    start = counts[0] + counts[1] + counts[2]
    start = jnp.where(counts[2] == HALF, counts[0] + counts[1], start)
    start = jnp.where(counts[1] == HALF, counts[0], start)
    return jnp.where(counts[0] == HALF, 0.0, start)


def turn(t, start, back):
    row = (lax.broadcasted_iota(jnp.int32, (ROWS, TOK), 0) + t * ROWS).astype(f32)
    col = lax.broadcasted_iota(jnp.int32, (ROWS, TOK), 1).astype(f32)
    source = row - start if back else row + start
    source = jnp.where(source < 0.0, source + TOK, jnp.where(source >= TOK, source - TOK, source))
    return jnp.where(source == col, 1.0, 0.0).astype(bf16)


def column_of(row):
    return jnp.broadcast_to(row, (128, row.shape[1])).T


def attend_pair(q, k, v, bias, prob_ref):
    q = q * jnp.bfloat16(0.125)
    outs = []
    for h in range(2):
        qh = jnp.where(lane_half(h, q.shape), q, jnp.bfloat16(0))
        scores = dot(qh, k, NT) + bias
        scores = jnp.exp(scores - jnp.max(scores, 1, keepdims=True))
        probs = (scores * (1.0 / jnp.sum(scores, 1, keepdims=True))).astype(bf16)
        prob_ref[h] = probs
        outs.append(dot(probs, v, NN))
    return jnp.where(lane_half(0, outs[0].shape), outs[0], outs[1]).astype(bf16)


def attend_pair_back(q, k, v, grad, ctx, prob_ref):
    product = grad.astype(f32) * ctx.astype(f32)
    dq, dk, dv = [], [], []
    for h in range(2):
        lanes = lane_half(h, grad.shape)
        grad_h = jnp.where(lanes, grad, jnp.bfloat16(0))
        row_dot = jnp.sum(jnp.where(lanes, product, 0.0), 1, keepdims=True)
        probs = prob_ref[h]
        ds = (probs.astype(f32) * (dot(grad_h, v, NT) - row_dot)).astype(bf16)
        dq.append(dot(ds, k, NN))
        dk.append(dot(ds, q, TN))
        dv.append(dot(probs, grad, TN))
    lanes = lane_half(0, grad.shape)
    return [
        (jnp.where(lanes, dq[0], dq[1]) * 0.125).astype(bf16),
        (jnp.where(lanes, dk[0], dk[1]) * 0.125).astype(bf16),
        jnp.where(lanes, dv[0], dv[1]).astype(bf16),
    ]


def bias_row(small_ref, first, bias_len):
    total = jnp.zeros((8, 1024), f32)
    lanes = lax.broadcasted_iota(jnp.int32, (8, 256), 1)
    for d in range(first // bias_len, (first + D - 1) // bias_len + 1):
        piece = jnp.where(lanes < bias_len, jnp.broadcast_to(small_ref[8 * d : 8 * d + 1, :], (8, 256)), 0.0)
        piece = jnp.concatenate([piece, jnp.zeros((8, 768), f32)], axis=1)
        shift = (bias_len * d - first) % 1024
        total = total + (pltpu.roll(piece, shift, 1) if shift else piece)
    return total[:1, :D]


PAIRS = H // 2


def normed_of(residual):
    center = residual - jnp.mean(residual, 1, keepdims=True)
    scale = lax.rsqrt(jnp.mean(center * center, 1, keepdims=True) + EPSILON)
    return center * scale, scale


def norm_back(grad, gain, unit, scale):
    grad = grad * gain
    return scale * (grad - jnp.mean(grad, 1, keepdims=True) - unit * jnp.mean(grad * unit, 1, keepdims=True))


PAIRS = H // 2
THIRD = D // 3
PAIR = 2 * HD


def entry_cols(j, matrix, feat, pos, cot, entry, low, cot_out):
    cols = cols_of(j, 256)
    value = dot(matrix[...], feat[:, cols], NN) + dot(matrix[...], pos[:, cols], NN)
    entry[:, cols] = value
    low[:, cols] = value.astype(bf16)
    cot_out[:, cols] = dot(matrix[...], cot[:, cols], NN).astype(bf16)


def mask_half(h, matrix, stack, mask):
    matrix = matrix[h * HALF : (h + 1) * HALF, :]
    by_row = dot(stack, matrix, NT)
    by_col = dot(matrix, stack, NT)
    rows = lax.broadcasted_iota(jnp.int32, (HALF, HALF), 0)
    cols = lax.broadcasted_iota(jnp.int32, (HALF, HALF), 1)
    allowed = (by_col[:, 1:2] == by_row[1:2, :]) & ((by_row[0:1, :] > 0.0) | (rows == cols))
    mask[h] = jnp.where(allowed, 0.0, MASKED)


def stack_of(valid, seg):
    row = lax.broadcasted_iota(jnp.int32, (8, TOK), 0)
    both = jnp.where(row == 0, valid.astype(f32), jnp.where(row == 1, seg.astype(f32), 0.0))
    return both.astype(bf16)


def gain_row(small, which, gain_len):
    ranks = small.shape[0] // 8
    row = lax.broadcasted_iota(jnp.int32, (ranks, 8 * ranks), 0)
    col = lax.broadcasted_iota(jnp.int32, (ranks, 8 * ranks), 1)
    pick = jnp.where(col == 8 * row + which, 1.0, 0.0).astype(bf16)
    values = dot(pick, small[...].astype(bf16), NN).astype(bf16)
    lane = lax.broadcasted_iota(jnp.int32, (256, D), 1).astype(f32)
    home = jnp.floor((lane + 0.5) * (1.0 / gain_len))
    spot = lax.broadcasted_iota(jnp.int32, (256, D), 0).astype(f32)
    spread = dot(values, jnp.where(lane - home * gain_len == spot, 1.0, 0.0).astype(bf16), NN)
    owner = lax.broadcasted_iota(jnp.int32, (ranks, D), 0).astype(f32)
    return jnp.sum(jnp.where(home[:ranks] == owner, spread, 0.0), 0, keepdims=True)


SLOPE_COLS = 768
STRIPS = [[(which * D + g * THIRD, which * THIRD, THIRD) for which in range(3)] for g in range(3)]


def front_kernel(linked, bias_len, gain_len, *refs):
    n = 7
    if linked:
        (bias_in, gains_in, qkv_w, proj_w, expand_w, reduce_w), refs = refs[:6], refs[6:]
    else:
        (bias_in, gains_in, *weights_in), refs = refs[:8], refs[8:]
    (feat_in, pos_in, cot_in, seg_ref, valid_ref), refs = refs[:5], refs[5:]
    if linked:
        weights_out, refs = refs[:6], refs[6:]
    outs, refs = refs[:10], refs[10:]
    low_out, qkv_out, ctx_out, prob_out, unit_out, nlow_out, act_out, slope_out, gs_out, layer_out = outs
    (gains, dvec), refs = refs[:2], refs[2:]
    (feat, pos, cot_raw, entry, low, cot, mask, small, w_a, w_b, w_c, w_p, w_e, w_r, bias), refs = refs[:15], refs[15:]
    (qkv, ctx, probs, act, slope, total, unit_stage, ins, sent, psem, ssem, usem), refs = refs[:12], refs[12:]
    loads = [pltpu.make_async_copy(a, b, ins.at[i]) for i, (a, b) in enumerate(((feat_in, feat), (pos_in, pos), (cot_in, cot_raw)))]
    thirds = [w_a, w_b, w_c]
    homes = [*thirds, w_p, w_e, w_r]
    nlow, layer = feat, pos
    counted = iter(range(16))
    store = lambda a, b: pltpu.make_async_copy(a, b, sent.at[next(counted)])
    store_low, store_ctx, store_nlow = store(low, low_out), store(ctx, ctx_out), store(nlow, nlow_out)
    store_act, store_gs, store_layer = store(act, act_out), store(total, gs_out), store(layer, layer_out)
    store_qkv = [store(qkv.at[g], qkv_out.at[g]) for g in range(3)]
    store_w = [store(a, b) for a, b in zip(homes, weights_out)] if linked else []
    for copy in loads:
        copy.start()
    steps = Steps()
    ready = lambda i: None
    if linked:
        (shard, *refs) = refs
        place = Place()
        shard[...] = jnp.zeros_like(shard)
        shard[0:1, :bias_len] = bias_in[...].astype(bf16).astype(f32)
        shard[1:3, :gain_len] = gains_in[...].astype(bf16).astype(f32)
        place.greet()
        sources = [(qkv_w, w, STRIPS[g]) for g, w in enumerate(thirds)]
        sources += [(a, b, [(0, 0, b.shape[1])]) for a, b in ((proj_w, w_p), (expand_w, w_e), (reduce_w, w_r), (shard, small))]
        jobs = [Gather(place, *args, refs[i * GATHER_SCRATCH : (i + 1) * GATHER_SCRATCH]) for i, args in enumerate(sources)]
        for i in (0, 6, 1, 2, 3, 4, 5):
            jobs[i].load()
        tables = [job.timetable(*time) for job, time in zip(jobs, TIMES)]
        for table in tables:
            steps.add(table)

        def ready(i):
            if any(step is tables[i][-1][1] for _, step in steps.queue):
                steps.until(tables[i][-1][1])
            jobs[i].arrive_all()
            if i < 6:
                store_w[i].start()

    else:
        for i, (a, b) in enumerate(zip(weights_in, homes)):
            copy = pltpu.make_async_copy(a, b, sent.at[9 + i])
            copy.start()
            copy.wait()
    steps.clock = 0.5
    steps.run()
    for copy in loads:
        copy.wait()
    seg = seg_ref[...]
    start = rotation(seg)
    stack = stack_of(valid_ref[...], seg)
    matrix = act.at[:, :TOK]
    valid = column_of(valid_ref[...].astype(f32))[:, :1].astype(bf16)
    feat[...] = feat[...] * valid
    pos[...] = pos[...] * valid

    @pl.loop(0, 4)
    def _(t):
        matrix[tile(t, ROWS), :] = turn(t, start, False)

    steps.clock = 3.0
    steps.loop(3, 1.5, lambda j: entry_cols(j, matrix, feat, pos, cot_raw, entry, low, cot))
    store_low.start()
    for h in range(2):
        steps.run(0.8)
        mask_half(h, matrix, stack, mask)
    dvec[...] = jnp.zeros_like(dvec)
    ready(6)
    ready(0)
    if linked:
        for block in range(2):
            bias[0:1, block * D : (block + 1) * D] = bias_row(small, block * D, bias_len)
    else:
        bias[0:1, :] = bias_in[...]
        gains[0:2, :] = gains_in[...]
    steps.clock = 17.0

    def prob_store(it):
        return pltpu.make_async_copy(probs.at[it % 2], prob_out.at[pl.ds(2 * it, 2)], psem.at[it % 2])

    for g in range(3):
        if g:
            ready(g)

        for which in range(3):
            steps.run(0.9)
            cols = slice(which * THIRD, (which + 1) * THIRD)
            value = dot(low[...], thirds[g][:, cols], NN)
            if which != 1:
                first = (which // 2) * D + g * THIRD
                value = value + bias[0:1, first : first + THIRD]
            qkv[g, :, cols] = value.astype(bf16)
        store_qkv[g].start()

        def attention(i):
            it = 4 * g + i
            pair, half = i // 2, i % 2
            rows = tile(half, HALF)
            cut = lambda which: qkv[g, rows, cols_of(2 * which + pair, PAIR)]
            if g:
                prob_store(it - 2).wait()
            else:
                pl.when(it >= 2)(lambda: prob_store(it - 2).wait())
            ctx[rows, cols_of(2 * g + pair, PAIR)] = attend_pair(cut(0), cut(1), cut(2), mask[half], probs.at[it % 2])
            prob_store(it).start()

        steps.loop(4, 1.65, attention)
    store_ctx.start()
    if linked:
        for block in range(2, 10):
            bias[0:1, block * D : (block + 1) * D] = bias_row(small, block * D, bias_len)
        for which in range(2):
            gains[which : which + 1, :] = gain_row(small, 1 + which, gain_len)
    b_2 = bias[0:1, 3 * D + FF : 4 * D + FF]
    c_1, c_2 = bias[0:1, 4 * D + FF : 5 * D + FF], bias[0:1, 5 * D + FF : 6 * D + FF]
    g_1, g_2 = gains[0:1, :], gains[1:2, :]
    ready(3)

    def slope_store(j):
        return pltpu.make_async_copy(slope.at[j % 2], slope_out.at[:, cols_of(j, 256)], ssem.at[j % 2])

    def unit_store(t):
        return pltpu.make_async_copy(unit_stage.at[t % 2], unit_out.at[tile(t, ROWS)], usem.at[t % 2])

    def project(j):
        cols = cols_of(j, 256)
        entry[:, cols] = entry[:, cols] + dot(ctx[...], w_p[:, cols], NN) + bias[0:1, pl.ds(pl.multiple_of(2 * D + j * 256, 128), 256)]

    def first_norm(t):
        rows = tile(t, ROWS)
        unit, scale = normed_of(entry[rows, :])
        pl.when(t >= 2)(lambda: unit_store(t - 2).wait())
        unit_stage[t % 2, :, :D] = unit
        unit_stage[t % 2, :, D:] = jnp.broadcast_to(scale, (ROWS, 128))
        unit_store(t).start()
        normed = unit * g_1 + c_1
        nlow[rows, :] = normed.astype(bf16)
        total[rows, :] = normed + b_2

    def expand(j):
        cols = cols_of(j, 256)
        pre = dot(nlow[...], w_e[:, cols], NN) + bias[0:1, pl.ds(pl.multiple_of(3 * D + j * 256, 128), 256)]
        cdf = 0.5 + 0.5 * lax.erf(pre * 0.7071067811865476)
        act[:, cols] = (pre * cdf).astype(bf16)
        pl.when(j >= 2)(lambda: slope_store(j - 2).wait())
        slope[j % 2] = (cdf + pre * (0.3989422804014327 * jnp.exp(-0.5 * pre * pre))).astype(bf16)
        slope_store(j).start()

    steps.loop(3, 0.5, project)
    steps.loop(4, 0.5, first_norm)
    ready(4)
    steps.loop(12, 0.7, expand)
    store_nlow.start()
    store_act.start()
    for k in range(4):
        if linked:
            corner = tables[5][(4, 8, 10, 11)[k]][1]
            if any(step is corner for _, step in steps.queue):
                steps.until(corner)
            jobs[5].arrive(k)
            zz = place.order[k]
        else:
            zz = k

        def reduce(j):
            cols = cols_of(j, 256)
            total[:, cols] += dot(act[:, cols_of(zz, D)], w_r[cols_of(zz, D), cols], NN)

        pl.loop(0, 3)(reduce)

    @pl.loop(0, 4)
    def _(t):
        rows = tile(t, ROWS)
        unit, scale = normed_of(total[rows, :])
        layer[rows, :] = (unit * g_2 + c_2).astype(bf16)
        grad = cot[rows, :].astype(f32)
        dvec[0:1, :] += jnp.sum(grad * unit, 0, keepdims=True)
        dvec[1:2, :] += jnp.sum(grad, 0, keepdims=True)
        value = norm_back(grad, g_2, unit, scale)
        total[rows, :] = value
        dvec[2:3, :] += jnp.sum(value.astype(bf16).astype(f32), 0, keepdims=True)

    store_gs.start()
    store_layer.start()
    prob_store(10).wait()
    prob_store(11).wait()
    slope_store(10).wait()
    slope_store(11).wait()
    unit_store(2).wait()
    unit_store(3).wait()
    if linked:
        store_w[5].start()
        for job in jobs:
            job.drain()
    for copy in (store_low, store_ctx, store_nlow, store_act, store_gs, store_layer, *store_qkv, *store_w):
        copy.wait()


def front(linked, bias_len, gain_len, bias, gains, weights, features, pos_conv, cotangent, segments, valid):
    wide = [S((D, D), bf16)] * 4 + [S((D, FF), bf16), S((FF, D), bf16)]
    outs = list(wide) if linked else []
    outs += [
        S((TOK, D), bf16), S((3, TOK, D), bf16), S((TOK, D), bf16), S((2 * H, HALF, HALF), bf16), S((TOK, D + 128), f32),
        S((TOK, D), bf16), S((TOK, FF), bf16), S((TOK, FF), bf16), S((TOK, D), f32), S((TOK, D), bf16),
    ]
    hbm = len(outs)
    outs += [S((8, D), f32), S((8, D), f32)]
    half = pltpu.VMEM((TOK, D), bf16)
    scratch = [half, half, half, pltpu.VMEM((TOK, D), f32), half, half, pltpu.VMEM((2, HALF, HALF), f32), pltpu.VMEM((256, 256), f32)]
    scratch += [pltpu.VMEM(w.shape, bf16) for w in wide] + [pltpu.VMEM((1, 6 * D + FF), f32)]
    scratch += [
        pltpu.VMEM((3, TOK, D), bf16), half, pltpu.VMEM((2, 2, HALF, HALF), bf16), pltpu.VMEM((TOK, FF), bf16),
        pltpu.VMEM((2, TOK, 256), bf16), pltpu.VMEM((TOK, D), f32), pltpu.VMEM((2, ROWS, D + 128), f32),
        DMA((3,)), DMA((16,)), DMA((2,)), DMA((2,)), DMA((2,)),
    ]
    more = {}
    if linked:
        more = dict(collective_id=0, has_side_effects=True)
        scratch += [pltpu.VMEM((8, 256), f32)]
        for w in wide:
            scratch += Gather.scratch(w.shape[0] // 32, w.shape[1], bf16)
        scratch += Gather.scratch(8, 256, f32)
    return pl.pallas_call(
        functools.partial(front_kernel, linked, bias_len, gain_len),
        in_specs=[IN_VMEM] * 2 + [IN_HBM] * (len(weights) + 3) + [IN_VMEM] * 2,
        out_specs=[IN_HBM] * hbm + [IN_VMEM] * 2,
        out_shape=outs,
        scratch_shapes=scratch,
        compiler_params=params(**more),
        name="front",
    )(bias, gains, *weights, features, pos_conv, cotangent, segments, valid)


class Exchange:
    def __init__(self, place, total, slots, send, recv):
        z = place.z
        self.others = (place.partner, place.xn, place.yn, place.me + 8 - 16 * (z % 2), place.me + 16 - 32 * (z // 2))
        self.total, self.slots, self.send, self.recv = total, slots, send, recv

    def copy(self, n):
        return remote(self.slots.at[n], self.slots.at[5 + n], self.send.at[n], self.recv.at[n], self.others[n])

    def begin(self, n):
        self.slots[n] = self.total[...]
        self.copy(n).start()

    def end(self, n):
        self.copy(n).wait()
        self.total[...] += self.slots[5 + n]


VECTOR_ROWS = 72


def put(vector, row, value):
    for i in range(value.shape[1] // 128):
        vector[row + i : row + i + 1, :] = value[:, 128 * i : 128 * (i + 1)]


def back_kernel(linked, *refs):
    weights_in, refs = refs[:6], refs[6:]
    (low_in, qkv_in, ctx_in, prob_in, unit_in, nlow_in, act_in, slope_in, gs_in, layer_in), refs = refs[:10], refs[10:]
    (gains, dvec, seg_ref, valid_ref), refs = refs[:4], refs[4:]
    names = 6
    if linked:
        sums, refs = refs[:names], refs[names:]
    else:
        parts_out, refs = refs[:names], refs[names:]
    (input_out, layer_out, vector), refs = refs[:3], refs[3:]
    (big, w_e, w_r, hold_r, w_p, gs, grad, branch, ctx, low, probs, slope, unit, hold_p, hold_a, hold_b, hold_c, gain, db1), refs = refs[:19], refs[19:]
    (ins, psem, ssem, usem), refs = refs[:4], refs[4:]
    holds = [hold_a, hold_b, hold_c, hold_p, w_e, hold_r]
    counted = iter(range(24))
    copy = lambda a, b: pltpu.make_async_copy(a, b, ins.at[next(counted)])
    load_gs, load_act, load_wr, load_we = copy(gs_in, gs), copy(act_in, big), copy(weights_in[5], w_r), copy(weights_in[4], w_e)
    load_wp, load_nlow, load_ctx = copy(weights_in[3], w_p), copy(nlow_in, low), copy(ctx_in, ctx)
    load_low, load_layer = copy(low_in, low), copy(layer_in, branch)
    load_qkv = [copy(qkv_in.at[g], w_r.at[g * TOK : (g + 1) * TOK]) for g in range(3)]
    load_w = [copy(weights_in[g], hold_r.at[g * D : (g + 1) * D]) for g in range(3)]
    store_layer, store_input = copy(grad, layer_out), copy(ctx, input_out)
    load_gs.start()
    load_act.start()

    def slope_load(t, k):
        return pltpu.make_async_copy(slope_in.at[tile(t, ROWS), slice(k * SLOPE_COLS, (k + 1) * SLOPE_COLS)], slope.at[k % 2], ssem.at[k % 2])

    def unit_load(t):
        return pltpu.make_async_copy(unit_in.at[tile(t, ROWS)], unit.at[t % 2], usem.at[t % 2])

    def prob_load(it):
        return pltpu.make_async_copy(prob_in.at[pl.ds(2 * it, 2)], probs.at[it % 2], psem.at[it % 2])

    steps = Steps()
    sender = 0
    if linked:
        (slots, send, recv), refs = refs[:3], refs[3:]
        place = Place()
        sender = 1 - place.c
        jobs = [Scatter(place, holds[i], sums[i], refs[i * SCATTER_SCRATCH : (i + 1) * SCATTER_SCRATCH]) for i in range(names)]
        swap = Exchange(place, vector, slots, send, recv)
        place.greet(swap.others[4])
    else:
        jobs = [None] * names

    def exchange(i, unit):
        if linked:
            for k in (3, 2, 1, 0):
                jobs[i].exchange(k)
            steps.hold = jobs[i].timetable(0.0, unit)

    def computed(delay):
        if linked:
            steps.add([(time + steps.clock + delay, step) for time, step in steps.hold])

    load_gs.wait()

    @pl.loop(0, 4)
    def _(t):
        rows = tile(t, ROWS)
        grad[rows, :] = gs[rows, :].astype(bf16)

    load_act.wait()
    for load in (load_wr, load_we, load_wp, load_nlow, load_ctx):
        load.start()
    slope_load(0, 0).start()
    slope_load(0, 1).start()
    unit_load(0).start()
    prob_load(0).start()
    if linked:
        steps.clock = 4.0
        steps.add(jobs[5].timetable(5.5, 3.2))
    for k in (3, 2, 1, 0):
        zz = place.order[k] if linked else k
        steps.run(1.7)

        hold_r[tile(zz, D), :] = dot(big[:, cols_of(zz, D)], grad[...], TN).astype(bf16)

        if linked:
            jobs[5].exchange(k)
    for load in (load_wr, load_we, load_wp):
        load.wait()
    gain[...] = jnp.zeros_like(gain)
    db1[...] = jnp.zeros_like(db1)
    g_1 = gains[0:1, :]

    def ffn_back(t):
        rows = tile(t, ROWS)
        pl.when(t < 3)(lambda: unit_load(t + 1).start())
        gffn = grad[rows, :]
        total = gs[rows, :]
        for k in range(FF // SLOPE_COLS):
            cols = slice(k * SLOPE_COLS, (k + 1) * SLOPE_COLS)
            slope_load(t, k).wait()
            gpre = (dot(gffn, w_r[cols, :], NT) * slope[k % 2].astype(f32)).astype(bf16)
            if k < 2:
                slope_load(t, k + 2).start()
            else:
                pl.when(t < 3)(lambda: slope_load(t + 1, k - 2).start())
            big[rows, cols] = gpre
            db1[0:1, cols] += jnp.sum(gpre.astype(f32), 0, keepdims=True)
            total = total + dot(gpre, w_e[:, cols], NT)
        unit_load(t).wait()
        unit_1, scale_1 = unit[t % 2, :, :D], unit[t % 2, :, D : D + 1]
        gain[0:1, :] += jnp.sum(total * unit_1, 0, keepdims=True)
        gain[1:2, :] += jnp.sum(total, 0, keepdims=True)
        first = norm_back(total, g_1, unit_1, scale_1)
        gs[rows, :] = first
        lowered = first.astype(bf16)
        branch[rows, :] = lowered
        gain[2:3, :] += jnp.sum(lowered.astype(f32), 0, keepdims=True)
        grad[rows, :] = dot(lowered, w_p[...], NT).astype(bf16)

    steps.loop(4, 3.8, ffn_back)
    for load in load_qkv:
        load.start()
    load_nlow.wait()

    def expand_grad(j):
        cols = pl.ds(pl.multiple_of(((sender + j // 2) % 2) * (FF // 2) + (j % 2) * D, 256), D)
        w_e[:, cols] = dot(low[...], big[:, cols], TN).astype(bf16)

    steps.loop(2, 1.6, expand_grad)
    exchange(4, 3.2)
    steps.loop(2, 1.6, lambda j: expand_grad(j + 2))
    computed(DELAY_E)
    load_low.start()
    load_ctx.wait()

    def square_grad(hold, left, right, at):
        def half(j):
            first = ((sender + j) % 2) * (D // 2)
            cols = pl.ds(pl.multiple_of(first, 128), D // 2)
            source = pl.ds(pl.multiple_of(at + first, 128), D // 2)
            hold[:, cols] = dot(left[...], right[:, source], TN).astype(bf16)

        return half

    square = square_grad(hold_p, ctx, branch, 0)
    square(0)
    exchange(3, 0.8)
    square(1)
    steps.clock += 1.5
    computed(DELAY_P)
    load_layer.start()
    for load in load_qkv:
        load.wait()
    load_low.wait()
    for g in range(3):

        def attention(i):
            it = 4 * g + i
            pair, half = i // 2, i % 2
            rows = tile(half, HALF)
            cut = lambda which: w_r[pl.ds(pl.multiple_of(g * TOK + half * HALF, HALF), HALF), cols_of(2 * which + pair, PAIR)]
            if g < 2:
                prob_load(it + 1).start()
            else:
                pl.when(i < 3)(lambda: prob_load(it + 1).start())
            prob_load(it).wait()
            own = cols_of(2 * g + pair, PAIR)
            three = attend_pair_back(cut(0), cut(1), cut(2), grad[rows, own], ctx[rows, own], probs.at[it % 2])
            for which, value in enumerate(three):
                big[rows, cols_of(6 * g + 2 * which + pair, PAIR)] = value

        steps.loop(4, 1.7, attention)
        square = square_grad(holds[g], low, big, g * D)
        steps.run(0.7)
        square(0)
        exchange(g, 0.8)
        steps.run(0.7)
        square(1)
        computed(DELAY_T)
    start = rotation(seg_ref[...])
    load_layer.wait()

    def layer_back(t):
        rows = tile(t, ROWS)
        grad[rows, :] = dot(turn(t, start, True), branch[...], NN).astype(bf16)

    steps.loop(4, 0.6, layer_back)
    store_layer.start()
    for g in range(3):
        for which, row in ((0, 2 * g), (2, 6 + 2 * g)):
            at = g * D + which * THIRD
            put(vector, row, jnp.sum(big[:, at : at + THIRD].astype(f32), 0, keepdims=True))
    put(vector, 12, gain[2:3, :])
    put(vector, 18, db1[...])
    put(vector, 42, dvec[2:3, :])
    put(vector, 48, gain[1:2, :])
    put(vector, 54, dvec[1:2, :])
    put(vector, 60, gain[0:1, :])
    put(vector, 66, dvec[0:1, :])
    if linked:
        swap.begin(0)
        final = [step for _, step in steps.queue if step == jobs[5].total]
        if final:
            steps.until(final[0])
        jobs[5].finish()
    else:
        outs = [pltpu.make_async_copy(a, b, ins.at[18 + i]) for i, (a, b) in enumerate(zip(holds, parts_out))]
        for store in outs:
            store.start()
        for store in outs:
            store.wait()
    for load in load_w:
        load.start()
    for load in load_w:
        load.wait()

    def input_grad(t):
        rows = tile(t, ROWS)
        value = gs[rows, :]
        for g in range(3):
            value = value + dot(big[rows, g * D : (g + 1) * D], hold_r[g * D : (g + 1) * D, :], NT)
        big[rows, 3 * D : 4 * D] = value.astype(bf16)

    steps.loop(4, 1.3, input_grad)

    def input_back(t):
        rows = tile(t, ROWS)
        ctx[rows, :] = dot(turn(t, start, True), big[:, 3 * D : 4 * D], NN).astype(bf16)

    steps.loop(4, 0.6, input_back)
    ctx[...] = ctx[...] * column_of(valid_ref[...].astype(f32))[:, :1].astype(bf16)
    store_input.start()
    if linked:
        final = steps.queue
        steps.queue = []
        for n in range(5):
            swap_step = n
            for _, step in final[len(final) * n // 5 : len(final) * (n + 1) // 5]:
                step()
            swap.end(swap_step)
            if n < 4:
                swap.begin(n + 1)
        for job in jobs[:5]:
            job.finish()
    store_layer.wait()
    store_input.wait()


def back(linked, weights, *arrays):
    wide = [(D, D)] * 4 + [(D, FF), (FF, D)]
    outs = [S((r // 32, c), f32) for r, c in wide] if linked else [S(s, bf16) for s in wide]
    outs += [S((TOK, D), bf16), S((TOK, D), bf16), S((VECTOR_ROWS, 128), f32)]
    half = pltpu.VMEM((TOK, D), bf16)
    square = pltpu.VMEM((D, D), bf16)
    scratch = [
        pltpu.VMEM((TOK, FF), bf16), pltpu.VMEM((D, FF), bf16), pltpu.VMEM((FF, D), bf16), pltpu.VMEM((FF, D), bf16), square,
        pltpu.VMEM((TOK, D), f32), half, half, half, half, pltpu.VMEM((2, 2, HALF, HALF), bf16), pltpu.VMEM((2, ROWS, SLOPE_COLS), bf16),
        pltpu.VMEM((2, ROWS, D + 128), f32), square, square, square, square, pltpu.VMEM((8, D), f32), pltpu.VMEM((1, FF), f32),
        DMA((24,)), DMA((2,)), DMA((2,)), DMA((2,)),
    ]
    more = {}
    if linked:
        more = dict(collective_id=1, has_side_effects=True)
        scratch += [pltpu.VMEM((10, VECTOR_ROWS, 128), f32), DMA((5,)), DMA((5,))]
        for r, c in wide:
            scratch += Scatter.scratch(r // 32, c, bf16)
    return pl.pallas_call(
        functools.partial(back_kernel, linked),
        in_specs=[IN_HBM] * 16 + [IN_VMEM] * 4,
        out_specs=[IN_VMEM if linked else IN_HBM] * 6 + [IN_HBM] * 2 + [IN_VMEM],
        out_shape=outs,
        scratch_shapes=scratch,
        compiler_params=params(**more),
        name="back",
    )(*weights, *arrays)


def update_kernel(rates, *refs):
    thirds, refs = refs[:3], refs[3:]
    count = len(rates)
    ins, outs = refs[: 4 * count - 1], refs[4 * count - 1 :]
    for i, rate in enumerate(rates):
        if i:
            w_ref, g_ref, m_ref, a_ref = ins[4 * i - 1 : 4 * i + 3]
            pieces = [(slice(None), g_ref[...])]
        else:
            w_ref, m_ref, a_ref = ins[:3]
            pieces = []
            for g in range(3):
                for which in range(3):
                    at = which * D + g * THIRD
                    pieces.append((slice(at, at + THIRD), thirds[g][:, which * THIRD : (which + 1) * THIRD]))
        for cols, grad in pieces:
            velocity = 0.5 * m_ref[:, cols] + grad
            master = w_ref[:, cols] - rate * (grad + 0.5 * velocity)
            for ref, value in zip(outs[4 * i : 4 * i + 4], (grad, master, velocity, 0.5 * a_ref[:, cols] + 0.5 * master)):
                ref[:, cols] = value


def update(rates, thirds, arrays):
    shapes = [arrays[0].shape] * 4
    for a in arrays[3::4]:
        shapes += [a.shape] * 4
    return pl.pallas_call(
        functools.partial(update_kernel, rates),
        in_specs=[IN_VMEM] * (3 + len(arrays)),
        out_specs=[IN_VMEM] * len(shapes),
        out_shape=[S(s, f32) for s in shapes],
        compiler_params=params(),
        name="update",
    )(*thirds, *arrays)


def local(linked, *args):
    (
        features, pos_conv, segment_ids, frame_valid, cotangent,
        qkv_weight, proj_weight, expand_weight, reduce_weight, norm_gains, bias_vector,
        qkv_moment, proj_moment, expand_moment, reduce_moment, gains_moment, bias_moment,
        qkv_average, proj_average, expand_average, reduce_average, gains_average, bias_average,
    ) = args
    ranks = lax.axis_size("dp")
    me = lax.axis_index("dp")
    bias_len = bias_vector.shape[0]
    gain_len = norm_gains.shape[1]
    if linked:
        bias, gains = bias_vector[None], norm_gains
        weights = [qkv_weight, proj_weight, expand_weight, reduce_weight]
    else:
        round_to = lambda w: lax.reduce_precision(w, 8, 7)
        bias = lax.all_gather(round_to(bias_vector), "dp", axis=0, tiled=True)[None]
        gains = lax.all_gather(round_to(norm_gains), "dp", axis=1, tiled=True)
        qkv_full, *weights = [
            lax.all_gather(w.astype(bf16), "dp", axis=0, tiled=True) for w in (qkv_weight, proj_weight, expand_weight, reduce_weight)
        ]
        weights = [jnp.concatenate([qkv_full[:, a : a + w] for a, _, w in STRIPS[g]], axis=1) for g in range(3)] + weights
    outs = front(linked, bias_len, gain_len, bias, gains, weights, features, pos_conv, cotangent, segment_ids, frame_valid)
    if linked:
        weights, outs = outs[:6], outs[6:]
    *sums, grad_input, layer_out, vector = back(linked, weights, *outs, segment_ids, frame_valid)
    if not linked:
        sums = [lax.psum_scatter(p.astype(f32), "dp", scatter_dimension=0, tiled=True) for p in sums]
        vector = lax.psum(vector, "dp")
    *thirds, proj_grad, expand_grad, reduce_grad = sums
    vector = vector.reshape(-1)
    bias_grad = lax.dynamic_slice(vector, (me * bias_len,), (bias_len,))
    gains_grad = lax.dynamic_slice(vector[6 * D + FF :].reshape(2, D), (0, me * gain_len), (2, gain_len))
    root = math.sqrt(ranks * features.shape[0])
    matrix, proj, little = rate_matrix / root, rate_proj / root, rate_small / root
    updated = update(
        (matrix, proj, matrix, matrix),
        thirds,
        [
            qkv_weight, qkv_moment, qkv_average,
            proj_weight, proj_grad, proj_moment, proj_average,
            expand_weight, expand_grad, expand_moment, expand_average,
            reduce_weight, reduce_grad, reduce_moment, reduce_average,
        ],
    )

    def nesterov(master, gradient, moment, average):
        velocity = 0.5 * moment + gradient
        renewed = master - little * (gradient + 0.5 * velocity)
        return gradient, renewed, velocity, 0.5 * average + 0.5 * renewed

    gains_new = nesterov(norm_gains, gains_grad, gains_moment, gains_average)
    bias_new = nesterov(bias_vector, bias_grad, bias_moment, bias_average)
    results = [layer_out, grad_input]
    for i in range(4):
        results += [updated[i], updated[4 + i], updated[8 + i], updated[12 + i], gains_new[i], bias_new[i]]
    return tuple(results)


def solution(mesh):
    linked = mesh.shape["dp"] == 32
    rows, lanes, line = P("dp", None), P(None, "dp"), P("dp")
    six = (rows, rows, rows, rows, lanes, line)
    return jax.shard_map(
        functools.partial(local, linked),
        mesh=mesh,
        in_specs=(rows,) * 5 + six * 3,
        out_specs=(rows, rows) + six * 4,
        check_vma=False,
    )
```

```python
import functools
import math

import jax
import jax.numpy as jnp
from jax import lax
from jax.experimental import pallas as pl
from jax.experimental.pallas import tpu as pltpu
from jax.sharding import PartitionSpec as P

D = 768
H = 12
HD = 64
FF = 3072
TOK = 1024
HALF = 512
ROWS = 256
COLS = 768

EPSILON = 1e-05
MASKED = -1000000000.0
rate_matrix = 0.04
rate_proj = 0.5
rate_small = 0.2

f32 = jnp.float32
bf16 = jnp.bfloat16
NN = (((1,), (0,)), ((), ()))
NT = (((1,), (1,)), ((), ()))
TN = (((0,), (0,)), ((), ()))
MESH = pl.DeviceIdType.MESH
VMEM_LIMIT = 60 << 20
IN_VMEM = pl.BlockSpec(memory_space=pltpu.VMEM)
IN_HBM = pl.BlockSpec(memory_space=pl.ANY)
S = jax.ShapeDtypeStruct


def dot(a, b, dims):
    return lax.dot_general(a, b, dims, preferred_element_type=f32)


def lane_half(h, shape):
    return (lax.broadcasted_iota(jnp.int32, shape, 1) // HD) == h


def params(**more):
    return pltpu.CompilerParams(vmem_limit_bytes=VMEM_LIMIT, **more)


class Place:
    def __init__(self):
        me = lax.axis_index("dp")
        self.me = me
        self.c, self.x, self.y, self.z = me % 2, (me // 2) % 2, (me // 4) % 2, me // 8
        self.chip = me // 2
        self.partner = me + 1 - 2 * self.c
        self.xn = me + 2 - 4 * self.x
        self.yn = me + 4 - 8 * self.y
        self.up = me + 8
        self.down = me - 8
        z = self.z
        first = jnp.where(z == 0, 1, jnp.where(z == 1, 0, jnp.where(z == 2, 3, 2)))
        second = jnp.where(z == 0, 2, jnp.where(z == 1, 2, 1))
        third = jnp.where(z < 2, 3, 0)
        self.order = (z, first, second, third)

    def other(self, zz, dx=False, dy=False):
        x = 1 - self.x if dx else self.x
        y = 1 - self.y if dy else self.y
        return zz * 4 + y * 2 + x

    def greet(self):
        barrier = pltpu.get_barrier_semaphore()
        for other in (self.partner, self.xn, self.yn, *(zz * 8 + self.me % 8 for zz in self.order[1:])):
            pl.semaphore_signal(barrier, inc=1, device_id=(other,), device_id_type=MESH)
        pl.semaphore_wait(barrier, 6)


def remote(src, dst, send, recv, other):
    return pltpu.make_async_remote_copy(
        src_ref=src, dst_ref=dst, send_sem=send, recv_sem=recv, device_id=(other,), device_id_type=MESH
    )


def arrived(view, sem):
    pltpu.make_async_copy(view, view, sem).wait()


DMA = pltpu.SemaphoreType.DMA


class Gather:
    def __init__(self, place, shard, full, strips, direct, scratch):
        self.p = place
        self.shard = shard
        self.full = full
        self.strips = strips
        self.direct = direct
        self.rows = 2 * shard.shape[0]
        self.half = full.shape[1] // 2
        self.stage, self.own, self.ls, self.zs, self.zr, self.xs, self.xr, self.ys, self.yr, self.hs, self.hr, self.ps, self.pr = scratch

    @staticmethod
    def scratch(rows, cols, dtype):
        return [pltpu.VMEM((2 * rows, cols), f32), pltpu.VMEM((2 * rows, cols), dtype), DMA((10,)), DMA((5,))] + [DMA((4,))] * 9

    def cut(self, c):
        return pl.ds(pl.multiple_of(c * self.half, 128), self.half)

    def at(self, chip, count=1):
        start = pl.multiple_of(chip * self.rows, 16)
        return self.full.at[pl.ds(start, count * self.rows), self.cut(self.p.c)]

    def loads(self):
        p = self.p
        rows = pl.ds(pl.multiple_of(p.c * (self.rows // 2), 8), self.rows // 2)
        pairs = []
        for n, (src, dst, width) in enumerate(self.strips):
            part, mine = self.shard.at[:, src : src + width], self.stage.at[rows, dst : dst + width]
            pairs.append(
                (
                    pltpu.make_async_copy(part, mine, self.ls.at[3 * n]),
                    remote(part, mine, self.ls.at[3 * n + 1], self.ls.at[3 * n + 2], p.partner),
                )
            )
        return pairs

    def keep(self):
        return pltpu.make_async_copy(self.own.at[:, self.cut(self.p.c)], self.at(self.p.chip), self.ls.at[9])

    def along_z(self, k):
        p = self.p
        zz = p.order[k]
        view = self.at(p.other(zz))
        src = view if k else self.own.at[:, self.cut(p.c)]
        up = remote(src, view, self.zs.at[k], self.zr.at[zz], p.up)
        if k == 0:
            down = remote(src, view, self.zs.at[4], self.zr.at[zz], p.down)
            return (p.z < 3, up), (p.z > 0, down)
        down = remote(src, view, self.zs.at[k], self.zr.at[zz], p.down)
        return ((p.z < 3) & (zz < p.z), up), ((p.z > 0) & (zz > p.z), down)

    def straight(self, k):
        p = self.p
        view = self.at(p.chip)
        return remote(self.own.at[:, self.cut(p.c)], view, self.zs.at[k], self.zr.at[p.z], p.order[k] * 8 + p.me % 8)

    def across(self, k):
        p = self.p
        zz = p.order[k]
        view = self.at(p.other(zz))
        src = view if k else self.own.at[:, self.cut(p.c)]
        return (
            remote(src, view, self.xs.at[zz], self.xr.at[zz], p.xn),
            remote(src, view, self.ys.at[zz], self.yr.at[zz], p.yn),
        )

    def onward(self, k):
        p = self.p
        zz = p.order[k]
        even = k % 2 == 0
        view = self.at(p.other(zz, dx=even, dy=not even))
        return remote(view, view, self.hs.at[zz], self.hr.at[zz], p.yn if even else p.xn)

    def to_partner(self, k):
        zz = self.p.order[k]
        view = self.at(4 * zz, 4)
        return remote(view, view, self.ps.at[zz], self.pr.at[zz], self.p.partner)

    def load(self):
        for local, pair in self.loads():
            local.start()
            pair.start()

    def begin(self):
        for local, pair in self.loads():
            local.wait()
            pair.wait_recv()
        self.own[...] = self.stage[...].astype(self.own.dtype)
        if self.direct:
            for k in (3, 2, 1):
                self.straight(k).start()
        else:
            for cond, copy in self.along_z(0):
                pl.when(cond)(copy.start)
        for copy in self.across(0):
            copy.start()
        self.keep().start()

    def column(self, k):
        zz = self.p.order[k]
        arrived(self.at(self.p.other(zz)), self.zr.at[zz])
        if not self.direct:
            for cond, copy in self.along_z(k):
                pl.when(cond)(copy.start)
        for copy in self.across(k):
            copy.start()

    def plane(self, k):
        p = self.p
        zz = p.order[k]
        even = k % 2 == 0
        arrived(self.at(p.other(zz, dx=even, dy=not even)), (self.xr if even else self.yr).at[zz])
        self.onward(k).start()

    def corner(self, k):
        p = self.p
        zz = p.order[k]
        even = k % 2 == 0
        arrived(self.at(p.other(zz, dx=not even, dy=even)), (self.yr if even else self.xr).at[zz])
        arrived(self.at(p.other(zz, True, True)), self.hr.at[zz])
        if k == 0:
            self.keep().wait()
        self.to_partner(k).start()

    def arrive(self, k):
        p = self.p
        zz = p.order[k]
        start = pl.multiple_of(4 * zz * self.rows, 16)
        arrived(self.full.at[pl.ds(start, 4 * self.rows), self.cut(1 - p.c)], self.pr.at[zz])

    def arrive_all(self):
        for k in range(4):
            self.arrive(k)

    def drain(self):
        for local, pair in self.loads():
            pair.wait_send()
        for k in range(4):
            if not self.direct:
                for cond, copy in self.along_z(k):
                    pl.when(cond)(copy.wait_send)
            elif k:
                self.straight(k).wait_send()
            for copy in self.across(k):
                copy.wait_send()
            self.onward(k).wait_send()
            self.to_partner(k).wait_send()

    def step(self, n):
        z = self.p.z
        inner = (z == 1) | (z == 2)
        if n == 0:
            self.begin()
        elif n == 1 or (self.direct and n < 4):
            self.column(n)
        elif n == 2:
            pl.when(inner)(lambda: self.column(2))
        elif n == 3:
            pl.when(inner)(lambda: self.column(3))
            pl.when(~inner)(lambda: self.column(2))
        elif n == 12:
            if not self.direct:
                pl.when(~inner)(lambda: self.column(3))
        elif n < 8:
            self.plane(n - 4)
        else:
            self.corner(n - 8)


GATHER_SCRATCH = 13


class Scatter:
    def __init__(self, place, grad, out, scratch):
        self.p = place
        self.grad = grad
        self.out = out
        self.rows = 2 * out.shape[0]
        self.half = out.shape[1] // 2
        self.bp, self.bh, self.bx, self.by, self.bz, self.fin = scratch[:6]
        self.ps, self.pr, self.hs, self.hr, self.xs, self.xr, self.ys, self.yr, self.zs, self.zr, self.fs = scratch[6:]

    @staticmethod
    def scratch(rows, cols, dtype):
        rows, half = 2 * rows, cols // 2
        bufs = [pltpu.VMEM((n * rows, half), dtype) for n in (16, 4, 4, 4, 5)]
        return bufs + [pltpu.VMEM((rows, half), f32)] + [DMA((4,))] * 9 + [DMA((5,)), DMA((3,))]

    def cut(self, c):
        return pl.ds(pl.multiple_of(c * self.half, 128), self.half)

    def span(self, n, count=1):
        return pl.ds(pl.multiple_of(n * self.rows, 16), count * self.rows)

    def at(self, chip):
        return self.grad.at[self.span(chip), self.cut(self.p.c)]

    def slot(self, buf, n):
        return buf.at[self.span(n)]

    def add(self, view, *terms):
        total = view[...].astype(f32)
        for term in terms:
            total = total + term[...].astype(f32)
        view[...] = total.astype(view.dtype)

    def to_partner(self, zz):
        p = self.p
        src = self.grad.at[self.span(4 * zz, 4), self.cut(1 - p.c)]
        return remote(src, self.bp.at[self.span(4 * zz, 4)], self.ps.at[zz], self.pr.at[zz], p.partner)

    def corner(self, k):
        p = self.p
        zz = p.order[k]
        return remote(self.at(p.other(zz, True, True)), self.slot(self.bh, zz), self.hs.at[zz], self.hr.at[zz], p.xn if k % 2 else p.yn)

    def side(self, k, along_x):
        p = self.p
        zz = p.order[k]
        src = self.at(p.other(zz, dx=along_x, dy=not along_x))
        if along_x:
            return remote(src, self.slot(self.bx, zz), self.xs.at[zz], self.xr.at[zz], p.xn)
        return remote(src, self.slot(self.by, zz), self.ys.at[zz], self.yr.at[zz], p.yn)

    def chain(self, k):
        p = self.p
        zz = p.order[k]
        src = self.at(p.other(zz))
        up = remote(src, self.slot(self.bz, zz), self.zs.at[k], self.zr.at[zz], p.up)
        place = jnp.where(zz == p.z - 1, 4, zz)
        down = remote(src, self.slot(self.bz, place), self.zs.at[k], self.zr.at[place], p.down)
        return (zz > p.z, up), (zz < p.z, down)

    def last(self):
        p = self.p
        rows = self.rows // 2
        part = lambda c: self.fin.at[pl.ds(pl.multiple_of(c * rows, 8), rows)]
        dst = self.out.at[:, self.cut(p.c)]
        return pltpu.make_async_copy(part(p.c), dst, self.fs.at[0]), remote(part(1 - p.c), dst, self.fs.at[1], self.fs.at[2], p.partner)

    def exchange(self, k):
        self.to_partner(self.p.order[k]).start()

    def step(self, n):
        if n == 8:
            self.total()
        else:
            (self.pair, self.side_on, self.column, self.relay)[n // 4](n % 4)

    def pair(self, k):
        p = self.p
        zz = p.order[k]
        self.to_partner(zz).wait_recv()

        @pl.loop(0, 4)
        def _(j):
            chip = 4 * zz + j
            self.add(self.at(chip), self.slot(self.bp, chip))

        self.corner(k).start()
        self.side(k, along_x=k % 2 == 1).start()

    def side_on(self, k):
        p = self.p
        zz = p.order[k]
        even = k % 2 == 0
        self.corner(k).wait_recv()
        self.add(self.at(p.other(zz, dx=even, dy=not even)), self.slot(self.bh, zz))
        self.side(k, along_x=even).start()

    def gathered(self, k):
        zz = self.p.order[k]
        self.side(k, True).wait_recv()
        self.side(k, False).wait_recv()
        self.add(self.at(self.p.other(zz)), self.slot(self.bx, zz), self.slot(self.by, zz))

    def column(self, k):
        p = self.p
        zz = p.order[k]
        self.gathered(k)
        ends = (p.z == 0) | (p.z == 3)
        for cond, copy in self.chain(k):
            pl.when(cond & ends)(copy.start)

    def relay(self, k):
        p = self.p
        zz = p.order[k]

        @pl.when((p.z == 1) | (p.z == 2))
        def _():
            arrived(self.slot(self.bz, zz), self.zr.at[zz])
            self.add(self.at(p.other(zz)), self.slot(self.bz, zz))
            for cond, copy in self.chain(k):
                pl.when(cond)(copy.start)

    def total(self):
        p = self.p
        self.gathered(0)
        self.fin[...] = self.at(p.chip)[...].astype(f32)

        @pl.when(p.z > 0)
        def _():
            arrived(self.slot(self.bz, p.z), self.zr.at[p.z])
            self.fin[...] += self.slot(self.bz, p.z)[...].astype(f32)

        @pl.when(p.z < 3)
        def _():
            arrived(self.slot(self.bz, 4), self.zr.at[4])
            self.fin[...] += self.slot(self.bz, 4)[...].astype(f32)

        for copy in self.last():
            copy.start()

    def finish(self):
        p = self.p
        for k in range(4):
            self.to_partner(p.order[k]).wait_send()
            self.corner(k).wait_send()
            self.side(k, True).wait_send()
            self.side(k, False).wait_send()
            if k:
                for cond, copy in self.chain(k):
                    pl.when(cond)(copy.wait_send)
        local, pair = self.last()
        local.wait()
        pair.wait_send()
        arrived(self.out.at[:, self.cut(1 - p.c)], self.fs.at[2])


SCATTER_SCRATCH = 17


FRONT_PLAN = (
    (0,), (96, 16, 32), (4, 100, 2, 3, 12), (1, 97, 98, 99, 108, 20, 36), (6, 8, 104, 18, 19, 28, 34), (7, 102, 17),
    (5, 101, 103, 35, 33, 44), (22, 24, 40, 38, 10, 48, 11, 23, 9, 105, 107, 106), (), (21, 39, 49, 50, 51, 60, 52, 64, 37), (26, 27), (),
    (42,), (25, 43, 53), (54, 55), (56, 65, 66), (), (), (), (), (68,), (41, 57, 58), (59, 67, 80), (69,), (), (), (), (), (), (76, 70, 82),
    (72,), (81,), (), (84,), (), (), (71,), (), (83,), (), (73, 74, 92, 86, 85, 75), (88,), (), (), (87,), (), (), (89,), (), (90,), (), (),
    (91,), (), (), (), (),
)
BACK_PLAN = (
    (), (), (), (), (83, 82), (), (81,), (), (80,), (), (87, 86), (), (), (), (), (), (85, 84), (), (), (), (), (), (91, 90), (), (89, 67),
    (), (66, 95), (65, 64, 51), (94, 71, 50, 49, 48), (93, 70), (), (), (), (69, 3), (88, 68, 2, 1, 0), (55,), (53,), (), (), (75, 54, 19),
    (74, 52, 7, 18, 17, 16), (), (79,), (73, 6, 5), (), (58, 78, 4), (23, 35, 34), (59, 33, 32), (77, 57), (), (63, 62, 11, 10, 22, 21, 20),
    (39,), (61, 15, 14, 9, 27, 37), (72, 26, 38), (13, 31, 36), (56, 30, 25), (43, 42), (41,), (8, 29, 47, 46, 45, 24, 40),
)


class Steps:
    def __init__(self, plan, jobs):
        self.plan, self.jobs, self.next = plan, jobs, 0

    def take(self):
        if not self.jobs:
            return ()
        self.next += 1
        return self.plan[self.next - 1]

    def do(self, codes):
        for code in codes:
            self.jobs[code // 16].step(code % 16)

    def slot(self):
        self.do(self.take())

    def loop(self, count, body, inner=1):
        plan = [[self.take() for _ in range(inner)] for _ in range(count)]

        @pl.loop(0, count)
        def _(it):
            def at(sub):
                for n in range(count):
                    if plan[n][sub]:
                        pl.when(it == n)(functools.partial(self.do, plan[n][sub]))

            at(0)
            if inner > 1:
                body(it, at)
            else:
                body(it)


def tile(t, size):
    return pl.ds(pl.multiple_of(t * size, size), size)


def cols_of(n, width):
    return pl.ds(pl.multiple_of(n * width, 128), width)


def rotation(seg):
    counts = [jnp.sum(jnp.where(seg == u, 1.0, 0.0), 1, keepdims=True) for u in range(3)]
    start = counts[0] + counts[1] + counts[2]
    start = jnp.where(counts[2] == HALF, counts[0] + counts[1], start)
    start = jnp.where(counts[1] == HALF, counts[0], start)
    return jnp.where(counts[0] == HALF, 0.0, start)


def turn(t, start, back):
    row = (lax.broadcasted_iota(jnp.int32, (ROWS, TOK), 0) + t * ROWS).astype(f32)
    col = lax.broadcasted_iota(jnp.int32, (ROWS, TOK), 1).astype(f32)
    source = row - start if back else row + start
    source = jnp.where(source < 0.0, source + TOK, jnp.where(source >= TOK, source - TOK, source))
    return jnp.where(source == col, 1.0, 0.0).astype(bf16)


def column_of(row):
    return jnp.broadcast_to(row, (128, row.shape[1])).T


def attend_pair(q, k, v, bias, prob_ref):
    q = q * jnp.bfloat16(0.125)
    outs = []
    for h in range(2):
        qh = jnp.where(lane_half(h, q.shape), q, jnp.bfloat16(0))
        scores = dot(qh, k, NT) + bias
        scores = jnp.exp(scores - jnp.max(scores, 1, keepdims=True))
        probs = (scores * (1.0 / jnp.sum(scores, 1, keepdims=True))).astype(bf16)
        prob_ref[h] = probs
        outs.append(dot(probs, v, NN))
    return jnp.where(lane_half(0, outs[0].shape), outs[0], outs[1]).astype(bf16)


def attend_pair_back(q, k, v, grad, ctx, prob_ref):
    product = grad.astype(f32) * ctx.astype(f32)
    dq, dk, dv = [], [], []
    for h in range(2):
        lanes = lane_half(h, grad.shape)
        grad_h = jnp.where(lanes, grad, jnp.bfloat16(0))
        row_dot = jnp.sum(jnp.where(lanes, product, 0.0), 1, keepdims=True)
        probs = prob_ref[h]
        ds = (probs.astype(f32) * (dot(grad_h, v, NT) - row_dot)).astype(bf16)
        dq.append(dot(ds, k, NN))
        dk.append(dot(ds, q, TN))
        dv.append(dot(probs, grad, TN))
    lanes = lane_half(0, grad.shape)
    return [
        (jnp.where(lanes, dq[0], dq[1]) * 0.125).astype(bf16),
        (jnp.where(lanes, dk[0], dk[1]) * 0.125).astype(bf16),
        jnp.where(lanes, dv[0], dv[1]).astype(bf16),
    ]


def bias_row(small_ref, first, bias_len):
    total = jnp.zeros((8, 1024), f32)
    lanes = lax.broadcasted_iota(jnp.int32, (8, 256), 1)
    for d in range(first // bias_len, (first + D - 1) // bias_len + 1):
        piece = jnp.where(lanes < bias_len, jnp.broadcast_to(small_ref[8 * d : 8 * d + 1, :], (8, 256)), 0.0)
        piece = jnp.concatenate([piece, jnp.zeros((8, 768), f32)], axis=1)
        shift = (bias_len * d - first) % 1024
        total = total + (pltpu.roll(piece, shift, 1) if shift else piece)
    return total[:1, :D]


PAIRS = H // 2


def normed_of(residual):
    center = residual - jnp.mean(residual, 1, keepdims=True)
    scale = lax.rsqrt(jnp.mean(center * center, 1, keepdims=True) + EPSILON)
    return center * scale, scale


def norm_back(grad, gain, unit, scale):
    grad = grad * gain
    return scale * (grad - jnp.mean(grad, 1, keepdims=True) - unit * jnp.mean(grad * unit, 1, keepdims=True))


PAIRS = H // 2
THIRD = D // 3
PAIR = 2 * HD


def entry_cols(j, matrix, feat, pos, cot, entry, low, cot_out):
    cols = cols_of(j, 256)
    value = dot(matrix[...], feat[:, cols], NN) + dot(matrix[...], pos[:, cols], NN)
    entry[:, cols] = value
    low[:, cols] = value.astype(bf16)
    cot_out[:, cols] = dot(matrix[...], cot[:, cols], NN).astype(bf16)


def mask_half(h, matrix, stack, mask):
    matrix = matrix[h * HALF : (h + 1) * HALF, :]
    by_row = dot(stack, matrix, NT)
    by_col = dot(matrix, stack, NT)
    rows = lax.broadcasted_iota(jnp.int32, (HALF, HALF), 0)
    cols = lax.broadcasted_iota(jnp.int32, (HALF, HALF), 1)
    allowed = (by_col[:, 1:2] == by_row[1:2, :]) & ((by_row[0:1, :] > 0.0) | (rows == cols))
    mask[h] = jnp.where(allowed, 0.0, MASKED)


def stack_of(valid, seg):
    row = lax.broadcasted_iota(jnp.int32, (8, TOK), 0)
    both = jnp.where(row == 0, valid.astype(f32), jnp.where(row == 1, seg.astype(f32), 0.0))
    return both.astype(bf16)


def gain_row(small, which, gain_len):
    ranks = small.shape[0] // 8
    row = lax.broadcasted_iota(jnp.int32, (ranks, 8 * ranks), 0)
    col = lax.broadcasted_iota(jnp.int32, (ranks, 8 * ranks), 1)
    pick = jnp.where(col == 8 * row + which, 1.0, 0.0).astype(bf16)
    values = dot(pick, small[...].astype(bf16), NN).astype(bf16)
    lane = lax.broadcasted_iota(jnp.int32, (256, D), 1).astype(f32)
    home = jnp.floor((lane + 0.5) * (1.0 / gain_len))
    spot = lax.broadcasted_iota(jnp.int32, (256, D), 0).astype(f32)
    spread = dot(values, jnp.where(lane - home * gain_len == spot, 1.0, 0.0).astype(bf16), NN)
    owner = lax.broadcasted_iota(jnp.int32, (ranks, D), 0).astype(f32)
    return jnp.sum(jnp.where(home[:ranks] == owner, spread, 0.0), 0, keepdims=True)


SLOPE_COLS = 768
STRIPS = [[(which * D + g * THIRD, which * THIRD, THIRD) for which in range(3)] for g in range(3)]


def front_kernel(linked, bias_len, gain_len, *refs):
    n = 7
    if linked:
        (bias_in, gains_in, qkv_w, proj_w, expand_w, reduce_w), refs = refs[:6], refs[6:]
    else:
        (bias_in, gains_in, *weights_in), refs = refs[:8], refs[8:]
    (feat_in, pos_in, cot_in, seg_ref, valid_ref), refs = refs[:5], refs[5:]
    if linked:
        weights_out, refs = refs[:6], refs[6:]
    outs, refs = refs[:10], refs[10:]
    low_out, qkv_out, ctx_out, prob_out, unit_out, nlow_out, act_out, slope_out, gs_out, layer_out = outs
    (gains, dvec), refs = refs[:2], refs[2:]
    (feat, pos, cot_raw, entry, low, cot, mask, small, w_a, w_b, w_c, w_p, w_e, w_r, bias), refs = refs[:15], refs[15:]
    (qkv, ctx, probs, act, slope, total, unit_stage, ins, sent, psem, ssem, usem), refs = refs[:12], refs[12:]
    loads = [pltpu.make_async_copy(a, b, ins.at[i]) for i, (a, b) in enumerate(((feat_in, feat), (pos_in, pos), (cot_in, cot_raw)))]
    thirds = [w_a, w_b, w_c]
    homes = [*thirds, w_p, w_e, w_r]
    nlow, layer = feat, pos
    counted = iter(range(16))
    store = lambda a, b: pltpu.make_async_copy(a, b, sent.at[next(counted)])
    store_low, store_ctx, store_nlow = store(low, low_out), store(ctx, ctx_out), store(nlow, nlow_out)
    store_act, store_gs, store_layer = store(act, act_out), store(total, gs_out), store(layer, layer_out)
    store_qkv = [store(qkv.at[g], qkv_out.at[g]) for g in range(3)]
    store_w = [store(a, b) for a, b in zip(homes, weights_out)] if linked else []
    for copy in loads:
        copy.start()
    jobs = []
    if linked:
        (shard, *refs) = refs
        place = Place()
        shard[...] = jnp.zeros_like(shard)
        shard[0:1, :bias_len] = bias_in[...].astype(bf16).astype(f32)
        shard[1:3, :gain_len] = gains_in[...].astype(bf16).astype(f32)
        place.greet()
        sources = [(qkv_w, w, STRIPS[g], True) for g, w in enumerate(thirds)]
        sources += [(a, b, [(0, 0, b.shape[1])], b is w_p or b is small) for a, b in ((proj_w, w_p), (expand_w, w_e), (reduce_w, w_r), (shard, small))]
        jobs = [Gather(place, *args, refs[i * GATHER_SCRATCH : (i + 1) * GATHER_SCRATCH]) for i, args in enumerate(sources)]
        for i in (0, 6, 1, 2, 3, 4, 5):
            jobs[i].load()
    else:
        for i, (a, b) in enumerate(zip(weights_in, homes)):
            copy = pltpu.make_async_copy(a, b, sent.at[9 + i])
            copy.start()
            copy.wait()
    steps = Steps(FRONT_PLAN, jobs)

    def ready(i):
        steps.slot()
        if linked:
            jobs[i].arrive_all()
            if i < 6:
                store_w[i].start()

    steps.slot()
    for copy in loads:
        copy.wait()
    seg = seg_ref[...]
    start = rotation(seg)
    stack = stack_of(valid_ref[...], seg)
    matrix = act.at[:, :TOK]
    valid = column_of(valid_ref[...].astype(f32))[:, :1].astype(bf16)
    feat[...] = feat[...] * valid
    pos[...] = pos[...] * valid

    steps.slot()

    @pl.loop(0, 4)
    def _(t):
        matrix[tile(t, ROWS), :] = turn(t, start, False)

    steps.loop(3, lambda j: entry_cols(j, matrix, feat, pos, cot_raw, entry, low, cot))
    store_low.start()
    for h in range(2):
        steps.slot()
        mask_half(h, matrix, stack, mask)
    dvec[...] = jnp.zeros_like(dvec)
    ready(6)
    ready(0)
    if linked:
        for block in range(2):
            bias[0:1, block * D : (block + 1) * D] = bias_row(small, block * D, bias_len)
    else:
        bias[0:1, :] = bias_in[...]
        gains[0:2, :] = gains_in[...]

    def prob_store(it):
        return pltpu.make_async_copy(probs.at[it % 2], prob_out.at[pl.ds(2 * it, 2)], psem.at[it % 2])

    for g in range(3):
        if g:
            ready(g)

        for which in range(3):
            steps.slot()
            cols = slice(which * THIRD, (which + 1) * THIRD)
            value = dot(low[...], thirds[g][:, cols], NN)
            if which != 1:
                first = (which // 2) * D + g * THIRD
                value = value + bias[0:1, first : first + THIRD]
            qkv[g, :, cols] = value.astype(bf16)
        store_qkv[g].start()

        def attention(i):
            it = 4 * g + i
            pair, half = i // 2, i % 2
            rows = tile(half, HALF)
            cut = lambda which: qkv[g, rows, cols_of(2 * which + pair, PAIR)]
            if g:
                prob_store(it - 2).wait()
            else:
                pl.when(it >= 2)(lambda: prob_store(it - 2).wait())
            ctx[rows, cols_of(2 * g + pair, PAIR)] = attend_pair(cut(0), cut(1), cut(2), mask[half], probs.at[it % 2])
            prob_store(it).start()

        steps.loop(4, attention)
    store_ctx.start()
    if linked:
        for block in range(2, 10):
            bias[0:1, block * D : (block + 1) * D] = bias_row(small, block * D, bias_len)
        for which in range(2):
            gains[which : which + 1, :] = gain_row(small, 1 + which, gain_len)
    b_2 = bias[0:1, 3 * D + FF : 4 * D + FF]
    c_1, c_2 = bias[0:1, 4 * D + FF : 5 * D + FF], bias[0:1, 5 * D + FF : 6 * D + FF]
    g_1, g_2 = gains[0:1, :], gains[1:2, :]
    ready(3)

    def slope_store(j):
        return pltpu.make_async_copy(slope.at[j % 2], slope_out.at[:, cols_of(j, 256)], ssem.at[j % 2])

    def unit_store(t):
        return pltpu.make_async_copy(unit_stage.at[t % 2], unit_out.at[tile(t, ROWS)], usem.at[t % 2])

    def project(j):
        cols = cols_of(j, 256)
        entry[:, cols] = entry[:, cols] + dot(ctx[...], w_p[:, cols], NN) + bias[0:1, pl.ds(pl.multiple_of(2 * D + j * 256, 128), 256)]

    def first_norm(t):
        rows = tile(t, ROWS)
        unit, scale = normed_of(entry[rows, :])
        pl.when(t >= 2)(lambda: unit_store(t - 2).wait())
        unit_stage[t % 2, :, :D] = unit
        unit_stage[t % 2, :, D:] = jnp.broadcast_to(scale, (ROWS, 128))
        unit_store(t).start()
        normed = unit * g_1 + c_1
        nlow[rows, :] = normed.astype(bf16)
        total[rows, :] = normed + b_2

    def expand(j):
        cols = cols_of(j, 256)
        pre = dot(nlow[...], w_e[:, cols], NN) + bias[0:1, pl.ds(pl.multiple_of(3 * D + j * 256, 128), 256)]
        cdf = 0.5 + 0.5 * lax.erf(pre * 0.7071067811865476)
        act[:, cols] = (pre * cdf).astype(bf16)
        pl.when(j >= 2)(lambda: slope_store(j - 2).wait())
        slope[j % 2] = (cdf + pre * (0.3989422804014327 * jnp.exp(-0.5 * pre * pre))).astype(bf16)
        slope_store(j).start()

    steps.loop(3, project)
    steps.loop(4, first_norm)
    ready(4)
    steps.loop(12, expand)
    store_nlow.start()
    store_act.start()
    for k in range(4):
        if linked:
            steps.slot()
            jobs[5].arrive(k)
            zz = place.order[k]
        else:
            zz = k

        def reduce(j):
            cols = cols_of(j, 256)
            total[:, cols] += dot(act[:, cols_of(zz, D)], w_r[cols_of(zz, D), cols], NN)

        pl.loop(0, 3)(reduce)

    @pl.loop(0, 4)
    def _(t):
        rows = tile(t, ROWS)
        unit, scale = normed_of(total[rows, :])
        layer[rows, :] = (unit * g_2 + c_2).astype(bf16)
        grad = cot[rows, :].astype(f32)
        dvec[0:1, :] += jnp.sum(grad * unit, 0, keepdims=True)
        dvec[1:2, :] += jnp.sum(grad, 0, keepdims=True)
        value = norm_back(grad, g_2, unit, scale)
        total[rows, :] = value
        dvec[2:3, :] += jnp.sum(value.astype(bf16).astype(f32), 0, keepdims=True)

    store_gs.start()
    store_layer.start()
    prob_store(10).wait()
    prob_store(11).wait()
    slope_store(10).wait()
    slope_store(11).wait()
    unit_store(2).wait()
    unit_store(3).wait()
    if linked:
        store_w[5].start()
        for job in jobs:
            job.drain()
    for copy in (store_low, store_ctx, store_nlow, store_act, store_gs, store_layer, *store_qkv, *store_w):
        copy.wait()


def front(linked, bias_len, gain_len, bias, gains, weights, features, pos_conv, cotangent, segments, valid):
    wide = [S((D, D), bf16)] * 4 + [S((D, FF), bf16), S((FF, D), bf16)]
    outs = list(wide) if linked else []
    outs += [
        S((TOK, D), bf16), S((3, TOK, D), bf16), S((TOK, D), bf16), S((2 * H, HALF, HALF), bf16), S((TOK, D + 128), f32),
        S((TOK, D), bf16), S((TOK, FF), bf16), S((TOK, FF), bf16), S((TOK, D), f32), S((TOK, D), bf16),
    ]
    hbm = len(outs)
    outs += [S((8, D), f32), S((8, D), f32)]
    half = pltpu.VMEM((TOK, D), bf16)
    scratch = [half, half, half, pltpu.VMEM((TOK, D), f32), half, half, pltpu.VMEM((2, HALF, HALF), f32), pltpu.VMEM((256, 256), f32)]
    scratch += [pltpu.VMEM(w.shape, bf16) for w in wide] + [pltpu.VMEM((1, 6 * D + FF), f32)]
    scratch += [
        pltpu.VMEM((3, TOK, D), bf16), half, pltpu.VMEM((2, 2, HALF, HALF), bf16), pltpu.VMEM((TOK, FF), bf16),
        pltpu.VMEM((2, TOK, 256), bf16), pltpu.VMEM((TOK, D), f32), pltpu.VMEM((2, ROWS, D + 128), f32),
        DMA((3,)), DMA((16,)), DMA((2,)), DMA((2,)), DMA((2,)),
    ]
    more = {}
    if linked:
        more = dict(collective_id=0, has_side_effects=True)
        scratch += [pltpu.VMEM((8, 256), f32)]
        for w in wide:
            scratch += Gather.scratch(w.shape[0] // 32, w.shape[1], bf16)
        scratch += Gather.scratch(8, 256, f32)
    return pl.pallas_call(
        functools.partial(front_kernel, linked, bias_len, gain_len),
        in_specs=[IN_VMEM] * 2 + [IN_HBM] * (len(weights) + 3) + [IN_VMEM] * 2,
        out_specs=[IN_HBM] * hbm + [IN_VMEM] * 2,
        out_shape=outs,
        scratch_shapes=scratch,
        compiler_params=params(**more),
        name="front",
    )(bias, gains, *weights, features, pos_conv, cotangent, segments, valid)


class Exchange:
    def __init__(self, place, total, slots, send, recv):
        z = place.z
        self.others = (place.partner, place.xn, place.yn, place.me + 8 - 16 * (z % 2), place.me + 16 - 32 * (z // 2))
        self.total, self.slots, self.send, self.recv = total, slots, send, recv

    def copy(self, n):
        return remote(self.slots.at[n], self.slots.at[5 + n], self.send.at[n], self.recv.at[n], self.others[n])

    def begin(self, n):
        self.slots[n] = self.total[...]
        self.copy(n).start()

    def end(self, n):
        self.copy(n).wait()
        self.total[...] += self.slots[5 + n]


VECTOR_ROWS = 72


def put(vector, row, value):
    for i in range(value.shape[1] // 128):
        vector[row + i : row + i + 1, :] = value[:, 128 * i : 128 * (i + 1)]


def back_kernel(linked, *refs):
    weights_in, refs = refs[:6], refs[6:]
    (low_in, qkv_in, ctx_in, prob_in, unit_in, nlow_in, act_in, slope_in, gs_in, layer_in), refs = refs[:10], refs[10:]
    (gains, dvec, seg_ref, valid_ref), refs = refs[:4], refs[4:]
    names = 6
    if linked:
        sums, refs = refs[:names], refs[names:]
    else:
        parts_out, refs = refs[:names], refs[names:]
    (input_out, layer_out, vector), refs = refs[:3], refs[3:]
    (big, w_e, w_r, hold_r, w_p, gs, grad, branch, ctx, low, probs, slope, unit, hold_p, hold_a, hold_b, hold_c, gain, db1), refs = refs[:19], refs[19:]
    (ins, psem, ssem, usem), refs = refs[:4], refs[4:]
    holds = [hold_a, hold_b, hold_c, hold_p, w_e, hold_r]
    counted = iter(range(24))
    copy = lambda a, b: pltpu.make_async_copy(a, b, ins.at[next(counted)])
    load_gs, load_act, load_wr, load_we = copy(gs_in, gs), copy(act_in, big), copy(weights_in[5], w_r), copy(weights_in[4], w_e)
    load_wp, load_nlow, load_ctx = copy(weights_in[3], w_p), copy(nlow_in, low), copy(ctx_in, ctx)
    load_low, load_layer = copy(low_in, low), copy(layer_in, branch)
    load_qkv = [copy(qkv_in.at[g], w_r.at[g * TOK : (g + 1) * TOK]) for g in range(3)]
    load_w = [copy(weights_in[g], hold_r.at[g * D : (g + 1) * D]) for g in range(3)]
    store_layer, store_input = copy(grad, layer_out), copy(ctx, input_out)
    load_gs.start()
    load_act.start()

    def slope_load(t, k):
        return pltpu.make_async_copy(slope_in.at[tile(t, ROWS), slice(k * SLOPE_COLS, (k + 1) * SLOPE_COLS)], slope.at[k % 2], ssem.at[k % 2])

    def unit_load(t):
        return pltpu.make_async_copy(unit_in.at[tile(t, ROWS)], unit.at[t % 2], usem.at[t % 2])

    def prob_load(it):
        return pltpu.make_async_copy(prob_in.at[pl.ds(2 * it, 2)], probs.at[it % 2], psem.at[it % 2])

    jobs = []
    sender = 0
    if linked:
        (slots, send, recv), refs = refs[:3], refs[3:]
        place = Place()
        sender = 1 - place.c
        jobs = [Scatter(place, holds[i], sums[i], refs[i * SCATTER_SCRATCH : (i + 1) * SCATTER_SCRATCH]) for i in range(names)]
        swap = Exchange(place, vector, slots, send, recv)
        place.greet()
    steps = Steps(BACK_PLAN, jobs)

    def exchange(i):
        if linked:
            for k in (3, 2, 1, 0):
                jobs[i].exchange(k)

    load_gs.wait()

    @pl.loop(0, 4)
    def _(t):
        rows = tile(t, ROWS)
        grad[rows, :] = gs[rows, :].astype(bf16)

    load_act.wait()
    for load in (load_wr, load_we, load_wp, load_nlow, load_ctx):
        load.start()
    slope_load(0, 0).start()
    slope_load(0, 1).start()
    unit_load(0).start()
    prob_load(0).start()
    for k in (3, 2, 1, 0):
        zz = place.order[k] if linked else k
        steps.slot()

        hold_r[tile(zz, D), :] = dot(big[:, cols_of(zz, D)], grad[...], TN).astype(bf16)

        if linked:
            jobs[5].exchange(k)
    for load in (load_wr, load_we, load_wp):
        load.wait()
    gain[...] = jnp.zeros_like(gain)
    db1[...] = jnp.zeros_like(db1)
    g_1 = gains[0:1, :]

    def ffn_back(t, at):
        rows = tile(t, ROWS)
        pl.when(t < 3)(lambda: unit_load(t + 1).start())
        gffn = grad[rows, :]
        total = gs[rows, :]
        for k in range(FF // SLOPE_COLS):
            if k:
                at(k)
            cols = slice(k * SLOPE_COLS, (k + 1) * SLOPE_COLS)
            slope_load(t, k).wait()
            gpre = (dot(gffn, w_r[cols, :], NT) * slope[k % 2].astype(f32)).astype(bf16)
            if k < 2:
                slope_load(t, k + 2).start()
            else:
                pl.when(t < 3)(lambda: slope_load(t + 1, k - 2).start())
            big[rows, cols] = gpre
            db1[0:1, cols] += jnp.sum(gpre.astype(f32), 0, keepdims=True)
            total = total + dot(gpre, w_e[:, cols], NT)
        unit_load(t).wait()
        unit_1, scale_1 = unit[t % 2, :, :D], unit[t % 2, :, D : D + 1]
        gain[0:1, :] += jnp.sum(total * unit_1, 0, keepdims=True)
        gain[1:2, :] += jnp.sum(total, 0, keepdims=True)
        first = norm_back(total, g_1, unit_1, scale_1)
        gs[rows, :] = first
        lowered = first.astype(bf16)
        branch[rows, :] = lowered
        gain[2:3, :] += jnp.sum(lowered.astype(f32), 0, keepdims=True)
        grad[rows, :] = dot(lowered, w_p[...], NT).astype(bf16)

    steps.loop(4, ffn_back, 4)
    for load in load_qkv:
        load.start()
    load_nlow.wait()

    def expand_grad(j):
        cols = pl.ds(pl.multiple_of(((sender + j // 2) % 2) * (FF // 2) + (j % 2) * D, 256), D)
        w_e[:, cols] = dot(low[...], big[:, cols], TN).astype(bf16)

    steps.loop(2, expand_grad)
    exchange(4)
    steps.loop(2, lambda j: expand_grad(j + 2))
    load_low.start()
    load_ctx.wait()

    def square_grad(hold, left, right, at):
        def half(j):
            first = ((sender + j) % 2) * (D // 2)
            cols = pl.ds(pl.multiple_of(first, 128), D // 2)
            source = pl.ds(pl.multiple_of(at + first, 128), D // 2)
            hold[:, cols] = dot(left[...], right[:, source], TN).astype(bf16)

        return half

    square = square_grad(hold_p, ctx, branch, 0)
    steps.slot()
    square(0)
    exchange(3)
    steps.slot()
    square(1)
    load_layer.start()
    for load in load_qkv:
        load.wait()
    load_low.wait()
    for g in range(3):

        def attention(i):
            it = 4 * g + i
            pair, half = i // 2, i % 2
            rows = tile(half, HALF)
            cut = lambda which: w_r[pl.ds(pl.multiple_of(g * TOK + half * HALF, HALF), HALF), cols_of(2 * which + pair, PAIR)]
            if g < 2:
                prob_load(it + 1).start()
            else:
                pl.when(i < 3)(lambda: prob_load(it + 1).start())
            prob_load(it).wait()
            own = cols_of(2 * g + pair, PAIR)
            three = attend_pair_back(cut(0), cut(1), cut(2), grad[rows, own], ctx[rows, own], probs.at[it % 2])
            for which, value in enumerate(three):
                big[rows, cols_of(6 * g + 2 * which + pair, PAIR)] = value

        steps.loop(4, attention)
        square = square_grad(holds[g], low, big, g * D)
        steps.slot()
        square(0)
        exchange(g)
        steps.slot()
        square(1)
    start = rotation(seg_ref[...])
    load_layer.wait()

    def layer_back(t):
        rows = tile(t, ROWS)
        grad[rows, :] = dot(turn(t, start, True), branch[...], NN).astype(bf16)

    steps.loop(4, layer_back)
    store_layer.start()
    steps.slot()
    for g in range(3):
        for which, row in ((0, 2 * g), (2, 6 + 2 * g)):
            at = g * D + which * THIRD
            put(vector, row, jnp.sum(big[:, at : at + THIRD].astype(f32), 0, keepdims=True))
    put(vector, 12, gain[2:3, :])
    put(vector, 18, db1[...])
    put(vector, 42, dvec[2:3, :])
    put(vector, 48, gain[1:2, :])
    put(vector, 54, dvec[1:2, :])
    put(vector, 60, gain[0:1, :])
    put(vector, 66, dvec[0:1, :])
    if linked:
        swap.begin(0)
        steps.slot()
        jobs[5].finish()
    else:
        outs = [pltpu.make_async_copy(a, b, ins.at[18 + i]) for i, (a, b) in enumerate(zip(holds, parts_out))]
        for store in outs:
            store.start()
        for store in outs:
            store.wait()
    for load in load_w:
        load.start()
    for load in load_w:
        load.wait()

    def input_grad(t):
        rows = tile(t, ROWS)
        value = gs[rows, :]
        for g in range(3):
            value = value + dot(big[rows, g * D : (g + 1) * D], hold_r[g * D : (g + 1) * D, :], NT)
        big[rows, 3 * D : 4 * D] = value.astype(bf16)

    steps.loop(4, input_grad)

    def input_back(t):
        rows = tile(t, ROWS)
        ctx[rows, :] = dot(turn(t, start, True), big[:, 3 * D : 4 * D], NN).astype(bf16)

    steps.loop(4, input_back)
    ctx[...] = ctx[...] * column_of(valid_ref[...].astype(f32))[:, :1].astype(bf16)
    store_input.start()
    if linked:
        codes = steps.take()
        for n in range(5):
            steps.do(codes[len(codes) * n // 5 : len(codes) * (n + 1) // 5])
            swap.end(n)
            if n < 4:
                swap.begin(n + 1)
        for job in jobs[:5]:
            job.finish()
    store_layer.wait()
    store_input.wait()


def back(linked, weights, *arrays):
    wide = [(D, D)] * 4 + [(D, FF), (FF, D)]
    outs = [S((r // 32, c), f32) for r, c in wide] if linked else [S(s, bf16) for s in wide]
    outs += [S((TOK, D), bf16), S((TOK, D), bf16), S((VECTOR_ROWS, 128), f32)]
    half = pltpu.VMEM((TOK, D), bf16)
    square = pltpu.VMEM((D, D), bf16)
    scratch = [
        pltpu.VMEM((TOK, FF), bf16), pltpu.VMEM((D, FF), bf16), pltpu.VMEM((FF, D), bf16), pltpu.VMEM((FF, D), bf16), square,
        pltpu.VMEM((TOK, D), f32), half, half, half, half, pltpu.VMEM((2, 2, HALF, HALF), bf16), pltpu.VMEM((2, ROWS, SLOPE_COLS), bf16),
        pltpu.VMEM((2, ROWS, D + 128), f32), square, square, square, square, pltpu.VMEM((8, D), f32), pltpu.VMEM((1, FF), f32),
        DMA((24,)), DMA((2,)), DMA((2,)), DMA((2,)),
    ]
    more = {}
    if linked:
        more = dict(collective_id=1, has_side_effects=True)
        scratch += [pltpu.VMEM((10, VECTOR_ROWS, 128), f32), DMA((5,)), DMA((5,))]
        for r, c in wide:
            scratch += Scatter.scratch(r // 32, c, bf16)
    return pl.pallas_call(
        functools.partial(back_kernel, linked),
        in_specs=[IN_HBM] * 16 + [IN_VMEM] * 4,
        out_specs=[IN_VMEM if linked else IN_HBM] * 6 + [IN_HBM] * 2 + [IN_VMEM],
        out_shape=outs,
        scratch_shapes=scratch,
        compiler_params=params(**more),
        name="back",
    )(*weights, *arrays)


def update_kernel(rates, *refs):
    thirds, refs = refs[:3], refs[3:]
    count = len(rates)
    ins, outs = refs[: 4 * count - 1], refs[4 * count - 1 :]
    for i, rate in enumerate(rates):
        if i:
            w_ref, g_ref, m_ref, a_ref = ins[4 * i - 1 : 4 * i + 3]
            pieces = [(slice(None), g_ref[...])]
        else:
            w_ref, m_ref, a_ref = ins[:3]
            pieces = []
            for g in range(3):
                for which in range(3):
                    at = which * D + g * THIRD
                    pieces.append((slice(at, at + THIRD), thirds[g][:, which * THIRD : (which + 1) * THIRD]))
        for cols, grad in pieces:
            velocity = 0.5 * m_ref[:, cols] + grad
            master = w_ref[:, cols] - rate * (grad + 0.5 * velocity)
            for ref, value in zip(outs[4 * i : 4 * i + 4], (grad, master, velocity, 0.5 * a_ref[:, cols] + 0.5 * master)):
                ref[:, cols] = value


def update(rates, thirds, arrays):
    shapes = [arrays[0].shape] * 4
    for a in arrays[3::4]:
        shapes += [a.shape] * 4
    return pl.pallas_call(
        functools.partial(update_kernel, rates),
        in_specs=[IN_VMEM] * (3 + len(arrays)),
        out_specs=[IN_VMEM] * len(shapes),
        out_shape=[S(s, f32) for s in shapes],
        compiler_params=params(),
        name="update",
    )(*thirds, *arrays)


def local(linked, *args):
    (
        features, pos_conv, segment_ids, frame_valid, cotangent,
        qkv_weight, proj_weight, expand_weight, reduce_weight, norm_gains, bias_vector,
        qkv_moment, proj_moment, expand_moment, reduce_moment, gains_moment, bias_moment,
        qkv_average, proj_average, expand_average, reduce_average, gains_average, bias_average,
    ) = args
    ranks = lax.axis_size("dp")
    me = lax.axis_index("dp")
    bias_len = bias_vector.shape[0]
    gain_len = norm_gains.shape[1]
    if linked:
        bias, gains = bias_vector[None], norm_gains
        weights = [qkv_weight, proj_weight, expand_weight, reduce_weight]
    else:
        round_to = lambda w: lax.reduce_precision(w, 8, 7)
        bias = lax.all_gather(round_to(bias_vector), "dp", axis=0, tiled=True)[None]
        gains = lax.all_gather(round_to(norm_gains), "dp", axis=1, tiled=True)
        qkv_full, *weights = [
            lax.all_gather(w.astype(bf16), "dp", axis=0, tiled=True) for w in (qkv_weight, proj_weight, expand_weight, reduce_weight)
        ]
        weights = [jnp.concatenate([qkv_full[:, a : a + w] for a, _, w in STRIPS[g]], axis=1) for g in range(3)] + weights
    outs = front(linked, bias_len, gain_len, bias, gains, weights, features, pos_conv, cotangent, segment_ids, frame_valid)
    if linked:
        weights, outs = outs[:6], outs[6:]
    *sums, grad_input, layer_out, vector = back(linked, weights, *outs, segment_ids, frame_valid)
    if not linked:
        sums = [lax.psum_scatter(p.astype(f32), "dp", scatter_dimension=0, tiled=True) for p in sums]
        vector = lax.psum(vector, "dp")
    *thirds, proj_grad, expand_grad, reduce_grad = sums
    vector = vector.reshape(-1)
    bias_grad = lax.dynamic_slice(vector, (me * bias_len,), (bias_len,))
    gains_grad = lax.dynamic_slice(vector[6 * D + FF :].reshape(2, D), (0, me * gain_len), (2, gain_len))
    root = math.sqrt(ranks * features.shape[0])
    matrix, proj, little = rate_matrix / root, rate_proj / root, rate_small / root
    updated = update(
        (matrix, proj, matrix, matrix),
        thirds,
        [
            qkv_weight, qkv_moment, qkv_average,
            proj_weight, proj_grad, proj_moment, proj_average,
            expand_weight, expand_grad, expand_moment, expand_average,
            reduce_weight, reduce_grad, reduce_moment, reduce_average,
        ],
    )

    def nesterov(master, gradient, moment, average):
        velocity = 0.5 * moment + gradient
        renewed = master - little * (gradient + 0.5 * velocity)
        return gradient, renewed, velocity, 0.5 * average + 0.5 * renewed

    gains_new = nesterov(norm_gains, gains_grad, gains_moment, gains_average)
    bias_new = nesterov(bias_vector, bias_grad, bias_moment, bias_average)
    results = [layer_out, grad_input]
    for i in range(4):
        results += [updated[i], updated[4 + i], updated[8 + i], updated[12 + i], gains_new[i], bias_new[i]]
    return tuple(results)


def solution(mesh):
    linked = mesh.shape["dp"] == 32
    rows, lanes, line = P("dp", None), P(None, "dp"), P("dp")
    six = (rows, rows, rows, rows, lanes, line)
    return jax.shard_map(
        functools.partial(local, linked),
        mesh=mesh,
        in_specs=(rows,) * 5 + six * 3,
        out_specs=(rows, rows) + six * 4,
        check_vma=False,
    )
```

```python
import functools
import math

import jax
import jax.numpy as jnp
from jax import lax
from jax.experimental import pallas as pl
from jax.experimental.pallas import tpu as pltpu
from jax.sharding import PartitionSpec as P

D = 768
H = 12
HD = 64
FF = 3072
TOK = 1024
HALF = 512
ROWS = 256
COLS = 768

EPSILON = 1e-05
MASKED = -1000000000.0
rate_matrix = 0.04
rate_proj = 0.5
rate_small = 0.2

f32 = jnp.float32
bf16 = jnp.bfloat16
NN = (((1,), (0,)), ((), ()))
NT = (((1,), (1,)), ((), ()))
TN = (((0,), (0,)), ((), ()))
MESH = pl.DeviceIdType.MESH
VMEM_LIMIT = 60 << 20
IN_VMEM = pl.BlockSpec(memory_space=pltpu.VMEM)
IN_HBM = pl.BlockSpec(memory_space=pl.ANY)
S = jax.ShapeDtypeStruct


def dot(a, b, dims):
    return lax.dot_general(a, b, dims, preferred_element_type=f32)


def lane_half(h, shape):
    return (lax.broadcasted_iota(jnp.int32, shape, 1) // HD) == h


def params(**more):
    return pltpu.CompilerParams(vmem_limit_bytes=VMEM_LIMIT, **more)


class Place:
    def __init__(self):
        me = lax.axis_index("dp")
        self.me = me
        self.c, self.x, self.y, self.z = me % 2, (me // 2) % 2, (me // 4) % 2, me // 8
        self.chip = me // 2
        self.partner = me + 1 - 2 * self.c
        self.xn = me + 2 - 4 * self.x
        self.yn = me + 4 - 8 * self.y
        self.up = me + 8
        self.down = me - 8
        z = self.z
        first = jnp.where(z == 0, 1, jnp.where(z == 1, 0, jnp.where(z == 2, 3, 2)))
        second = jnp.where(z == 0, 2, jnp.where(z == 1, 2, 1))
        third = jnp.where(z < 2, 3, 0)
        self.order = (z, first, second, third)

    def other(self, zz, dx=False, dy=False):
        x = 1 - self.x if dx else self.x
        y = 1 - self.y if dy else self.y
        return zz * 4 + y * 2 + x

    def greet(self):
        barrier = pltpu.get_barrier_semaphore()
        for other in (self.partner, self.xn, self.yn, *(zz * 8 + self.me % 8 for zz in self.order[1:])):
            pl.semaphore_signal(barrier, inc=1, device_id=(other,), device_id_type=MESH)
        pl.semaphore_wait(barrier, 6)


def remote(src, dst, send, recv, other):
    return pltpu.make_async_remote_copy(
        src_ref=src, dst_ref=dst, send_sem=send, recv_sem=recv, device_id=(other,), device_id_type=MESH
    )


def arrived(view, sem):
    pltpu.make_async_copy(view, view, sem).wait()


DMA = pltpu.SemaphoreType.DMA


class Gather:
    def __init__(self, place, shard, full, strips, direct, scratch):
        self.p = place
        self.shard = shard
        self.full = full
        self.strips = strips
        self.direct = direct
        self.rows = 2 * shard.shape[0]
        self.half = full.shape[1] // 2
        self.stage, self.own, self.ls, self.zs, self.zr, self.xs, self.xr, self.ys, self.yr, self.hs, self.hr, self.ps, self.pr = scratch

    @staticmethod
    def scratch(rows, cols, dtype):
        return [pltpu.VMEM((2 * rows, cols), f32), pltpu.VMEM((2 * rows, cols), dtype), DMA((10,)), DMA((5,))] + [DMA((4,))] * 9

    def cut(self, c):
        return pl.ds(pl.multiple_of(c * self.half, 128), self.half)

    def at(self, chip, count=1):
        start = pl.multiple_of(chip * self.rows, 16)
        return self.full.at[pl.ds(start, count * self.rows), self.cut(self.p.c)]

    def loads(self):
        p = self.p
        rows = pl.ds(pl.multiple_of(p.c * (self.rows // 2), 8), self.rows // 2)
        pairs = []
        for n, (src, dst, width) in enumerate(self.strips):
            part, mine = self.shard.at[:, src : src + width], self.stage.at[rows, dst : dst + width]
            pairs.append(
                (
                    pltpu.make_async_copy(part, mine, self.ls.at[3 * n]),
                    remote(part, mine, self.ls.at[3 * n + 1], self.ls.at[3 * n + 2], p.partner),
                )
            )
        return pairs

    def keep(self):
        return pltpu.make_async_copy(self.own.at[:, self.cut(self.p.c)], self.at(self.p.chip), self.ls.at[9])

    def along_z(self, k):
        p = self.p
        zz = p.order[k]
        view = self.at(p.other(zz))
        src = view if k else self.own.at[:, self.cut(p.c)]
        up = remote(src, view, self.zs.at[k], self.zr.at[zz], p.up)
        if k == 0:
            down = remote(src, view, self.zs.at[4], self.zr.at[zz], p.down)
            return (p.z < 3, up), (p.z > 0, down)
        down = remote(src, view, self.zs.at[k], self.zr.at[zz], p.down)
        return ((p.z < 3) & (zz < p.z), up), ((p.z > 0) & (zz > p.z), down)

    def straight(self, k):
        p = self.p
        view = self.at(p.chip)
        return remote(self.own.at[:, self.cut(p.c)], view, self.zs.at[k], self.zr.at[p.z], p.order[k] * 8 + p.me % 8)

    def across(self, k):
        p = self.p
        zz = p.order[k]
        view = self.at(p.other(zz))
        src = view if k else self.own.at[:, self.cut(p.c)]
        return (
            remote(src, view, self.xs.at[zz], self.xr.at[zz], p.xn),
            remote(src, view, self.ys.at[zz], self.yr.at[zz], p.yn),
        )

    def onward(self, k):
        p = self.p
        zz = p.order[k]
        even = k % 2 == 0
        view = self.at(p.other(zz, dx=even, dy=not even))
        return remote(view, view, self.hs.at[zz], self.hr.at[zz], p.yn if even else p.xn)

    def to_partner(self, k):
        zz = self.p.order[k]
        view = self.at(4 * zz, 4)
        return remote(view, view, self.ps.at[zz], self.pr.at[zz], self.p.partner)

    def load(self):
        for local, pair in self.loads():
            local.start()
            pair.start()

    def begin(self):
        for local, pair in self.loads():
            local.wait()
            pair.wait_recv()
        self.own[...] = self.stage[...].astype(self.own.dtype)
        if self.direct:
            for k in (3, 2, 1):
                self.straight(k).start()
        else:
            for cond, copy in self.along_z(0):
                pl.when(cond)(copy.start)
        for copy in self.across(0):
            copy.start()
        self.keep().start()

    def column(self, k):
        zz = self.p.order[k]
        arrived(self.at(self.p.other(zz)), self.zr.at[zz])
        if not self.direct:
            for cond, copy in self.along_z(k):
                pl.when(cond)(copy.start)
        for copy in self.across(k):
            copy.start()

    def plane(self, k):
        p = self.p
        zz = p.order[k]
        even = k % 2 == 0
        arrived(self.at(p.other(zz, dx=even, dy=not even)), (self.xr if even else self.yr).at[zz])
        self.onward(k).start()

    def corner(self, k):
        p = self.p
        zz = p.order[k]
        even = k % 2 == 0
        arrived(self.at(p.other(zz, dx=not even, dy=even)), (self.yr if even else self.xr).at[zz])
        arrived(self.at(p.other(zz, True, True)), self.hr.at[zz])
        if k == 0:
            self.keep().wait()
        self.to_partner(k).start()

    def arrive(self, k):
        p = self.p
        zz = p.order[k]
        start = pl.multiple_of(4 * zz * self.rows, 16)
        arrived(self.full.at[pl.ds(start, 4 * self.rows), self.cut(1 - p.c)], self.pr.at[zz])

    def arrive_all(self):
        for k in range(4):
            self.arrive(k)

    def drain(self):
        for local, pair in self.loads():
            pair.wait_send()
        for k in range(4):
            if not self.direct:
                for cond, copy in self.along_z(k):
                    pl.when(cond)(copy.wait_send)
            elif k:
                self.straight(k).wait_send()
            for copy in self.across(k):
                copy.wait_send()
            self.onward(k).wait_send()
            self.to_partner(k).wait_send()

    def step(self, n):
        z = self.p.z
        inner = (z == 1) | (z == 2)
        if n == 0:
            self.begin()
        elif n == 1 or (self.direct and n < 4):
            self.column(n)
        elif n == 2:
            pl.when(inner)(lambda: self.column(2))
        elif n == 3:
            pl.when(inner)(lambda: self.column(3))
            pl.when(~inner)(lambda: self.column(2))
        elif n == 12:
            if not self.direct:
                pl.when(~inner)(lambda: self.column(3))
        elif n < 8:
            self.plane(n - 4)
        else:
            self.corner(n - 8)


GATHER_SCRATCH = 13


class Scatter:
    def __init__(self, place, grad, out, scratch):
        self.p = place
        self.grad = grad
        self.out = out
        self.rows = 2 * out.shape[0]
        self.half = out.shape[1] // 2
        self.bp, self.bh, self.bx, self.by, self.bz, self.fin = scratch[:6]
        self.ps, self.pr, self.hs, self.hr, self.xs, self.xr, self.ys, self.yr, self.zs, self.zr, self.fs = scratch[6:]

    @staticmethod
    def scratch(rows, cols, dtype):
        rows, half = 2 * rows, cols // 2
        bufs = [pltpu.VMEM((n * rows, half), dtype) for n in (16, 4, 4, 4, 5)]
        return bufs + [pltpu.VMEM((rows, half), f32)] + [DMA((4,))] * 9 + [DMA((5,)), DMA((3,))]

    def cut(self, c):
        return pl.ds(pl.multiple_of(c * self.half, 128), self.half)

    def span(self, n, count=1):
        return pl.ds(pl.multiple_of(n * self.rows, 16), count * self.rows)

    def at(self, chip):
        return self.grad.at[self.span(chip), self.cut(self.p.c)]

    def slot(self, buf, n):
        return buf.at[self.span(n)]

    def add(self, view, *terms):
        total = view[...]
        for term in terms:
            total = total + term[...]
        view[...] = total

    def to_partner(self, zz):
        p = self.p
        src = self.grad.at[self.span(4 * zz, 4), self.cut(1 - p.c)]
        return remote(src, self.bp.at[self.span(4 * zz, 4)], self.ps.at[zz], self.pr.at[zz], p.partner)

    def corner(self, k):
        p = self.p
        zz = p.order[k]
        return remote(self.at(p.other(zz, True, True)), self.slot(self.bh, zz), self.hs.at[zz], self.hr.at[zz], p.xn if k % 2 else p.yn)

    def side(self, k, along_x):
        p = self.p
        zz = p.order[k]
        src = self.at(p.other(zz, dx=along_x, dy=not along_x))
        if along_x:
            return remote(src, self.slot(self.bx, zz), self.xs.at[zz], self.xr.at[zz], p.xn)
        return remote(src, self.slot(self.by, zz), self.ys.at[zz], self.yr.at[zz], p.yn)

    def chain(self, k):
        p = self.p
        zz = p.order[k]
        src = self.at(p.other(zz))
        up = remote(src, self.slot(self.bz, zz), self.zs.at[k], self.zr.at[zz], p.up)
        place = jnp.where(zz == p.z - 1, 4, zz)
        down = remote(src, self.slot(self.bz, place), self.zs.at[k], self.zr.at[place], p.down)
        return (zz > p.z, up), (zz < p.z, down)

    def last(self):
        p = self.p
        rows = self.rows // 2
        part = lambda c: self.fin.at[pl.ds(pl.multiple_of(c * rows, 8), rows)]
        dst = self.out.at[:, self.cut(p.c)]
        return pltpu.make_async_copy(part(p.c), dst, self.fs.at[0]), remote(part(1 - p.c), dst, self.fs.at[1], self.fs.at[2], p.partner)

    def exchange(self, k):
        self.to_partner(self.p.order[k]).start()

    def step(self, n):
        if n == 8:
            self.total()
        else:
            (self.pair, self.side_on, self.column, self.relay)[n // 4](n % 4)

    def pair(self, k):
        p = self.p
        zz = p.order[k]
        self.to_partner(zz).wait_recv()

        @pl.loop(0, 4)
        def _(j):
            chip = 4 * zz + j
            self.add(self.at(chip), self.slot(self.bp, chip))

        self.corner(k).start()
        self.side(k, along_x=k % 2 == 1).start()

    def side_on(self, k):
        p = self.p
        zz = p.order[k]
        even = k % 2 == 0
        self.corner(k).wait_recv()
        self.add(self.at(p.other(zz, dx=even, dy=not even)), self.slot(self.bh, zz))
        self.side(k, along_x=even).start()

    def gathered(self, k):
        zz = self.p.order[k]
        self.side(k, True).wait_recv()
        self.side(k, False).wait_recv()
        self.add(self.at(self.p.other(zz)), self.slot(self.bx, zz), self.slot(self.by, zz))

    def column(self, k):
        p = self.p
        zz = p.order[k]
        self.gathered(k)
        ends = (p.z == 0) | (p.z == 3)
        for cond, copy in self.chain(k):
            pl.when(cond & ends)(copy.start)

    def relay(self, k):
        p = self.p
        zz = p.order[k]

        @pl.when((p.z == 1) | (p.z == 2))
        def _():
            arrived(self.slot(self.bz, zz), self.zr.at[zz])
            self.add(self.at(p.other(zz)), self.slot(self.bz, zz))
            for cond, copy in self.chain(k):
                pl.when(cond)(copy.start)

    def total(self):
        p = self.p
        self.gathered(0)
        self.fin[...] = self.at(p.chip)[...].astype(f32)

        @pl.when(p.z > 0)
        def _():
            arrived(self.slot(self.bz, p.z), self.zr.at[p.z])
            self.fin[...] += self.slot(self.bz, p.z)[...].astype(f32)

        @pl.when(p.z < 3)
        def _():
            arrived(self.slot(self.bz, 4), self.zr.at[4])
            self.fin[...] += self.slot(self.bz, 4)[...].astype(f32)

        for copy in self.last():
            copy.start()

    def finish(self):
        p = self.p
        for k in range(4):
            self.to_partner(p.order[k]).wait_send()
            self.corner(k).wait_send()
            self.side(k, True).wait_send()
            self.side(k, False).wait_send()
            if k:
                for cond, copy in self.chain(k):
                    pl.when(cond)(copy.wait_send)
        local, pair = self.last()
        local.wait()
        pair.wait_send()
        arrived(self.out.at[:, self.cut(1 - p.c)], self.fs.at[2])


SCATTER_SCRATCH = 17


FRONT_PLAN = (
    (0,), (96, 48, 16, 64), (2, 3, 12, 4, 98, 100), (1, 97, 99, 108, 20, 50, 52), (18, 49, 51, 60), (19, 28, 32, 6, 68), (7, 102, 17, 66),
    (8, 104, 5, 54, 101, 103, 65, 34, 22, 24, 35, 44, 33, 56, 36, 53, 11, 55, 67, 23, 10, 9, 105, 107, 72, 76, 106), (), (21, 38), (), (),
    (58,), (57, 80, 59, 70), (69,), (), (26, 25, 27), (37, 39, 40, 81, 82), (), (84,), (71,), (42,), (73,), (41, 43, 83), (), (), (74,), (),
    (), (92,), (85,), (), (), (75, 86), (), (), (88,), (), (), (), (), (), (87, 89), (), (), (90,), (91,), (), (), (), (),
)
BACK_PLAN = (
    (), (), (), (83,), (82,), (), (81,), (), (87, 80), (86,), (), (), (), (), (85,), (), (91,), (), (), (84,), (90,), (95,), (), (89, 94),
    (93, 67), (66,), (), (65, 64, 51, 50, 49), (88, 71, 70, 48), (), (), (), (69,), (68, 3, 2, 1), (55, 0), (54, 53), (), (), (75,),
    (74, 52, 19, 18, 17), (16,), (79, 73, 7, 6, 5), (59, 58, 4), (78,), (57, 23), (22, 21), (77, 35, 34), (63, 10, 20, 62, 33, 32), (11,),
    (), (61, 15, 14, 9, 27, 26, 25, 39, 38), (72, 37, 36), (13, 31, 30, 43, 56, 42), (47, 41), (29, 46), (), (8, 45), (), (24, 40),
)


class Steps:
    def __init__(self, plan, jobs):
        self.plan, self.jobs, self.next = plan, jobs, 0

    def take(self):
        if not self.jobs:
            return ()
        self.next += 1
        return self.plan[self.next - 1]

    def do(self, codes):
        for code in codes:
            self.jobs[code // 16].step(code % 16)

    def slot(self):
        self.do(self.take())

    def loop(self, count, body, inner=1):
        plan = [[self.take() for _ in range(inner)] for _ in range(count)]

        @pl.loop(0, count)
        def _(it):
            def at(sub):
                for n in range(count):
                    if plan[n][sub]:
                        pl.when(it == n)(functools.partial(self.do, plan[n][sub]))

            at(0)
            if inner > 1:
                body(it, at)
            else:
                body(it)


def tile(t, size):
    return pl.ds(pl.multiple_of(t * size, size), size)


def cols_of(n, width):
    return pl.ds(pl.multiple_of(n * width, 128), width)


def rotation(seg):
    counts = [jnp.sum(jnp.where(seg == u, 1.0, 0.0), 1, keepdims=True) for u in range(3)]
    start = counts[0] + counts[1] + counts[2]
    start = jnp.where(counts[2] == HALF, counts[0] + counts[1], start)
    start = jnp.where(counts[1] == HALF, counts[0], start)
    return jnp.where(counts[0] == HALF, 0.0, start)


def turn(t, start, back):
    row = (lax.broadcasted_iota(jnp.int32, (ROWS, TOK), 0) + t * ROWS).astype(f32)
    col = lax.broadcasted_iota(jnp.int32, (ROWS, TOK), 1).astype(f32)
    source = row - start if back else row + start
    source = jnp.where(source < 0.0, source + TOK, jnp.where(source >= TOK, source - TOK, source))
    return jnp.where(source == col, 1.0, 0.0).astype(bf16)


def column_of(row):
    return jnp.broadcast_to(row, (128, row.shape[1])).T


def attend_pair(q, k, v, bias, prob_ref):
    q = q * jnp.bfloat16(0.125)
    outs = []
    for h in range(2):
        qh = jnp.where(lane_half(h, q.shape), q, jnp.bfloat16(0))
        scores = dot(qh, k, NT) + bias
        scores = jnp.exp(scores - jnp.max(scores, 1, keepdims=True))
        probs = (scores * (1.0 / jnp.sum(scores, 1, keepdims=True))).astype(bf16)
        prob_ref[h] = probs
        outs.append(dot(probs, v, NN))
    return jnp.where(lane_half(0, outs[0].shape), outs[0], outs[1]).astype(bf16)


def attend_pair_back(q, k, v, grad, ctx, prob_ref):
    product = grad.astype(f32) * ctx.astype(f32)
    dq, dk, dv = [], [], []
    for h in range(2):
        lanes = lane_half(h, grad.shape)
        grad_h = jnp.where(lanes, grad, jnp.bfloat16(0))
        row_dot = jnp.sum(jnp.where(lanes, product, 0.0), 1, keepdims=True)
        probs = prob_ref[h]
        ds = (probs.astype(f32) * (dot(grad_h, v, NT) - row_dot)).astype(bf16)
        dq.append(dot(ds, k, NN))
        dk.append(dot(ds, q, TN))
        dv.append(dot(probs, grad, TN))
    lanes = lane_half(0, grad.shape)
    return [
        (jnp.where(lanes, dq[0], dq[1]) * 0.125).astype(bf16),
        (jnp.where(lanes, dk[0], dk[1]) * 0.125).astype(bf16),
        jnp.where(lanes, dv[0], dv[1]).astype(bf16),
    ]


def bias_row(small_ref, first, bias_len):
    total = jnp.zeros((8, 1024), f32)
    lanes = lax.broadcasted_iota(jnp.int32, (8, 256), 1)
    for d in range(first // bias_len, (first + D - 1) // bias_len + 1):
        piece = jnp.where(lanes < bias_len, jnp.broadcast_to(small_ref[8 * d : 8 * d + 1, :], (8, 256)), 0.0)
        piece = jnp.concatenate([piece, jnp.zeros((8, 768), f32)], axis=1)
        shift = (bias_len * d - first) % 1024
        total = total + (pltpu.roll(piece, shift, 1) if shift else piece)
    return total[:1, :D]


PAIRS = H // 2


def normed_of(residual):
    center = residual - jnp.mean(residual, 1, keepdims=True)
    scale = lax.rsqrt(jnp.mean(center * center, 1, keepdims=True) + EPSILON)
    return center * scale, scale


def norm_back(grad, gain, unit, scale):
    grad = grad * gain
    return scale * (grad - jnp.mean(grad, 1, keepdims=True) - unit * jnp.mean(grad * unit, 1, keepdims=True))


PAIRS = H // 2
THIRD = D // 3
PAIR = 2 * HD


def entry_cols(j, matrix, feat, pos, cot, entry, low, cot_out):
    cols = cols_of(j, 256)
    value = dot(matrix[...], feat[:, cols], NN) + dot(matrix[...], pos[:, cols], NN)
    entry[:, cols] = value
    low[:, cols] = value.astype(bf16)
    cot_out[:, cols] = dot(matrix[...], cot[:, cols], NN).astype(bf16)


def mask_half(h, matrix, stack, mask):
    matrix = matrix[h * HALF : (h + 1) * HALF, :]
    by_row = dot(stack, matrix, NT)
    by_col = dot(matrix, stack, NT)
    rows = lax.broadcasted_iota(jnp.int32, (HALF, HALF), 0)
    cols = lax.broadcasted_iota(jnp.int32, (HALF, HALF), 1)
    allowed = (by_col[:, 1:2] == by_row[1:2, :]) & ((by_row[0:1, :] > 0.0) | (rows == cols))
    mask[h] = jnp.where(allowed, 0.0, MASKED)


def stack_of(valid, seg):
    row = lax.broadcasted_iota(jnp.int32, (8, TOK), 0)
    both = jnp.where(row == 0, valid.astype(f32), jnp.where(row == 1, seg.astype(f32), 0.0))
    return both.astype(bf16)


def gain_row(small, which, gain_len):
    ranks = small.shape[0] // 8
    row = lax.broadcasted_iota(jnp.int32, (ranks, 8 * ranks), 0)
    col = lax.broadcasted_iota(jnp.int32, (ranks, 8 * ranks), 1)
    pick = jnp.where(col == 8 * row + which, 1.0, 0.0).astype(bf16)
    values = dot(pick, small[...].astype(bf16), NN).astype(bf16)
    lane = lax.broadcasted_iota(jnp.int32, (256, D), 1).astype(f32)
    home = jnp.floor((lane + 0.5) * (1.0 / gain_len))
    spot = lax.broadcasted_iota(jnp.int32, (256, D), 0).astype(f32)
    spread = dot(values, jnp.where(lane - home * gain_len == spot, 1.0, 0.0).astype(bf16), NN)
    owner = lax.broadcasted_iota(jnp.int32, (ranks, D), 0).astype(f32)
    return jnp.sum(jnp.where(home[:ranks] == owner, spread, 0.0), 0, keepdims=True)


SLOPE_COLS = 768
WIDE = 512
STRIPS = [[(which * D + g * THIRD, which * THIRD, THIRD) for which in range(3)] for g in range(3)]


def front_kernel(linked, bias_len, gain_len, *refs):
    n = 7
    if linked:
        (bias_in, gains_in, qkv_w, proj_w, expand_w, reduce_w), refs = refs[:6], refs[6:]
    else:
        (bias_in, gains_in, *weights_in), refs = refs[:8], refs[8:]
    (feat_in, pos_in, cot_in, seg_ref, valid_ref), refs = refs[:5], refs[5:]
    if linked:
        weights_out, refs = refs[:6], refs[6:]
    outs, refs = refs[:10], refs[10:]
    low_out, qkv_out, ctx_out, prob_out, unit_out, nlow_out, act_out, slope_out, gs_out, layer_out = outs
    (gains, dvec), refs = refs[:2], refs[2:]
    (feat, pos, cot_raw, entry, low, cot, mask, small, w_a, w_b, w_c, w_p, w_e, w_r, bias), refs = refs[:15], refs[15:]
    (qkv, ctx, probs, act, slope, total, unit_stage, ins, sent, psem, ssem, usem, rsem), refs = refs[:13], refs[13:]
    loads = [pltpu.make_async_copy(a, b, ins.at[i]) for i, (a, b) in enumerate(((feat_in, feat), (pos_in, pos), (cot_in, cot_raw)))]
    thirds = [w_a, w_b, w_c]
    homes = [*thirds, w_p, w_e, w_r]
    nlow, layer = feat, pos
    counted = iter(range(16))
    store = lambda a, b: pltpu.make_async_copy(a, b, sent.at[next(counted)])
    store_low, store_ctx, store_nlow = store(low, low_out), store(ctx, ctx_out), store(nlow, nlow_out)
    store_act, store_layer = store(act, act_out), store(layer, layer_out)
    store_qkv = [store(qkv.at[g], qkv_out.at[g]) for g in range(3)]
    store_w = [store(a, b) for a, b in zip(homes, weights_out)] if linked else []
    for copy in loads:
        copy.start()
    jobs = []
    if linked:
        (shard, *refs) = refs
        place = Place()
        shard[...] = jnp.zeros_like(shard)
        shard[0:1, :bias_len] = bias_in[...].astype(bf16).astype(f32)
        shard[1:3, :gain_len] = gains_in[...].astype(bf16).astype(f32)
        place.greet()
        sources = [(qkv_w, w, STRIPS[g], True) for g, w in enumerate(thirds)]
        sources += [(a, b, [(0, 0, b.shape[1])], b is w_p or b is small) for a, b in ((proj_w, w_p), (expand_w, w_e), (reduce_w, w_r), (shard, small))]
        jobs = [Gather(place, *args, refs[i * GATHER_SCRATCH : (i + 1) * GATHER_SCRATCH]) for i, args in enumerate(sources)]
        for i in (0, 6, 1, 2, 3, 4, 5):
            jobs[i].load()
    else:
        for i, (a, b) in enumerate(zip(weights_in, homes)):
            copy = pltpu.make_async_copy(a, b, sent.at[9 + i])
            copy.start()
            copy.wait()
    steps = Steps(FRONT_PLAN, jobs)

    def ready(i):
        steps.slot()
        if linked:
            jobs[i].arrive_all()
            if i < 6:
                store_w[i].start()

    steps.slot()
    for copy in loads:
        copy.wait()
    seg = seg_ref[...]
    start = rotation(seg)
    stack = stack_of(valid_ref[...], seg)
    matrix = act.at[:, :TOK]
    valid = column_of(valid_ref[...].astype(f32))[:, :1].astype(bf16)
    feat[...] = feat[...] * valid
    pos[...] = pos[...] * valid

    steps.slot()

    @pl.loop(0, 4)
    def _(t):
        matrix[tile(t, ROWS), :] = turn(t, start, False)

    steps.loop(3, lambda j: entry_cols(j, matrix, feat, pos, cot_raw, entry, low, cot))
    store_low.start()
    for h in range(2):
        steps.slot()
        mask_half(h, matrix, stack, mask)
    dvec[...] = jnp.zeros_like(dvec)
    ready(6)
    ready(0)
    if linked:
        for block in range(2):
            bias[0:1, block * D : (block + 1) * D] = bias_row(small, block * D, bias_len)
    else:
        bias[0:1, :] = bias_in[...]
        gains[0:2, :] = gains_in[...]

    def prob_store(it):
        return pltpu.make_async_copy(probs.at[it % 2], prob_out.at[pl.ds(2 * it, 2)], psem.at[it % 2])

    for g in range(3):
        if g:
            ready(g)

        for which in range(3):
            steps.slot()
            cols = slice(which * THIRD, (which + 1) * THIRD)
            value = dot(low[...], thirds[g][:, cols], NN)
            if which != 1:
                first = (which // 2) * D + g * THIRD
                value = value + bias[0:1, first : first + THIRD]
            qkv[g, :, cols] = value.astype(bf16)
        store_qkv[g].start()

        def attention(i):
            it = 4 * g + i
            pair, half = i // 2, i % 2
            rows = tile(half, HALF)
            cut = lambda which: qkv[g, rows, cols_of(2 * which + pair, PAIR)]
            if g:
                prob_store(it - 2).wait()
            else:
                pl.when(it >= 2)(lambda: prob_store(it - 2).wait())
            ctx[rows, cols_of(2 * g + pair, PAIR)] = attend_pair(cut(0), cut(1), cut(2), mask[half], probs.at[it % 2])
            prob_store(it).start()

        steps.loop(4, attention)
    store_ctx.start()
    if linked:
        for block in range(2, 10):
            bias[0:1, block * D : (block + 1) * D] = bias_row(small, block * D, bias_len)
        for which in range(2):
            gains[which : which + 1, :] = gain_row(small, 1 + which, gain_len)
    b_2 = bias[0:1, 3 * D + FF : 4 * D + FF]
    c_1, c_2 = bias[0:1, 4 * D + FF : 5 * D + FF], bias[0:1, 5 * D + FF : 6 * D + FF]
    g_1, g_2 = gains[0:1, :], gains[1:2, :]
    ready(3)

    def slope_store(j):
        return pltpu.make_async_copy(slope.at[j % 2], slope_out.at[:, cols_of(j, WIDE)], ssem.at[j % 2])

    def unit_store(t):
        return pltpu.make_async_copy(unit_stage.at[t % 2], unit_out.at[tile(t, ROWS)], usem.at[t % 2])

    def first_norm(t):
        rows = tile(t, ROWS)
        unit, scale = normed_of(entry[rows, :])
        pl.when(t >= 2)(lambda: unit_store(t - 2).wait())
        unit_stage[t % 2, :, :D] = unit
        unit_stage[t % 2, :, D:] = jnp.broadcast_to(scale, (ROWS, 128))
        unit_store(t).start()
        normed = unit * g_1 + c_1
        nlow[rows, :] = normed.astype(bf16)
        total[rows, :] = normed + b_2

    def expand(j):
        cols = cols_of(j, WIDE)
        pre = dot(nlow[...], w_e[:, cols], NN) + bias[0:1, pl.ds(pl.multiple_of(3 * D + j * WIDE, 128), WIDE)]
        cdf = 0.5 + 0.5 * lax.erf(pre * 0.7071067811865476)
        act[:, cols] = (pre * cdf).astype(bf16)
        pl.when(j >= 2)(lambda: slope_store(j - 2).wait())
        slope[j % 2] = (cdf + pre * (0.3989422804014327 * jnp.exp(-0.5 * pre * pre))).astype(bf16)
        slope_store(j).start()

    for j in range(3):
        steps.slot()
        cols = slice(j * 256, (j + 1) * 256)
        entry[:, cols] = entry[:, cols] + dot(ctx[...], w_p[:, cols], NN) + bias[0:1, 2 * D + j * 256 : 2 * D + (j + 1) * 256]
    steps.loop(4, first_norm)
    ready(4)
    steps.loop(FF // WIDE, expand)
    store_nlow.start()
    store_act.start()
    for k in range(4):
        if linked:
            steps.slot()
            jobs[5].arrive(k)
            zz = place.order[k]
        else:
            zz = k

        if linked and k == 3:
            store_w[5].start()
        for j in range(3):
            cols = slice(j * 256, (j + 1) * 256)
            total[:, cols] += dot(act[:, cols_of(zz, D)], w_r[cols_of(zz, D), cols], NN)

    def row_store(t):
        return pltpu.make_async_copy(total.at[tile(t, ROWS)], gs_out.at[tile(t, ROWS)], rsem.at[t])

    @pl.loop(0, 4)
    def _(t):
        rows = tile(t, ROWS)
        unit, scale = normed_of(total[rows, :])
        layer[rows, :] = (unit * g_2 + c_2).astype(bf16)
        grad = cot[rows, :].astype(f32)
        dvec[0:1, :] += jnp.sum(grad * unit, 0, keepdims=True)
        dvec[1:2, :] += jnp.sum(grad, 0, keepdims=True)
        value = norm_back(grad, g_2, unit, scale)
        total[rows, :] = value
        dvec[2:3, :] += jnp.sum(value.astype(bf16).astype(f32), 0, keepdims=True)
        row_store(t).start()

    store_layer.start()
    prob_store(10).wait()
    prob_store(11).wait()
    slope_store(FF // WIDE - 2).wait()
    slope_store(FF // WIDE - 1).wait()
    unit_store(2).wait()
    unit_store(3).wait()
    if linked:
        for job in jobs:
            job.drain()
    for copy in (store_low, store_ctx, store_nlow, store_act, store_layer, *store_qkv, *store_w):
        copy.wait()
    for t in range(4):
        row_store(t).wait()


def front(linked, bias_len, gain_len, bias, gains, weights, features, pos_conv, cotangent, segments, valid):
    wide = [S((D, D), bf16)] * 4 + [S((D, FF), bf16), S((FF, D), bf16)]
    outs = list(wide) if linked else []
    outs += [
        S((TOK, D), bf16), S((3, TOK, D), bf16), S((TOK, D), bf16), S((2 * H, HALF, HALF), bf16), S((TOK, D + 128), f32),
        S((TOK, D), bf16), S((TOK, FF), bf16), S((TOK, FF), bf16), S((TOK, D), f32), S((TOK, D), bf16),
    ]
    hbm = len(outs)
    outs += [S((8, D), f32), S((8, D), f32)]
    half = pltpu.VMEM((TOK, D), bf16)
    scratch = [half, half, half, pltpu.VMEM((TOK, D), f32), half, half, pltpu.VMEM((2, HALF, HALF), f32), pltpu.VMEM((256, 256), f32)]
    scratch += [pltpu.VMEM(w.shape, bf16) for w in wide] + [pltpu.VMEM((1, 6 * D + FF), f32)]
    scratch += [
        pltpu.VMEM((3, TOK, D), bf16), half, pltpu.VMEM((2, 2, HALF, HALF), bf16), pltpu.VMEM((TOK, FF), bf16),
        pltpu.VMEM((2, TOK, WIDE), bf16), pltpu.VMEM((TOK, D), f32), pltpu.VMEM((2, ROWS, D + 128), f32),
        DMA((3,)), DMA((16,)), DMA((2,)), DMA((2,)), DMA((2,)), DMA((4,)),
    ]
    more = {}
    if linked:
        more = dict(collective_id=0, has_side_effects=True)
        scratch += [pltpu.VMEM((8, 256), f32)]
        for w in wide:
            scratch += Gather.scratch(w.shape[0] // 32, w.shape[1], bf16)
        scratch += Gather.scratch(8, 256, f32)
    return pl.pallas_call(
        functools.partial(front_kernel, linked, bias_len, gain_len),
        in_specs=[IN_VMEM] * 2 + [IN_HBM] * (len(weights) + 3) + [IN_VMEM] * 2,
        out_specs=[IN_HBM] * hbm + [IN_VMEM] * 2,
        out_shape=outs,
        scratch_shapes=scratch,
        compiler_params=params(**more),
        name="front",
    )(bias, gains, *weights, features, pos_conv, cotangent, segments, valid)


class Exchange:
    def __init__(self, place, total, slots, send, recv):
        z = place.z
        self.others = (place.partner, place.xn, place.yn, place.me + 8 - 16 * (z % 2), place.me + 16 - 32 * (z // 2))
        self.total, self.slots, self.send, self.recv = total, slots, send, recv

    def copy(self, n):
        return remote(self.slots.at[n], self.slots.at[5 + n], self.send.at[n], self.recv.at[n], self.others[n])

    def begin(self, n):
        self.slots[n] = self.total[...]
        self.copy(n).start()

    def end(self, n):
        self.copy(n).wait()
        self.total[...] += self.slots[5 + n]


VECTOR_ROWS = 72


def put(vector, row, value):
    for i in range(value.shape[1] // 128):
        vector[row + i : row + i + 1, :] = value[:, 128 * i : 128 * (i + 1)]


def back_kernel(linked, *refs):
    weights_in, refs = refs[:6], refs[6:]
    (low_in, qkv_in, ctx_in, prob_in, unit_in, nlow_in, act_in, slope_in, gs_in, layer_in), refs = refs[:10], refs[10:]
    (gains, dvec, seg_ref, valid_ref), refs = refs[:4], refs[4:]
    names = 6
    if linked:
        sums, refs = refs[:names], refs[names:]
    else:
        parts_out, refs = refs[:names], refs[names:]
    (input_out, layer_out, vector), refs = refs[:3], refs[3:]
    (big, w_e, w_r, hold_r, w_p, gs, grad, branch, ctx, low, probs, slope, unit, hold_p, hold_a, hold_b, hold_c, gain, db1), refs = refs[:19], refs[19:]
    (ins, psem, ssem, usem), refs = refs[:4], refs[4:]
    holds = [hold_a, hold_b, hold_c, hold_p, w_e, hold_r]
    counted = iter(range(24))
    copy = lambda a, b: pltpu.make_async_copy(a, b, ins.at[next(counted)])
    load_gs, load_act, load_wr, load_we = copy(gs_in, gs), copy(act_in, big), copy(weights_in[5], w_r), copy(weights_in[4], w_e)
    load_wp, load_nlow, load_ctx = copy(weights_in[3], w_p), copy(nlow_in, low), copy(ctx_in, ctx)
    load_low, load_layer = copy(low_in, low), copy(layer_in, branch)
    load_qkv = [copy(qkv_in.at[g], w_r.at[g * TOK : (g + 1) * TOK]) for g in range(3)]
    load_w = [copy(weights_in[g], hold_r.at[g * D : (g + 1) * D]) for g in range(3)]
    store_layer, store_input = copy(grad, layer_out), copy(ctx, input_out)
    load_gs.start()
    load_act.start()

    def slope_load(t, k):
        return pltpu.make_async_copy(slope_in.at[tile(t, ROWS), slice(k * SLOPE_COLS, (k + 1) * SLOPE_COLS)], slope.at[k % 2], ssem.at[k % 2])

    def unit_load(t):
        return pltpu.make_async_copy(unit_in.at[tile(t, ROWS)], unit.at[t % 2], usem.at[t % 2])

    def prob_load(it):
        return pltpu.make_async_copy(prob_in.at[pl.ds(2 * it, 2)], probs.at[it % 2], psem.at[it % 2])

    jobs = []
    sender = 0
    if linked:
        (slots, send, recv), refs = refs[:3], refs[3:]
        place = Place()
        sender = 1 - place.c
        jobs = [Scatter(place, holds[i], sums[i], refs[i * SCATTER_SCRATCH : (i + 1) * SCATTER_SCRATCH]) for i in range(names)]
        swap = Exchange(place, vector, slots, send, recv)
        place.greet()
    steps = Steps(BACK_PLAN, jobs)

    def exchange(i):
        if linked:
            for k in (3, 2, 1, 0):
                jobs[i].exchange(k)

    load_gs.wait()

    @pl.loop(0, 4)
    def _(t):
        rows = tile(t, ROWS)
        grad[rows, :] = gs[rows, :].astype(bf16)

    load_act.wait()
    for load in (load_wr, load_we, load_wp, load_nlow, load_ctx):
        load.start()
    slope_load(0, 0).start()
    slope_load(0, 1).start()
    unit_load(0).start()
    prob_load(0).start()
    for k in (3, 2, 1, 0):
        zz = place.order[k] if linked else k
        steps.slot()

        hold_r[tile(zz, D), :] = dot(big[:, cols_of(zz, D)], grad[...], TN).astype(bf16)

        if linked:
            jobs[5].exchange(k)
    for load in (load_wr, load_we, load_wp):
        load.wait()
    gain[...] = jnp.zeros_like(gain)
    db1[...] = jnp.zeros_like(db1)
    g_1 = gains[0:1, :]

    def ffn_back(t, at):
        rows = tile(t, ROWS)
        pl.when(t < 3)(lambda: unit_load(t + 1).start())
        gffn = grad[rows, :]
        total = gs[rows, :]
        for k in range(FF // SLOPE_COLS):
            if k:
                at(k)
            cols = slice(k * SLOPE_COLS, (k + 1) * SLOPE_COLS)
            slope_load(t, k).wait()
            gpre = (dot(gffn, w_r[cols, :], NT) * slope[k % 2].astype(f32)).astype(bf16)
            if k < 2:
                slope_load(t, k + 2).start()
            else:
                pl.when(t < 3)(lambda: slope_load(t + 1, k - 2).start())
            big[rows, cols] = gpre
            db1[0:1, cols] += jnp.sum(gpre.astype(f32), 0, keepdims=True)
            total = total + dot(gpre, w_e[:, cols], NT)
        unit_load(t).wait()
        unit_1, scale_1 = unit[t % 2, :, :D], unit[t % 2, :, D : D + 1]
        gain[0:1, :] += jnp.sum(total * unit_1, 0, keepdims=True)
        gain[1:2, :] += jnp.sum(total, 0, keepdims=True)
        first = norm_back(total, g_1, unit_1, scale_1)
        gs[rows, :] = first
        lowered = first.astype(bf16)
        branch[rows, :] = lowered
        gain[2:3, :] += jnp.sum(lowered.astype(f32), 0, keepdims=True)
        grad[rows, :] = dot(lowered, w_p[...], NT).astype(bf16)

    steps.loop(4, ffn_back, 4)
    for load in load_qkv:
        load.start()
    load_nlow.wait()

    def expand_grad(j):
        cols = pl.ds(pl.multiple_of(((sender + j // 2) % 2) * (FF // 2) + (j % 2) * D, 256), D)
        w_e[:, cols] = dot(low[...], big[:, cols], TN).astype(bf16)

    steps.loop(2, expand_grad)
    exchange(4)
    steps.loop(2, lambda j: expand_grad(j + 2))
    load_low.start()
    load_ctx.wait()

    def square_grad(hold, left, right, at):
        def half(j):
            first = ((sender + j) % 2) * (D // 2)
            cols = pl.ds(pl.multiple_of(first, 128), D // 2)
            source = pl.ds(pl.multiple_of(at + first, 128), D // 2)
            hold[:, cols] = dot(left[...], right[:, source], TN).astype(bf16)

        return half

    square = square_grad(hold_p, ctx, branch, 0)
    steps.slot()
    square(0)
    exchange(3)
    steps.slot()
    square(1)
    load_layer.start()
    for load in load_qkv:
        load.wait()
    load_low.wait()
    for g in range(3):

        def attention(i):
            it = 4 * g + i
            pair, half = i // 2, i % 2
            rows = tile(half, HALF)
            cut = lambda which: w_r[pl.ds(pl.multiple_of(g * TOK + half * HALF, HALF), HALF), cols_of(2 * which + pair, PAIR)]
            if g < 2:
                prob_load(it + 1).start()
            else:
                pl.when(i < 3)(lambda: prob_load(it + 1).start())
            prob_load(it).wait()
            own = cols_of(2 * g + pair, PAIR)
            three = attend_pair_back(cut(0), cut(1), cut(2), grad[rows, own], ctx[rows, own], probs.at[it % 2])
            for which, value in enumerate(three):
                big[rows, cols_of(6 * g + 2 * which + pair, PAIR)] = value

        steps.loop(4, attention)
        square = square_grad(holds[g], low, big, g * D)
        steps.slot()
        square(0)
        exchange(g)
        steps.slot()
        square(1)
    for g in range(3):
        for which, row in ((0, 2 * g), (2, 6 + 2 * g)):
            at = g * D + which * THIRD
            put(vector, row, jnp.sum(big[:, at : at + THIRD].astype(f32), 0, keepdims=True))
    put(vector, 12, gain[2:3, :])
    put(vector, 18, db1[...])
    put(vector, 42, dvec[2:3, :])
    put(vector, 48, gain[1:2, :])
    put(vector, 54, dvec[1:2, :])
    put(vector, 60, gain[0:1, :])
    put(vector, 66, dvec[0:1, :])
    if linked:
        swap.begin(0)
    start = rotation(seg_ref[...])
    load_layer.wait()

    def layer_back(t):
        rows = tile(t, ROWS)
        grad[rows, :] = dot(turn(t, start, True), branch[...], NN).astype(bf16)

    steps.loop(4, layer_back)
    store_layer.start()
    steps.slot()
    if linked:
        swap.end(0)
        swap.begin(1)
        steps.slot()
        jobs[5].finish()
    else:
        outs = [pltpu.make_async_copy(a, b, ins.at[18 + i]) for i, (a, b) in enumerate(zip(holds, parts_out))]
        for store in outs:
            store.start()
        for store in outs:
            store.wait()
    for load in load_w:
        load.start()
    for load in load_w:
        load.wait()

    def swapped(n):
        swap.end(n)
        swap.begin(n + 1)

    def input_grad(t):
        if linked:
            pl.when(t == 2)(lambda: swapped(1))
        rows = tile(t, ROWS)
        value = gs[rows, :]
        for g in range(3):
            value = value + dot(big[rows, g * D : (g + 1) * D], hold_r[g * D : (g + 1) * D, :], NT)
        big[rows, 3 * D : 4 * D] = value.astype(bf16)

    steps.loop(4, input_grad)

    def input_back(t):
        if linked:
            pl.when(t == 1)(lambda: swapped(2))
        rows = tile(t, ROWS)
        ctx[rows, :] = dot(turn(t, start, True), big[:, 3 * D : 4 * D], NN).astype(bf16)

    steps.loop(4, input_back)
    ctx[...] = ctx[...] * column_of(valid_ref[...].astype(f32))[:, :1].astype(bf16)
    store_input.start()
    if linked:
        swapped(3)
        steps.slot()
        swap.end(4)
        for job in jobs[:5]:
            job.finish()
    store_layer.wait()
    store_input.wait()


def back(linked, weights, *arrays):
    wide = [(D, D)] * 4 + [(D, FF), (FF, D)]
    outs = [S((r // 32, c), f32) for r, c in wide] if linked else [S(s, bf16) for s in wide]
    outs += [S((TOK, D), bf16), S((TOK, D), bf16), S((VECTOR_ROWS, 128), f32)]
    half = pltpu.VMEM((TOK, D), bf16)
    square = pltpu.VMEM((D, D), bf16)
    scratch = [
        pltpu.VMEM((TOK, FF), bf16), pltpu.VMEM((D, FF), bf16), pltpu.VMEM((FF, D), bf16), pltpu.VMEM((FF, D), bf16), square,
        pltpu.VMEM((TOK, D), f32), half, half, half, half, pltpu.VMEM((2, 2, HALF, HALF), bf16), pltpu.VMEM((2, ROWS, SLOPE_COLS), bf16),
        pltpu.VMEM((2, ROWS, D + 128), f32), square, square, square, square, pltpu.VMEM((8, D), f32), pltpu.VMEM((1, FF), f32),
        DMA((24,)), DMA((2,)), DMA((2,)), DMA((2,)),
    ]
    more = {}
    if linked:
        more = dict(collective_id=1, has_side_effects=True)
        scratch += [pltpu.VMEM((10, VECTOR_ROWS, 128), f32), DMA((5,)), DMA((5,))]
        for r, c in wide:
            scratch += Scatter.scratch(r // 32, c, bf16)
    return pl.pallas_call(
        functools.partial(back_kernel, linked),
        in_specs=[IN_HBM] * 16 + [IN_VMEM] * 4,
        out_specs=[IN_VMEM if linked else IN_HBM] * 6 + [IN_HBM] * 2 + [IN_VMEM],
        out_shape=outs,
        scratch_shapes=scratch,
        compiler_params=params(**more),
        name="back",
    )(*weights, *arrays)


def update_kernel(rates, *refs):
    passed, thirds, refs = refs[:2], refs[2:5], refs[5:]
    count = len(rates)
    ins, outs, sent, held, sems = refs[: 4 * count - 1], refs[4 * count - 1 : -5], refs[-5:-3], refs[-3:-1], refs[-1]
    loads = [pltpu.make_async_copy(a, b, sems.at[i]) for i, (a, b) in enumerate(zip(passed, held))]
    copies = [pltpu.make_async_copy(a, b, sems.at[2 + i]) for i, (a, b) in enumerate(zip(held, sent))]
    for load in loads:
        load.start()
    for load, copy in zip(loads, copies):
        load.wait()
        copy.start()
    for i, rate in enumerate(rates):
        if i:
            w_ref, g_ref, m_ref, a_ref = ins[4 * i - 1 : 4 * i + 3]
            pieces = [(slice(None), g_ref[...])]
        else:
            w_ref, m_ref, a_ref = ins[:3]
            pieces = []
            for g in range(3):
                for which in range(3):
                    at = which * D + g * THIRD
                    pieces.append((slice(at, at + THIRD), thirds[g][:, which * THIRD : (which + 1) * THIRD]))
        for cols, grad in pieces:
            velocity = 0.5 * m_ref[:, cols] + grad
            master = w_ref[:, cols] - rate * (grad + 0.5 * velocity)
            for ref, value in zip(outs[4 * i : 4 * i + 4], (grad, master, velocity, 0.5 * a_ref[:, cols] + 0.5 * master)):
                ref[:, cols] = value
    for copy in copies:
        copy.wait()


def update(rates, passed, thirds, arrays):
    shapes = [arrays[0].shape] * 4
    for a in arrays[3::4]:
        shapes += [a.shape] * 4
    return pl.pallas_call(
        functools.partial(update_kernel, rates),
        in_specs=[IN_HBM] * 2 + [IN_VMEM] * (3 + len(arrays)),
        out_specs=[IN_VMEM] * len(shapes) + [IN_HBM] * 2,
        out_shape=[S(s, f32) for s in shapes] + [S(a.shape, a.dtype) for a in passed],
        scratch_shapes=[pltpu.VMEM(a.shape, a.dtype) for a in passed] + [DMA((4,))],
        compiler_params=params(),
        name="update",
    )(*passed, *thirds, *arrays)


def local(linked, *args):
    (
        features, pos_conv, segment_ids, frame_valid, cotangent,
        qkv_weight, proj_weight, expand_weight, reduce_weight, norm_gains, bias_vector,
        qkv_moment, proj_moment, expand_moment, reduce_moment, gains_moment, bias_moment,
        qkv_average, proj_average, expand_average, reduce_average, gains_average, bias_average,
    ) = args
    ranks = lax.axis_size("dp")
    me = lax.axis_index("dp")
    bias_len = bias_vector.shape[0]
    gain_len = norm_gains.shape[1]
    if linked:
        bias, gains = bias_vector[None], norm_gains
        weights = [qkv_weight, proj_weight, expand_weight, reduce_weight]
    else:
        round_to = lambda w: lax.reduce_precision(w, 8, 7)
        bias = lax.all_gather(round_to(bias_vector), "dp", axis=0, tiled=True)[None]
        gains = lax.all_gather(round_to(norm_gains), "dp", axis=1, tiled=True)
        qkv_full, *weights = [
            lax.all_gather(w.astype(bf16), "dp", axis=0, tiled=True) for w in (qkv_weight, proj_weight, expand_weight, reduce_weight)
        ]
        weights = [jnp.concatenate([qkv_full[:, a : a + w] for a, _, w in STRIPS[g]], axis=1) for g in range(3)] + weights
    outs = front(linked, bias_len, gain_len, bias, gains, weights, features, pos_conv, cotangent, segment_ids, frame_valid)
    if linked:
        weights, outs = outs[:6], outs[6:]
    *sums, grad_input, layer_out, vector = back(linked, weights, *outs, segment_ids, frame_valid)
    if not linked:
        sums = [lax.psum_scatter(p.astype(f32), "dp", scatter_dimension=0, tiled=True) for p in sums]
        vector = lax.psum(vector, "dp")
    *thirds, proj_grad, expand_grad, reduce_grad = sums
    vector = vector.reshape(-1)
    bias_grad = lax.dynamic_slice(vector, (me * bias_len,), (bias_len,))
    gains_grad = lax.dynamic_slice(vector[6 * D + FF :].reshape(2, D), (0, me * gain_len), (2, gain_len))
    root = math.sqrt(ranks * features.shape[0])
    matrix, proj, little = rate_matrix / root, rate_proj / root, rate_small / root
    *updated, layer_out, grad_input = update(
        (matrix, proj, matrix, matrix),
        [layer_out, grad_input],
        thirds,
        [
            qkv_weight, qkv_moment, qkv_average,
            proj_weight, proj_grad, proj_moment, proj_average,
            expand_weight, expand_grad, expand_moment, expand_average,
            reduce_weight, reduce_grad, reduce_moment, reduce_average,
        ],
    )

    def nesterov(master, gradient, moment, average):
        velocity = 0.5 * moment + gradient
        renewed = master - little * (gradient + 0.5 * velocity)
        return gradient, renewed, velocity, 0.5 * average + 0.5 * renewed

    gains_new = nesterov(norm_gains, gains_grad, gains_moment, gains_average)
    bias_new = nesterov(bias_vector, bias_grad, bias_moment, bias_average)
    results = [layer_out, grad_input]
    for i in range(4):
        results += [updated[i], updated[4 + i], updated[8 + i], updated[12 + i], gains_new[i], bias_new[i]]
    return tuple(results)


def solution(mesh):
    linked = mesh.shape["dp"] == 32
    rows, lanes, line = P("dp", None), P(None, "dp"), P("dp")
    six = (rows, rows, rows, rows, lanes, line)
    return jax.shard_map(
        functools.partial(local, linked),
        mesh=mesh,
        in_specs=(rows,) * 5 + six * 3,
        out_specs=(rows, rows) + six * 4,
        check_vma=False,
    )
```

```python
import functools
import math

import jax
import jax.numpy as jnp
from jax import lax
from jax.experimental import pallas as pl
from jax.experimental.pallas import tpu as pltpu
from jax.sharding import PartitionSpec as P

D = 768
H = 12
HD = 64
FF = 3072
TOK = 1024
HALF = 512
ROWS = 256
COLS = 768

EPSILON = 1e-05
MASKED = -1000000000.0
rate_matrix = 0.04
rate_proj = 0.5
rate_small = 0.2

f32 = jnp.float32
bf16 = jnp.bfloat16
NN = (((1,), (0,)), ((), ()))
NT = (((1,), (1,)), ((), ()))
TN = (((0,), (0,)), ((), ()))
MESH = pl.DeviceIdType.MESH
VMEM_LIMIT = 60 << 20
IN_VMEM = pl.BlockSpec(memory_space=pltpu.VMEM)
IN_HBM = pl.BlockSpec(memory_space=pl.ANY)
S = jax.ShapeDtypeStruct


def dot(a, b, dims):
    return lax.dot_general(a, b, dims, preferred_element_type=f32)


def lane_half(h, shape):
    return (lax.broadcasted_iota(jnp.int32, shape, 1) // HD) == h


def params(**more):
    return pltpu.CompilerParams(vmem_limit_bytes=VMEM_LIMIT, **more)


class Place:
    def __init__(self):
        me = lax.axis_index("dp")
        self.me = me
        self.c, self.x, self.y, self.z = me % 2, (me // 2) % 2, (me // 4) % 2, me // 8
        self.chip = me // 2
        self.partner = me + 1 - 2 * self.c
        self.xn = me + 2 - 4 * self.x
        self.yn = me + 4 - 8 * self.y
        self.up = me + 8
        self.down = me - 8
        z = self.z
        first = jnp.where(z == 0, 1, jnp.where(z == 1, 0, jnp.where(z == 2, 3, 2)))
        second = jnp.where(z == 0, 2, jnp.where(z == 1, 2, 1))
        third = jnp.where(z < 2, 3, 0)
        self.order = (z, first, second, third)

    def other(self, zz, dx=False, dy=False):
        x = 1 - self.x if dx else self.x
        y = 1 - self.y if dy else self.y
        return zz * 4 + y * 2 + x

    def greet(self):
        barrier = pltpu.get_barrier_semaphore()
        for other in (self.partner, self.xn, self.yn, *(zz * 8 + self.me % 8 for zz in self.order[1:])):
            pl.semaphore_signal(barrier, inc=1, device_id=(other,), device_id_type=MESH)
        pl.semaphore_wait(barrier, 6)


def remote(src, dst, send, recv, other):
    return pltpu.make_async_remote_copy(
        src_ref=src, dst_ref=dst, send_sem=send, recv_sem=recv, device_id=(other,), device_id_type=MESH
    )


def arrived(view, sem):
    pltpu.make_async_copy(view, view, sem).wait()


DMA = pltpu.SemaphoreType.DMA


class Gather:
    def __init__(self, place, shard, full, strips, direct, scratch):
        self.p = place
        self.shard = shard
        self.full = full
        self.strips = strips
        self.direct = direct
        self.rows = 2 * shard.shape[0]
        self.half = full.shape[1] // 2
        self.stage, self.own, self.ls, self.zs, self.zr, self.xs, self.xr, self.ys, self.yr, self.hs, self.hr, self.ps, self.pr = scratch

    @staticmethod
    def scratch(rows, cols, dtype):
        return [pltpu.VMEM((2 * rows, cols), f32), pltpu.VMEM((2 * rows, cols), dtype), DMA((10,)), DMA((5,))] + [DMA((4,))] * 9

    def cut(self, c):
        return pl.ds(pl.multiple_of(c * self.half, 128), self.half)

    def at(self, chip, count=1):
        start = pl.multiple_of(chip * self.rows, 16)
        return self.full.at[pl.ds(start, count * self.rows), self.cut(self.p.c)]

    def loads(self):
        p = self.p
        rows = pl.ds(pl.multiple_of(p.c * (self.rows // 2), 8), self.rows // 2)
        pairs = []
        for n, (src, dst, width) in enumerate(self.strips):
            part, mine = self.shard.at[:, src : src + width], self.stage.at[rows, dst : dst + width]
            pairs.append(
                (
                    pltpu.make_async_copy(part, mine, self.ls.at[3 * n]),
                    remote(part, mine, self.ls.at[3 * n + 1], self.ls.at[3 * n + 2], p.partner),
                )
            )
        return pairs

    def keep(self):
        return pltpu.make_async_copy(self.own.at[:, self.cut(self.p.c)], self.at(self.p.chip), self.ls.at[9])

    def along_z(self, k):
        p = self.p
        zz = p.order[k]
        view = self.at(p.other(zz))
        src = view if k else self.own.at[:, self.cut(p.c)]
        up = remote(src, view, self.zs.at[k], self.zr.at[zz], p.up)
        if k == 0:
            down = remote(src, view, self.zs.at[4], self.zr.at[zz], p.down)
            return (p.z < 3, up), (p.z > 0, down)
        down = remote(src, view, self.zs.at[k], self.zr.at[zz], p.down)
        return ((p.z < 3) & (zz < p.z), up), ((p.z > 0) & (zz > p.z), down)

    def straight(self, k):
        p = self.p
        view = self.at(p.chip)
        return remote(self.own.at[:, self.cut(p.c)], view, self.zs.at[k], self.zr.at[p.z], p.order[k] * 8 + p.me % 8)

    def across(self, k):
        p = self.p
        zz = p.order[k]
        view = self.at(p.other(zz))
        src = view if k else self.own.at[:, self.cut(p.c)]
        return (
            remote(src, view, self.xs.at[zz], self.xr.at[zz], p.xn),
            remote(src, view, self.ys.at[zz], self.yr.at[zz], p.yn),
        )

    def onward(self, k):
        p = self.p
        zz = p.order[k]
        even = k % 2 == 0
        view = self.at(p.other(zz, dx=even, dy=not even))
        return remote(view, view, self.hs.at[zz], self.hr.at[zz], p.yn if even else p.xn)

    def to_partner(self, k):
        zz = self.p.order[k]
        view = self.at(4 * zz, 4)
        return remote(view, view, self.ps.at[zz], self.pr.at[zz], self.p.partner)

    def load(self):
        for local, pair in self.loads():
            local.start()
            pair.start()

    def begin(self):
        for local, pair in self.loads():
            local.wait()
            pair.wait_recv()
        self.own[...] = self.stage[...].astype(self.own.dtype)
        if self.direct:
            for k in (3, 2, 1):
                self.straight(k).start()
        else:
            for cond, copy in self.along_z(0):
                pl.when(cond)(copy.start)
        for copy in self.across(0):
            copy.start()
        self.keep().start()

    def column(self, k):
        zz = self.p.order[k]
        arrived(self.at(self.p.other(zz)), self.zr.at[zz])
        if not self.direct:
            for cond, copy in self.along_z(k):
                pl.when(cond)(copy.start)
        for copy in self.across(k):
            copy.start()

    def plane(self, k):
        p = self.p
        zz = p.order[k]
        even = k % 2 == 0
        arrived(self.at(p.other(zz, dx=even, dy=not even)), (self.xr if even else self.yr).at[zz])
        self.onward(k).start()

    def corner(self, k):
        p = self.p
        zz = p.order[k]
        even = k % 2 == 0
        arrived(self.at(p.other(zz, dx=not even, dy=even)), (self.yr if even else self.xr).at[zz])
        arrived(self.at(p.other(zz, True, True)), self.hr.at[zz])
        if k == 0:
            self.keep().wait()
        self.to_partner(k).start()

    def arrive(self, k):
        p = self.p
        zz = p.order[k]
        start = pl.multiple_of(4 * zz * self.rows, 16)
        arrived(self.full.at[pl.ds(start, 4 * self.rows), self.cut(1 - p.c)], self.pr.at[zz])

    def arrive_all(self):
        for k in range(4):
            self.arrive(k)

    def drain(self):
        for local, pair in self.loads():
            pair.wait_send()
        for k in range(4):
            if not self.direct:
                for cond, copy in self.along_z(k):
                    pl.when(cond)(copy.wait_send)
            elif k:
                self.straight(k).wait_send()
            for copy in self.across(k):
                copy.wait_send()
            self.onward(k).wait_send()
            self.to_partner(k).wait_send()

    def step(self, n):
        z = self.p.z
        inner = (z == 1) | (z == 2)
        if n == 0:
            self.begin()
        elif n == 1 or (self.direct and n < 4):
            self.column(n)
        elif n == 2:
            pl.when(inner)(lambda: self.column(2))
        elif n == 3:
            pl.when(inner)(lambda: self.column(3))
            pl.when(~inner)(lambda: self.column(2))
        elif n == 12:
            if not self.direct:
                pl.when(~inner)(lambda: self.column(3))
        elif n < 8:
            self.plane(n - 4)
        else:
            self.corner(n - 8)


GATHER_SCRATCH = 13


class Scatter:
    def __init__(self, place, grad, out, scratch):
        self.p = place
        self.grad = grad
        self.out = out
        self.rows = 2 * out.shape[0]
        self.half = out.shape[1] // 2
        self.bp, self.bh, self.bx, self.by, self.bz, self.fin = scratch[:6]
        self.ps, self.pr, self.hs, self.hr, self.xs, self.xr, self.ys, self.yr, self.zs, self.zr, self.fs = scratch[6:]

    @staticmethod
    def scratch(rows, cols, dtype):
        rows, half = 2 * rows, cols // 2
        bufs = [pltpu.VMEM((n * rows, half), dtype) for n in (16, 4, 4, 4, 5)]
        return bufs + [pltpu.VMEM((rows, half), f32)] + [DMA((4,))] * 9 + [DMA((5,)), DMA((3,))]

    def cut(self, c):
        return pl.ds(pl.multiple_of(c * self.half, 128), self.half)

    def span(self, n, count=1):
        return pl.ds(pl.multiple_of(n * self.rows, 16), count * self.rows)

    def at(self, chip):
        return self.grad.at[self.span(chip), self.cut(self.p.c)]

    def slot(self, buf, n):
        return buf.at[self.span(n)]

    def add(self, view, *terms):
        total = view[...]
        for term in terms:
            total = total + term[...]
        view[...] = total

    def to_partner(self, zz):
        p = self.p
        src = self.grad.at[self.span(4 * zz, 4), self.cut(1 - p.c)]
        return remote(src, self.bp.at[self.span(4 * zz, 4)], self.ps.at[zz], self.pr.at[zz], p.partner)

    def corner(self, k):
        p = self.p
        zz = p.order[k]
        return remote(self.at(p.other(zz, True, True)), self.slot(self.bh, zz), self.hs.at[zz], self.hr.at[zz], p.xn if k % 2 else p.yn)

    def side(self, k, along_x):
        p = self.p
        zz = p.order[k]
        src = self.at(p.other(zz, dx=along_x, dy=not along_x))
        if along_x:
            return remote(src, self.slot(self.bx, zz), self.xs.at[zz], self.xr.at[zz], p.xn)
        return remote(src, self.slot(self.by, zz), self.ys.at[zz], self.yr.at[zz], p.yn)

    def chain(self, k):
        p = self.p
        zz = p.order[k]
        src = self.at(p.other(zz))
        up = remote(src, self.slot(self.bz, zz), self.zs.at[k], self.zr.at[zz], p.up)
        place = jnp.where(zz == p.z - 1, 4, zz)
        down = remote(src, self.slot(self.bz, place), self.zs.at[k], self.zr.at[place], p.down)
        return (zz > p.z, up), (zz < p.z, down)

    def last(self):
        p = self.p
        rows = self.rows // 2
        part = lambda c: self.fin.at[pl.ds(pl.multiple_of(c * rows, 8), rows)]
        dst = self.out.at[:, self.cut(p.c)]
        return pltpu.make_async_copy(part(p.c), dst, self.fs.at[0]), remote(part(1 - p.c), dst, self.fs.at[1], self.fs.at[2], p.partner)

    def exchange(self, k):
        self.to_partner(self.p.order[k]).start()

    def step(self, n):
        if n == 8:
            self.total()
        else:
            (self.pair, self.side_on, self.column, self.relay)[n // 4](n % 4)

    def pair(self, k):
        p = self.p
        zz = p.order[k]
        self.to_partner(zz).wait_recv()

        @pl.loop(0, 4)
        def _(j):
            chip = 4 * zz + j
            self.add(self.at(chip), self.slot(self.bp, chip))

        self.corner(k).start()
        self.side(k, along_x=k % 2 == 1).start()

    def side_on(self, k):
        p = self.p
        zz = p.order[k]
        even = k % 2 == 0
        self.corner(k).wait_recv()
        self.add(self.at(p.other(zz, dx=even, dy=not even)), self.slot(self.bh, zz))
        self.side(k, along_x=even).start()

    def gathered(self, k):
        zz = self.p.order[k]
        self.side(k, True).wait_recv()
        self.side(k, False).wait_recv()
        self.add(self.at(self.p.other(zz)), self.slot(self.bx, zz), self.slot(self.by, zz))

    def column(self, k):
        p = self.p
        zz = p.order[k]
        self.gathered(k)
        ends = (p.z == 0) | (p.z == 3)
        for cond, copy in self.chain(k):
            pl.when(cond & ends)(copy.start)

    def relay(self, k):
        p = self.p
        zz = p.order[k]

        @pl.when((p.z == 1) | (p.z == 2))
        def _():
            arrived(self.slot(self.bz, zz), self.zr.at[zz])
            self.add(self.at(p.other(zz)), self.slot(self.bz, zz))
            for cond, copy in self.chain(k):
                pl.when(cond)(copy.start)

    def total(self):
        p = self.p
        self.gathered(0)
        self.fin[...] = self.at(p.chip)[...].astype(f32)

        @pl.when(p.z > 0)
        def _():
            arrived(self.slot(self.bz, p.z), self.zr.at[p.z])
            self.fin[...] += self.slot(self.bz, p.z)[...].astype(f32)

        @pl.when(p.z < 3)
        def _():
            arrived(self.slot(self.bz, 4), self.zr.at[4])
            self.fin[...] += self.slot(self.bz, 4)[...].astype(f32)

        for copy in self.last():
            copy.start()

    def finish(self):
        p = self.p
        for k in range(4):
            self.to_partner(p.order[k]).wait_send()
            self.corner(k).wait_send()
            self.side(k, True).wait_send()
            self.side(k, False).wait_send()
            if k:
                for cond, copy in self.chain(k):
                    pl.when(cond)(copy.wait_send)
        local, pair = self.last()
        local.wait()
        pair.wait_send()
        arrived(self.out.at[:, self.cut(1 - p.c)], self.fs.at[2])


SCATTER_SCRATCH = 17


FRONT_PLAN = (
    (0,), (96, 48, 16, 64), (2, 3, 12, 4, 98, 100), (1, 97, 99, 108, 20, 50, 52), (18, 49, 51, 60), (19, 28, 32, 6, 68), (7, 102, 17, 66),
    (8, 104, 5, 54, 101, 103, 65, 34, 22, 24, 35, 44, 33, 56, 36, 53, 11, 55, 67, 23, 10, 9, 105, 107, 72, 76, 106), (), (21, 38), (), (),
    (58,), (57, 80, 59, 70), (69,), (), (26, 25, 27), (37, 39, 40, 81, 82), (), (84,), (71,), (42,), (73,), (41, 43, 83), (), (), (74,), (),
    (), (92,), (85,), (), (), (75, 86), (), (), (88,), (), (), (), (), (), (87, 89), (), (), (90,), (91,), (), (), (), (),
)
BACK_PLAN = (
    (), (), (), (83,), (82,), (), (81,), (), (87, 80), (86,), (), (), (), (), (85,), (), (91,), (), (), (84,), (90,), (95,), (), (89, 94),
    (93, 67), (66,), (), (65, 64, 51, 50, 49), (88, 71, 70, 48), (), (), (), (69,), (68, 3, 2, 1), (55, 0), (54, 53), (), (), (75,),
    (74, 52, 19, 18, 17), (16,), (79, 73, 7, 6, 5), (59, 58, 4), (78,), (57, 23), (22, 21), (77, 35, 34), (63, 10, 20, 62, 33, 32), (11,),
    (), (61, 15, 14, 9, 27, 26, 25, 39, 38), (72, 37, 36), (13, 31, 30, 43, 56, 42), (47, 41), (29, 46), (), (8, 45), (), (24, 40),
)


class Steps:
    def __init__(self, plan, jobs):
        self.plan, self.jobs, self.next = plan, jobs, 0

    def take(self):
        if not self.jobs:
            return ()
        self.next += 1
        return self.plan[self.next - 1]

    def do(self, codes):
        for code in codes:
            self.jobs[code // 16].step(code % 16)

    def slot(self):
        self.do(self.take())

    def loop(self, count, body, inner=1):
        plan = [[self.take() for _ in range(inner)] for _ in range(count)]

        @pl.loop(0, count)
        def _(it):
            def at(sub):
                for n in range(count):
                    if plan[n][sub]:
                        pl.when(it == n)(functools.partial(self.do, plan[n][sub]))

            at(0)
            if inner > 1:
                body(it, at)
            else:
                body(it)


def tile(t, size):
    return pl.ds(pl.multiple_of(t * size, size), size)


def cols_of(n, width):
    return pl.ds(pl.multiple_of(n * width, 128), width)


def rotation(seg):
    counts = [jnp.sum(jnp.where(seg == u, 1.0, 0.0), 1, keepdims=True) for u in range(3)]
    start = counts[0] + counts[1] + counts[2]
    start = jnp.where(counts[2] == HALF, counts[0] + counts[1], start)
    start = jnp.where(counts[1] == HALF, counts[0], start)
    return jnp.where(counts[0] == HALF, 0.0, start)


def turn(t, start, back):
    row = (lax.broadcasted_iota(jnp.int32, (ROWS, TOK), 0) + t * ROWS).astype(f32)
    col = lax.broadcasted_iota(jnp.int32, (ROWS, TOK), 1).astype(f32)
    source = row - start if back else row + start
    source = jnp.where(source < 0.0, source + TOK, jnp.where(source >= TOK, source - TOK, source))
    return jnp.where(source == col, 1.0, 0.0).astype(bf16)


def column_of(row):
    return jnp.broadcast_to(row, (128, row.shape[1])).T


def attend_pair(q, k, v, bias, prob_ref):
    q = q * jnp.bfloat16(0.125)
    outs = []
    for h in range(2):
        qh = jnp.where(lane_half(h, q.shape), q, jnp.bfloat16(0))
        scores = dot(qh, k, NT) + bias
        scores = jnp.exp(scores - jnp.max(scores, 1, keepdims=True))
        probs = (scores * (1.0 / jnp.sum(scores, 1, keepdims=True))).astype(bf16)
        prob_ref[h] = probs
        outs.append(dot(probs, v, NN))
    return jnp.where(lane_half(0, outs[0].shape), outs[0], outs[1]).astype(bf16)


def attend_pair_back(q, k, v, grad, ctx, prob_ref):
    product = grad.astype(f32) * ctx.astype(f32)
    dq, dk, dv = [], [], []
    for h in range(2):
        lanes = lane_half(h, grad.shape)
        grad_h = jnp.where(lanes, grad, jnp.bfloat16(0))
        row_dot = jnp.sum(jnp.where(lanes, product, 0.0), 1, keepdims=True)
        probs = prob_ref[h]
        ds = (probs.astype(f32) * (dot(grad_h, v, NT) - row_dot)).astype(bf16)
        dq.append(dot(ds, k, NN))
        dk.append(dot(ds, q, TN))
        dv.append(dot(probs, grad, TN))
    lanes = lane_half(0, grad.shape)
    return [
        (jnp.where(lanes, dq[0], dq[1]) * 0.125).astype(bf16),
        (jnp.where(lanes, dk[0], dk[1]) * 0.125).astype(bf16),
        jnp.where(lanes, dv[0], dv[1]).astype(bf16),
    ]


def bias_row(small_ref, first, bias_len):
    total = jnp.zeros((8, 1024), f32)
    lanes = lax.broadcasted_iota(jnp.int32, (8, 256), 1)
    for d in range(first // bias_len, (first + D - 1) // bias_len + 1):
        piece = jnp.where(lanes < bias_len, jnp.broadcast_to(small_ref[8 * d : 8 * d + 1, :], (8, 256)), 0.0)
        piece = jnp.concatenate([piece, jnp.zeros((8, 768), f32)], axis=1)
        shift = (bias_len * d - first) % 1024
        total = total + (pltpu.roll(piece, shift, 1) if shift else piece)
    return total[:1, :D]


PAIRS = H // 2


def normed_of(residual):
    center = residual - jnp.mean(residual, 1, keepdims=True)
    scale = lax.rsqrt(jnp.mean(center * center, 1, keepdims=True) + EPSILON)
    return center * scale, scale


def norm_back(grad, gain, unit, scale):
    grad = grad * gain
    return scale * (grad - jnp.mean(grad, 1, keepdims=True) - unit * jnp.mean(grad * unit, 1, keepdims=True))


PAIRS = H // 2
THIRD = D // 3
PAIR = 2 * HD


def entry_cols(j, matrix, feat, pos, cot, entry, low, cot_out):
    cols = cols_of(j, 256)
    value = dot(matrix[...], feat[:, cols], NN) + dot(matrix[...], pos[:, cols], NN)
    entry[:, cols] = value
    low[:, cols] = value.astype(bf16)
    cot_out[:, cols] = dot(matrix[...], cot[:, cols], NN).astype(bf16)


def mask_half(h, matrix, stack, mask):
    matrix = matrix[h * HALF : (h + 1) * HALF, :]
    by_row = dot(stack, matrix, NT)
    by_col = dot(matrix, stack, NT)
    rows = lax.broadcasted_iota(jnp.int32, (HALF, HALF), 0)
    cols = lax.broadcasted_iota(jnp.int32, (HALF, HALF), 1)
    allowed = (by_col[:, 1:2] == by_row[1:2, :]) & ((by_row[0:1, :] > 0.0) | (rows == cols))
    mask[h] = jnp.where(allowed, 0.0, MASKED)


def stack_of(valid, seg):
    row = lax.broadcasted_iota(jnp.int32, (8, TOK), 0)
    both = jnp.where(row == 0, valid.astype(f32), jnp.where(row == 1, seg.astype(f32), 0.0))
    return both.astype(bf16)


def gain_row(small, which, gain_len):
    ranks = small.shape[0] // 8
    row = lax.broadcasted_iota(jnp.int32, (ranks, 8 * ranks), 0)
    col = lax.broadcasted_iota(jnp.int32, (ranks, 8 * ranks), 1)
    pick = jnp.where(col == 8 * row + which, 1.0, 0.0).astype(bf16)
    values = dot(pick, small[...].astype(bf16), NN).astype(bf16)
    lane = lax.broadcasted_iota(jnp.int32, (256, D), 1).astype(f32)
    home = jnp.floor((lane + 0.5) * (1.0 / gain_len))
    spot = lax.broadcasted_iota(jnp.int32, (256, D), 0).astype(f32)
    spread = dot(values, jnp.where(lane - home * gain_len == spot, 1.0, 0.0).astype(bf16), NN)
    owner = lax.broadcasted_iota(jnp.int32, (ranks, D), 0).astype(f32)
    return jnp.sum(jnp.where(home[:ranks] == owner, spread, 0.0), 0, keepdims=True)


SLOPE_COLS = 768
WIDE = 512
STRIPS = [[(which * D + g * THIRD, which * THIRD, THIRD) for which in range(3)] for g in range(3)]


def front_kernel(linked, bias_len, gain_len, *refs):
    n = 7
    if linked:
        (bias_in, gains_in, qkv_w, proj_w, expand_w, reduce_w), refs = refs[:6], refs[6:]
    else:
        (bias_in, gains_in, *weights_in), refs = refs[:8], refs[8:]
    (feat_in, pos_in, cot_in, seg_ref, valid_ref), refs = refs[:5], refs[5:]
    if linked:
        weights_out, refs = refs[:6], refs[6:]
    outs, refs = refs[:10], refs[10:]
    low_out, qkv_out, ctx_out, prob_out, unit_out, nlow_out, act_out, slope_out, gs_out, layer_out = outs
    (gains, dvec), refs = refs[:2], refs[2:]
    (feat, pos, cot_raw, entry, low, cot, mask, small, w_a, w_b, w_c, w_p, w_e, w_r, bias), refs = refs[:15], refs[15:]
    (qkv, ctx, probs, act, slope, total, unit_stage, ins, sent, psem, ssem, usem, rsem), refs = refs[:13], refs[13:]
    loads = [pltpu.make_async_copy(a, b, ins.at[i]) for i, (a, b) in enumerate(((feat_in, feat), (pos_in, pos), (cot_in, cot_raw)))]
    thirds = [w_a, w_b, w_c]
    homes = [*thirds, w_p, w_e, w_r]
    nlow, layer = feat, pos
    counted = iter(range(16))
    store = lambda a, b: pltpu.make_async_copy(a, b, sent.at[next(counted)])
    store_low, store_ctx, store_nlow = store(low, low_out), store(ctx, ctx_out), store(nlow, nlow_out)
    store_act, store_layer = store(act, act_out), store(layer, layer_out)
    store_qkv = [store(qkv.at[g], qkv_out.at[g]) for g in range(3)]
    store_w = [store(a, b) for a, b in zip(homes, weights_out)] if linked else []
    for copy in loads:
        copy.start()
    jobs = []
    if linked:
        (shard, *refs) = refs
        place = Place()
        shard[...] = jnp.zeros_like(shard)
        shard[0:1, :bias_len] = bias_in[...].astype(bf16).astype(f32)
        shard[1:3, :gain_len] = gains_in[...].astype(bf16).astype(f32)
        place.greet()
        sources = [(qkv_w, w, STRIPS[g], True) for g, w in enumerate(thirds)]
        sources += [(a, b, [(0, 0, b.shape[1])], b is w_p or b is small) for a, b in ((proj_w, w_p), (expand_w, w_e), (reduce_w, w_r), (shard, small))]
        jobs = [Gather(place, *args, refs[i * GATHER_SCRATCH : (i + 1) * GATHER_SCRATCH]) for i, args in enumerate(sources)]
        for i in (0, 6, 1, 2, 3, 4, 5):
            jobs[i].load()
    else:
        for i, (a, b) in enumerate(zip(weights_in, homes)):
            copy = pltpu.make_async_copy(a, b, sent.at[9 + i])
            copy.start()
            copy.wait()
    steps = Steps(FRONT_PLAN, jobs)

    def ready(i):
        steps.slot()
        if linked:
            jobs[i].arrive_all()
            if i < 6:
                store_w[i].start()

    steps.slot()
    for copy in loads:
        copy.wait()
    seg = seg_ref[...]
    start = rotation(seg)
    stack = stack_of(valid_ref[...], seg)
    matrix = act.at[:, :TOK]
    valid = column_of(valid_ref[...].astype(f32))[:, :1].astype(bf16)
    feat[...] = feat[...] * valid
    pos[...] = pos[...] * valid

    steps.slot()

    @pl.loop(0, 4)
    def _(t):
        matrix[tile(t, ROWS), :] = turn(t, start, False)

    steps.loop(3, lambda j: entry_cols(j, matrix, feat, pos, cot_raw, entry, low, cot))
    store_low.start()
    for h in range(2):
        steps.slot()
        mask_half(h, matrix, stack, mask)
    dvec[...] = jnp.zeros_like(dvec)
    ready(6)
    ready(0)
    if linked:
        for block in range(2):
            bias[0:1, block * D : (block + 1) * D] = bias_row(small, block * D, bias_len)
    else:
        bias[0:1, :] = bias_in[...]
        gains[0:2, :] = gains_in[...]

    def prob_store(it):
        return pltpu.make_async_copy(probs.at[it % 2], prob_out.at[pl.ds(2 * it, 2)], psem.at[it % 2])

    for g in range(3):
        if g:
            ready(g)

        for which in range(3):
            steps.slot()
            cols = slice(which * THIRD, (which + 1) * THIRD)
            value = dot(low[...], thirds[g][:, cols], NN)
            if which != 1:
                first = (which // 2) * D + g * THIRD
                value = value + bias[0:1, first : first + THIRD]
            qkv[g, :, cols] = value.astype(bf16)
        store_qkv[g].start()

        def attention(i):
            it = 4 * g + i
            pair, half = i // 2, i % 2
            rows = tile(half, HALF)
            cut = lambda which: qkv[g, rows, cols_of(2 * which + pair, PAIR)]
            if g:
                prob_store(it - 2).wait()
            else:
                pl.when(it >= 2)(lambda: prob_store(it - 2).wait())
            ctx[rows, cols_of(2 * g + pair, PAIR)] = attend_pair(cut(0), cut(1), cut(2), mask[half], probs.at[it % 2])
            prob_store(it).start()

        steps.loop(4, attention)
    store_ctx.start()
    if linked:
        for block in range(2, 10):
            bias[0:1, block * D : (block + 1) * D] = bias_row(small, block * D, bias_len)
        for which in range(2):
            gains[which : which + 1, :] = gain_row(small, 1 + which, gain_len)
    b_2 = bias[0:1, 3 * D + FF : 4 * D + FF]
    c_1, c_2 = bias[0:1, 4 * D + FF : 5 * D + FF], bias[0:1, 5 * D + FF : 6 * D + FF]
    g_1, g_2 = gains[0:1, :], gains[1:2, :]
    ready(3)

    def slope_store(j):
        return pltpu.make_async_copy(slope.at[j % 2], slope_out.at[:, cols_of(j, WIDE)], ssem.at[j % 2])

    def unit_store(t):
        return pltpu.make_async_copy(unit_stage.at[t % 2], unit_out.at[tile(t, ROWS)], usem.at[t % 2])

    def first_norm(t):
        rows = tile(t, ROWS)
        unit, scale = normed_of(entry[rows, :])
        pl.when(t >= 2)(lambda: unit_store(t - 2).wait())
        unit_stage[t % 2, :, :D] = unit
        unit_stage[t % 2, :, D:] = jnp.broadcast_to(scale, (ROWS, 128))
        unit_store(t).start()
        normed = unit * g_1 + c_1
        nlow[rows, :] = normed.astype(bf16)
        total[rows, :] = normed + b_2

    def expand(j):
        cols = cols_of(j, WIDE)
        pre = dot(nlow[...], w_e[:, cols], NN) + bias[0:1, pl.ds(pl.multiple_of(3 * D + j * WIDE, 128), WIDE)]
        cdf = 0.5 + 0.5 * lax.erf(pre * 0.7071067811865476)
        act[:, cols] = (pre * cdf).astype(bf16)
        pl.when(j >= 2)(lambda: slope_store(j - 2).wait())
        slope[j % 2] = (cdf + pre * (0.3989422804014327 * jnp.exp(-0.5 * pre * pre))).astype(bf16)
        slope_store(j).start()

    for j in range(3):
        steps.slot()
        cols = slice(j * 256, (j + 1) * 256)
        entry[:, cols] = entry[:, cols] + dot(ctx[...], w_p[:, cols], NN) + bias[0:1, 2 * D + j * 256 : 2 * D + (j + 1) * 256]
    steps.loop(4, first_norm)
    ready(4)
    steps.loop(FF // WIDE, expand)
    store_nlow.start()
    store_act.start()
    for k in range(4):
        if linked:
            steps.slot()
            jobs[5].arrive(k)
            zz = place.order[k]
        else:
            zz = k

        if linked and k == 3:
            store_w[5].start()
        for j in range(3):
            cols = slice(j * 256, (j + 1) * 256)
            total[:, cols] += dot(act[:, cols_of(zz, D)], w_r[cols_of(zz, D), cols], NN)

    def row_store(t):
        return pltpu.make_async_copy(total.at[tile(t, ROWS)], gs_out.at[tile(t, ROWS)], rsem.at[t])

    @pl.loop(0, 4)
    def _(t):
        rows = tile(t, ROWS)
        unit, scale = normed_of(total[rows, :])
        layer[rows, :] = (unit * g_2 + c_2).astype(bf16)
        grad = cot[rows, :].astype(f32)
        dvec[0:1, :] += jnp.sum(grad * unit, 0, keepdims=True)
        dvec[1:2, :] += jnp.sum(grad, 0, keepdims=True)
        value = norm_back(grad, g_2, unit, scale)
        total[rows, :] = value
        dvec[2:3, :] += jnp.sum(value.astype(bf16).astype(f32), 0, keepdims=True)
        row_store(t).start()

    store_layer.start()
    prob_store(10).wait()
    prob_store(11).wait()
    slope_store(FF // WIDE - 2).wait()
    slope_store(FF // WIDE - 1).wait()
    unit_store(2).wait()
    unit_store(3).wait()
    if linked:
        for job in jobs:
            job.drain()
    for copy in (store_low, store_ctx, store_nlow, store_act, store_layer, *store_qkv, *store_w):
        copy.wait()
    for t in range(4):
        row_store(t).wait()


def front(linked, bias_len, gain_len, bias, gains, weights, features, pos_conv, cotangent, segments, valid):
    wide = [S((D, D), bf16)] * 4 + [S((D, FF), bf16), S((FF, D), bf16)]
    outs = list(wide) if linked else []
    outs += [
        S((TOK, D), bf16), S((3, TOK, D), bf16), S((TOK, D), bf16), S((2 * H, HALF, HALF), bf16), S((TOK, D + 128), f32),
        S((TOK, D), bf16), S((TOK, FF), bf16), S((TOK, FF), bf16), S((TOK, D), f32), S((TOK, D), bf16),
    ]
    hbm = len(outs)
    outs += [S((8, D), f32), S((8, D), f32)]
    half = pltpu.VMEM((TOK, D), bf16)
    scratch = [half, half, half, pltpu.VMEM((TOK, D), f32), half, half, pltpu.VMEM((2, HALF, HALF), f32), pltpu.VMEM((256, 256), f32)]
    scratch += [pltpu.VMEM(w.shape, bf16) for w in wide] + [pltpu.VMEM((1, 6 * D + FF), f32)]
    scratch += [
        pltpu.VMEM((3, TOK, D), bf16), half, pltpu.VMEM((2, 2, HALF, HALF), bf16), pltpu.VMEM((TOK, FF), bf16),
        pltpu.VMEM((2, TOK, WIDE), bf16), pltpu.VMEM((TOK, D), f32), pltpu.VMEM((2, ROWS, D + 128), f32),
        DMA((3,)), DMA((16,)), DMA((2,)), DMA((2,)), DMA((2,)), DMA((4,)),
    ]
    more = {}
    if linked:
        more = dict(collective_id=0, has_side_effects=True)
        scratch += [pltpu.VMEM((8, 256), f32)]
        for w in wide:
            scratch += Gather.scratch(w.shape[0] // 32, w.shape[1], bf16)
        scratch += Gather.scratch(8, 256, f32)
    return pl.pallas_call(
        functools.partial(front_kernel, linked, bias_len, gain_len),
        in_specs=[IN_VMEM] * 2 + [IN_HBM] * (len(weights) + 3) + [IN_VMEM] * 2,
        out_specs=[IN_HBM] * hbm + [IN_VMEM] * 2,
        out_shape=outs,
        scratch_shapes=scratch,
        compiler_params=params(**more),
        name="front",
    )(bias, gains, *weights, features, pos_conv, cotangent, segments, valid)


class Exchange:
    def __init__(self, place, total, slots, send, recv):
        z = place.z
        self.others = (place.partner, place.xn, place.yn, place.me + 8 - 16 * (z % 2), place.me + 16 - 32 * (z // 2))
        self.total, self.slots, self.send, self.recv = total, slots, send, recv

    def copy(self, n):
        return remote(self.slots.at[n], self.slots.at[5 + n], self.send.at[n], self.recv.at[n], self.others[n])

    def begin(self, n):
        self.slots[n] = self.total[...]
        self.copy(n).start()

    def end(self, n):
        self.copy(n).wait()
        self.total[...] += self.slots[5 + n]


VECTOR_ROWS = 72


def put(vector, row, value):
    for i in range(value.shape[1] // 128):
        vector[row + i : row + i + 1, :] = value[:, 128 * i : 128 * (i + 1)]


def back_kernel(linked, *refs):
    weights_in, refs = refs[:6], refs[6:]
    (low_in, qkv_in, ctx_in, prob_in, unit_in, nlow_in, act_in, slope_in, gs_in, layer_in), refs = refs[:10], refs[10:]
    (gains, dvec, seg_ref, valid_ref), refs = refs[:4], refs[4:]
    names = 6
    if linked:
        sums, refs = refs[:names], refs[names:]
    else:
        parts_out, refs = refs[:names], refs[names:]
    (input_out, layer_out, vector), refs = refs[:3], refs[3:]
    (big, w_e, w_r, hold_r, w_p, gs, grad, branch, ctx, low, probs, slope, unit, hold_p, hold_a, hold_b, hold_c, gain, db1), refs = refs[:19], refs[19:]
    (ins, psem, ssem, usem), refs = refs[:4], refs[4:]
    holds = [hold_a, hold_b, hold_c, hold_p, w_e, hold_r]
    counted = iter(range(24))
    copy = lambda a, b: pltpu.make_async_copy(a, b, ins.at[next(counted)])
    load_gs, load_act, load_wr, load_we = copy(gs_in, gs), copy(act_in, big), copy(weights_in[5], w_r), copy(weights_in[4], w_e)
    load_wp, load_nlow, load_ctx = copy(weights_in[3], w_p), copy(nlow_in, low), copy(ctx_in, ctx)
    load_low, load_layer = copy(low_in, low), copy(layer_in, branch)
    load_qkv = [copy(qkv_in.at[g], w_r.at[g * TOK : (g + 1) * TOK]) for g in range(3)]
    load_w = [copy(weights_in[g], hold_r.at[g * D : (g + 1) * D]) for g in range(3)]
    store_layer, store_input = copy(grad, layer_out), copy(ctx, input_out)
    load_gs.start()
    load_act.start()

    def slope_load(t, k):
        return pltpu.make_async_copy(slope_in.at[tile(t, ROWS), slice(k * SLOPE_COLS, (k + 1) * SLOPE_COLS)], slope.at[k % 2], ssem.at[k % 2])

    def unit_load(t):
        return pltpu.make_async_copy(unit_in.at[tile(t, ROWS)], unit.at[t % 2], usem.at[t % 2])

    def prob_load(it):
        return pltpu.make_async_copy(prob_in.at[pl.ds(2 * it, 2)], probs.at[it % 2], psem.at[it % 2])

    jobs = []
    sender = 0
    if linked:
        (slots, send, recv), refs = refs[:3], refs[3:]
        place = Place()
        sender = 1 - place.c
        jobs = [Scatter(place, holds[i], sums[i], refs[i * SCATTER_SCRATCH : (i + 1) * SCATTER_SCRATCH]) for i in range(names)]
        swap = Exchange(place, vector, slots, send, recv)
        place.greet()
    steps = Steps(BACK_PLAN, jobs)

    def exchange(i):
        if linked:
            for k in (3, 2, 1, 0):
                jobs[i].exchange(k)

    load_gs.wait()

    @pl.loop(0, 4)
    def _(t):
        rows = tile(t, ROWS)
        grad[rows, :] = gs[rows, :].astype(bf16)

    load_act.wait()
    for load in (load_wr, load_we, load_wp, load_nlow, load_ctx):
        load.start()
    slope_load(0, 0).start()
    slope_load(0, 1).start()
    unit_load(0).start()
    prob_load(0).start()
    for k in (3, 2, 1, 0):
        zz = place.order[k] if linked else k
        steps.slot()

        hold_r[tile(zz, D), :] = dot(big[:, cols_of(zz, D)], grad[...], TN).astype(bf16)

        if linked:
            jobs[5].exchange(k)
    for load in (load_wr, load_we, load_wp):
        load.wait()
    gain[...] = jnp.zeros_like(gain)
    db1[...] = jnp.zeros_like(db1)
    g_1 = gains[0:1, :]

    def ffn_back(t, at):
        rows = tile(t, ROWS)
        pl.when(t < 3)(lambda: unit_load(t + 1).start())
        gffn = grad[rows, :]
        total = gs[rows, :]
        for k in range(FF // SLOPE_COLS):
            if k:
                at(k)
            cols = slice(k * SLOPE_COLS, (k + 1) * SLOPE_COLS)
            slope_load(t, k).wait()
            gpre = (dot(gffn, w_r[cols, :], NT) * slope[k % 2].astype(f32)).astype(bf16)
            if k < 2:
                slope_load(t, k + 2).start()
            else:
                pl.when(t < 3)(lambda: slope_load(t + 1, k - 2).start())
            big[rows, cols] = gpre
            db1[0:1, cols] += jnp.sum(gpre.astype(f32), 0, keepdims=True)
            total = total + dot(gpre, w_e[:, cols], NT)
        unit_load(t).wait()
        unit_1, scale_1 = unit[t % 2, :, :D], unit[t % 2, :, D : D + 1]
        gain[0:1, :] += jnp.sum(total * unit_1, 0, keepdims=True)
        gain[1:2, :] += jnp.sum(total, 0, keepdims=True)
        first = norm_back(total, g_1, unit_1, scale_1)
        gs[rows, :] = first
        lowered = first.astype(bf16)
        branch[rows, :] = lowered
        gain[2:3, :] += jnp.sum(lowered.astype(f32), 0, keepdims=True)
        grad[rows, :] = dot(lowered, w_p[...], NT).astype(bf16)

    steps.loop(4, ffn_back, 4)
    for load in load_qkv:
        load.start()
    load_nlow.wait()

    def expand_grad(j):
        cols = pl.ds(pl.multiple_of(((sender + j // 2) % 2) * (FF // 2) + (j % 2) * D, 256), D)
        w_e[:, cols] = dot(low[...], big[:, cols], TN).astype(bf16)

    steps.loop(2, expand_grad)
    exchange(4)
    steps.loop(2, lambda j: expand_grad(j + 2))
    load_low.start()
    load_ctx.wait()

    def square_grad(hold, left, right, at):
        def half(j):
            first = ((sender + j) % 2) * (D // 2)
            cols = pl.ds(pl.multiple_of(first, 128), D // 2)
            source = pl.ds(pl.multiple_of(at + first, 128), D // 2)
            hold[:, cols] = dot(left[...], right[:, source], TN).astype(bf16)

        return half

    square = square_grad(hold_p, ctx, branch, 0)
    steps.slot()
    square(0)
    exchange(3)
    steps.slot()
    square(1)
    load_layer.start()
    for load in load_qkv:
        load.wait()
    load_low.wait()
    for g in range(3):

        def attention(i):
            it = 4 * g + i
            pair, half = i // 2, i % 2
            rows = tile(half, HALF)
            cut = lambda which: w_r[pl.ds(pl.multiple_of(g * TOK + half * HALF, HALF), HALF), cols_of(2 * which + pair, PAIR)]
            if g < 2:
                prob_load(it + 1).start()
            else:
                pl.when(i < 3)(lambda: prob_load(it + 1).start())
            prob_load(it).wait()
            own = cols_of(2 * g + pair, PAIR)
            three = attend_pair_back(cut(0), cut(1), cut(2), grad[rows, own], ctx[rows, own], probs.at[it % 2])
            for which, value in enumerate(three):
                big[rows, cols_of(6 * g + 2 * which + pair, PAIR)] = value

        steps.loop(4, attention)
        square = square_grad(holds[g], low, big, g * D)
        steps.slot()
        square(0)
        exchange(g)
        steps.slot()
        square(1)
    for g in range(3):
        for which, row in ((0, 2 * g), (2, 6 + 2 * g)):
            at = g * D + which * THIRD
            put(vector, row, jnp.sum(big[:, at : at + THIRD].astype(f32), 0, keepdims=True))
    put(vector, 12, gain[2:3, :])
    put(vector, 18, db1[...])
    put(vector, 42, dvec[2:3, :])
    put(vector, 48, gain[1:2, :])
    put(vector, 54, dvec[1:2, :])
    put(vector, 60, gain[0:1, :])
    put(vector, 66, dvec[0:1, :])
    if linked:
        swap.begin(0)
    start = rotation(seg_ref[...])
    load_layer.wait()

    def layer_back(t):
        rows = tile(t, ROWS)
        grad[rows, :] = dot(turn(t, start, True), branch[...], NN).astype(bf16)

    steps.loop(4, layer_back)
    store_layer.start()
    steps.slot()
    if linked:
        swap.end(0)
        swap.begin(1)
        steps.slot()
        jobs[5].finish()
    else:
        outs = [pltpu.make_async_copy(a, b, ins.at[18 + i]) for i, (a, b) in enumerate(zip(holds, parts_out))]
        for store in outs:
            store.start()
        for store in outs:
            store.wait()
    for load in load_w:
        load.start()
    for load in load_w:
        load.wait()

    def swapped(n):
        swap.end(n)
        swap.begin(n + 1)

    def input_grad(t):
        if linked:
            pl.when(t == 2)(lambda: swapped(1))
        rows = tile(t, ROWS)
        value = gs[rows, :]
        for g in range(3):
            value = value + dot(big[rows, g * D : (g + 1) * D], hold_r[g * D : (g + 1) * D, :], NT)
        big[rows, 3 * D : 4 * D] = value.astype(bf16)

    steps.loop(4, input_grad)

    def input_back(t):
        if linked:
            pl.when(t == 1)(lambda: swapped(2))
        rows = tile(t, ROWS)
        ctx[rows, :] = dot(turn(t, start, True), big[:, 3 * D : 4 * D], NN).astype(bf16)

    steps.loop(4, input_back)
    ctx[...] = ctx[...] * column_of(valid_ref[...].astype(f32))[:, :1].astype(bf16)
    store_input.start()
    if linked:
        swapped(3)
        steps.slot()
        swap.end(4)
        for job in jobs[:5]:
            job.finish()
    store_layer.wait()
    store_input.wait()


def back(linked, weights, *arrays):
    wide = [(D, D)] * 4 + [(D, FF), (FF, D)]
    outs = [S((r // 32, c), f32) for r, c in wide] if linked else [S(s, bf16) for s in wide]
    outs += [S((TOK, D), bf16), S((TOK, D), bf16), S((VECTOR_ROWS, 128), f32)]
    half = pltpu.VMEM((TOK, D), bf16)
    square = pltpu.VMEM((D, D), bf16)
    scratch = [
        pltpu.VMEM((TOK, FF), bf16), pltpu.VMEM((D, FF), bf16), pltpu.VMEM((FF, D), bf16), pltpu.VMEM((FF, D), bf16), square,
        pltpu.VMEM((TOK, D), f32), half, half, half, half, pltpu.VMEM((2, 2, HALF, HALF), bf16), pltpu.VMEM((2, ROWS, SLOPE_COLS), bf16),
        pltpu.VMEM((2, ROWS, D + 128), f32), square, square, square, square, pltpu.VMEM((8, D), f32), pltpu.VMEM((1, FF), f32),
        DMA((24,)), DMA((2,)), DMA((2,)), DMA((2,)),
    ]
    more = {}
    if linked:
        more = dict(collective_id=1, has_side_effects=True)
        scratch += [pltpu.VMEM((10, VECTOR_ROWS, 128), f32), DMA((5,)), DMA((5,))]
        for r, c in wide:
            scratch += Scatter.scratch(r // 32, c, bf16)
    return pl.pallas_call(
        functools.partial(back_kernel, linked),
        in_specs=[IN_HBM] * 16 + [IN_VMEM] * 4,
        out_specs=[IN_VMEM if linked else IN_HBM] * 6 + [IN_HBM] * 2 + [IN_VMEM],
        out_shape=outs,
        scratch_shapes=scratch,
        compiler_params=params(**more),
        name="back",
    )(*weights, *arrays)


def update_kernel(rates, small_rate, *refs):
    passed, vector, little, refs = refs[:2], refs[2], refs[3:9], refs[9:]
    thirds, refs = refs[:3], refs[3:]
    count = len(rates)
    ins, outs, sent, held, sems = refs[: 4 * count - 1], refs[4 * count - 1 : -5], refs[-5:-3], refs[-3:-1], refs[-1]
    outs, small = outs[: 4 * count], outs[4 * count :]
    loads = [pltpu.make_async_copy(a, b, sems.at[i]) for i, (a, b) in enumerate(zip(passed, held))]
    copies = [pltpu.make_async_copy(a, b, sems.at[2 + i]) for i, (a, b) in enumerate(zip(held, sent))]
    for load in loads:
        load.start()
    for load, copy in zip(loads, copies):
        load.wait()
        copy.start()
    me = lax.axis_index("dp")
    rows = [vector[n : n + 1, :] for n in range(VECTOR_ROWS)]
    sides = [jnp.concatenate(rows[60 + 6 * n : 66 + 6 * n], axis=1) for n in range(2)] + [jnp.zeros((6, D), f32)]
    sums = [jnp.broadcast_to(jnp.concatenate(rows[:60], axis=1), (8, 6 * D + FF)), jnp.concatenate(sides, axis=0)]
    for n, total in enumerate(sums):
        w_ref, m_ref, a_ref = little[3 * n : 3 * n + 3]
        high, wide = w_ref.shape
        length = total.shape[1]
        grad = pltpu.roll(total, lax.rem(length - wide * me, length), 1)[:high, :wide]
        velocity = 0.5 * m_ref[...] + grad
        master = w_ref[...] - small_rate * (grad + 0.5 * velocity)
        for ref, value in zip(small[4 * n : 4 * n + 4], (grad, master, velocity, 0.5 * a_ref[...] + 0.5 * master)):
            ref[...] = value
    for i, rate in enumerate(rates):
        if i:
            w_ref, g_ref, m_ref, a_ref = ins[4 * i - 1 : 4 * i + 3]
            pieces = [(slice(None), g_ref[...])]
        else:
            w_ref, m_ref, a_ref = ins[:3]
            pieces = []
            for g in range(3):
                for which in range(3):
                    at = which * D + g * THIRD
                    pieces.append((slice(at, at + THIRD), thirds[g][:, which * THIRD : (which + 1) * THIRD]))
        for cols, grad in pieces:
            velocity = 0.5 * m_ref[:, cols] + grad
            master = w_ref[:, cols] - rate * (grad + 0.5 * velocity)
            for ref, value in zip(outs[4 * i : 4 * i + 4], (grad, master, velocity, 0.5 * a_ref[:, cols] + 0.5 * master)):
                ref[:, cols] = value
    for copy in copies:
        copy.wait()


def update(rates, small_rate, passed, vector, little, thirds, arrays):
    shapes = [arrays[0].shape] * 4
    for a in arrays[3::4]:
        shapes += [a.shape] * 4
    shapes += [little[0].shape] * 4 + [little[3].shape] * 4
    return pl.pallas_call(
        functools.partial(update_kernel, rates, small_rate),
        in_specs=[IN_HBM] * 2 + [IN_VMEM] * (10 + len(arrays)),
        out_specs=[IN_VMEM] * len(shapes) + [IN_HBM] * 2,
        out_shape=[S(s, f32) for s in shapes] + [S(a.shape, a.dtype) for a in passed],
        scratch_shapes=[pltpu.VMEM(a.shape, a.dtype) for a in passed] + [DMA((4,))],
        compiler_params=params(),
        name="update",
    )(*passed, vector, *little, *thirds, *arrays)


def local(linked, *args):
    (
        features, pos_conv, segment_ids, frame_valid, cotangent,
        qkv_weight, proj_weight, expand_weight, reduce_weight, norm_gains, bias_vector,
        qkv_moment, proj_moment, expand_moment, reduce_moment, gains_moment, bias_moment,
        qkv_average, proj_average, expand_average, reduce_average, gains_average, bias_average,
    ) = args
    ranks = lax.axis_size("dp")
    bias_len = bias_vector.shape[0]
    gain_len = norm_gains.shape[1]
    if linked:
        bias, gains = bias_vector[None], norm_gains
        weights = [qkv_weight, proj_weight, expand_weight, reduce_weight]
    else:
        round_to = lambda w: lax.reduce_precision(w, 8, 7)
        bias = lax.all_gather(round_to(bias_vector), "dp", axis=0, tiled=True)[None]
        gains = lax.all_gather(round_to(norm_gains), "dp", axis=1, tiled=True)
        qkv_full, *weights = [
            lax.all_gather(w.astype(bf16), "dp", axis=0, tiled=True) for w in (qkv_weight, proj_weight, expand_weight, reduce_weight)
        ]
        weights = [jnp.concatenate([qkv_full[:, a : a + w] for a, _, w in STRIPS[g]], axis=1) for g in range(3)] + weights
    outs = front(linked, bias_len, gain_len, bias, gains, weights, features, pos_conv, cotangent, segment_ids, frame_valid)
    if linked:
        weights, outs = outs[:6], outs[6:]
    *sums, grad_input, layer_out, vector = back(linked, weights, *outs, segment_ids, frame_valid)
    if not linked:
        sums = [lax.psum_scatter(p.astype(f32), "dp", scatter_dimension=0, tiled=True) for p in sums]
        vector = lax.psum(vector, "dp")
    *thirds, proj_grad, expand_grad, reduce_grad = sums
    root = math.sqrt(ranks * features.shape[0])
    matrix, proj, little = rate_matrix / root, rate_proj / root, rate_small / root
    *updated, layer_out, grad_input = update(
        (matrix, proj, matrix, matrix),
        little,
        [layer_out, grad_input],
        vector,
        [bias_vector[None], bias_moment[None], bias_average[None], norm_gains, gains_moment, gains_average],
        thirds,
        [
            qkv_weight, qkv_moment, qkv_average,
            proj_weight, proj_grad, proj_moment, proj_average,
            expand_weight, expand_grad, expand_moment, expand_average,
            reduce_weight, reduce_grad, reduce_moment, reduce_average,
        ],
    )

    bias_new = [b[0] for b in updated[16:20]]
    gains_new = updated[20:24]
    results = [layer_out, grad_input]
    for i in range(4):
        results += [updated[i], updated[4 + i], updated[8 + i], updated[12 + i], gains_new[i], bias_new[i]]
    return tuple(results)


def solution(mesh):
    linked = mesh.shape["dp"] == 32
    rows, lanes, line = P("dp", None), P(None, "dp"), P("dp")
    six = (rows, rows, rows, rows, lanes, line)
    return jax.shard_map(
        functools.partial(local, linked),
        mesh=mesh,
        in_specs=(rows,) * 5 + six * 3,
        out_specs=(rows, rows) + six * 4,
        check_vma=False,
    )
```
